32 devices in a mesh: dp: 8 (over z, x), tensor: 4 (over y, core).
Axes of the slice: x: 2, y: 2, z: 4, core: 2. Of those that a mesh axis runs over, the one named last changes fastest.
Arguments:
- tokens: bfloat16 [8192, 1024], P('dp'), may hold values from -6 to 6
- w_query: bfloat16 [1024, 1024], P(None, 'tensor'), may hold values from -0.1875 to 0.1875
- w_key: bfloat16 [1024, 1024], P(None, 'tensor'), may hold values from -0.1875 to 0.1875
- w_value: bfloat16 [1024, 1024], P(None, 'tensor'), may hold values from -0.1875 to 0.1875
- w_output: bfloat16 [1024, 1024], P('tensor'), may hold values from -1.5 to 1.5
- w_gate: bfloat16 [1024, 2816], P(None, 'tensor'), may hold values from -0.1875 to 0.1875
- w_up: bfloat16 [1024, 2816], P(None, 'tensor'), may hold values from -0.1875 to 0.1875
- w_down: bfloat16 [2816, 1024], P('tensor'), may hold values from -0.109375 to 0.109375
- gain_attn: float32 [1024], replicated, may hold values from 0.1 to 1.9
- gain_mlp: float32 [1024], replicated, may hold values from 0.1 to 1.9
- cache_keys: bfloat16 [8, 8, 4096, 128], P('dp', 'tensor'), may hold values from -6 to 6
- cache_values: bfloat16 [8, 8, 4096, 128], P('dp', 'tensor'), may hold values from -6 to 6
- knn_index: int32 [8192, 128], P('dp'), may hold values from 0 to 8191, as said below
- memory_flag: int32 [8], P('dp'), may hold values from 0 to 1, as said below
- pairing: int32 [8], P('dp'), may hold values from 0 to 7, as said below
- cotangent: bfloat16 [8192, 1024], P('dp'), may hold values from -6 to 6
Outputs:
- output: bfloat16 [8192, 1024], P(('dp', 'tensor'))
- grad_tokens: bfloat16 [8192, 1024], P(('dp', 'tensor'))
- grad_w_query: float32 [1024, 1024], P('dp', 'tensor')
- grad_w_key: float32 [1024, 1024], P('dp', 'tensor')
- grad_w_value: float32 [1024, 1024], P('dp', 'tensor')
- grad_w_output: float32 [1024, 1024], P('tensor', 'dp')
- grad_w_gate: float32 [1024, 2816], P('dp', 'tensor')
- grad_w_up: float32 [1024, 2816], P('dp', 'tensor')
- grad_w_down: float32 [2816, 1024], P('tensor', 'dp')
- grad_gain_attn: float32 [1024], P('dp')
- grad_gain_mlp: float32 [1024], P('dp')
The draws below stay inside these ranges and needn't reach their ends.
Inputs may be any that keep to these rules, and one draw needn't show every extreme that they name: `knn_index`: in every row, entry j lies in [j * 2 * 32, (j + 1) * 2 * 32); values below 4096 name rows of the document's own cache, the others row (value - 4096) of its partner's cache. `memory_flag`: exactly half of the documents have 1, among them documents 0, 4 and 7. pairing[pairing[b]] = b, and pairing[b] differs from b in exactly one bit of its binary number.
All inputs are finite; a program needn't handle non-finite values.
Results may differ from the reference program's by a relative error of at most 0.017.
Values may be sent and summed in bfloat16 or wider, within the bound.
No kernel may reach another device: no remote copies, remote signals or barrier semaphores. Data moves between devices by JAX's collectives and lax.ppermute only.
A program may use at most 256 MiB of HBM per device.

```python
import jax
import jax.numpy as jnp
from jax import lax

D = 1024
H = 8
HD = 128
FF = 2816
MEM = 4096
TOPK = 128
DOCS = 8
TOKENS = 8192


def draw_knn_index(key, part):
    spread = 2 * MEM // TOPK
    offsets = jax.random.randint(key, (TOKENS, TOPK), 0, spread)
    return (offsets + jnp.arange(TOPK, dtype=jnp.int32)[None, :] * spread).astype(jnp.int32)


def draw_memory_flag(key, part):
    order = jax.random.permutation(key, DOCS - 3)
    inner = (order < DOCS // 2 - 3).astype(jnp.int32)
    ends = jnp.ones((1,), jnp.int32)
    return jnp.concatenate([ends, inner[:DOCS // 2 - 1], ends, inner[DOCS // 2 - 1:], ends]).astype(jnp.int32)


def draw_pairing(key, part):
    levels = DOCS.bit_length() - 1
    first_key, second_key = jax.random.split(key, 2)
    order = jax.random.permutation(first_key, levels).astype(jnp.int32)
    xor_mask = jax.random.randint(second_key, (), 0, DOCS).astype(jnp.int32)
    bit_positions = jnp.arange(levels, dtype=jnp.int32)
    numbers = jnp.bitwise_xor(jnp.arange(DOCS, dtype=jnp.int32), xor_mask)
    binary_digits = jnp.right_shift(numbers[:, None], order[None, :]) % 2
    renamed_labels = jnp.sum(jnp.left_shift(binary_digits, bit_positions[None, :]), axis=1).astype(jnp.int32)
    power_values = jnp.left_shift(jnp.int32(1), bit_positions[1:])
    leading_bit = jnp.sum((renamed_labels[:, None] >= power_values[None, :]).astype(jnp.int32), axis=1)
    flipped_position = jnp.maximum(leading_bit - 1, 0)
    partner_identifier = jnp.bitwise_xor(renamed_labels, jnp.left_shift(jnp.int32(1), flipped_position))
    back_digits = jnp.right_shift(partner_identifier[:, None], bit_positions[None, :]) % 2
    partner = jnp.sum(jnp.left_shift(back_digits, order[None, :]), axis=1).astype(jnp.int32)
    return jnp.bitwise_xor(partner, xor_mask).astype(jnp.int32)


def shard_levels(key, shape, cuts, low, largest):
    def one(dim, blocks):
        draws = jax.random.uniform(jax.random.fold_in(jax.random.fold_in(key, 6), dim), (blocks,), jnp.float32, low / len(cuts), largest / len(cuts))
        return jnp.repeat(jnp.exp(draws), shape[dim] // blocks).reshape((-1,) + (1,) * (len(shape) - dim - 1))

    factor_of = one(*cuts[0])
    for cut in cuts[1:]:
        factor_of = factor_of * one(*cut)
    return factor_of


def normal_values(stream_key, extent, scale, bound, shards=(), kind=jnp.bfloat16):
    drawn = scale * jax.random.normal(stream_key, extent, jnp.float32)
    if shards:
        drawn = drawn * shard_levels(stream_key, extent, shards, -0.22, 0.18)
    return jnp.clip(drawn, -bound, bound).astype(kind)


def setup_inputs(seed: int = 0) -> dict:
    key_of = jax.random.split(jax.random.key(seed), 17)
    tokens = normal_values(key_of[0], (TOKENS, D), 1.0, 6.0, ((0, 8),))
    w_query = normal_values(key_of[1], (D, H * HD), D ** -0.5, 0.1875, ((1, 4),))
    w_key = normal_values(key_of[2], (D, H * HD), D ** -0.5, 0.1875, ((1, 4),))
    w_value = normal_values(key_of[3], (D, H * HD), D ** -0.5, 0.1875, ((1, 4),))
    w_output = normal_values(key_of[4], (H * HD, D), 16 ** -0.5, 1.5, ((0, 4),))
    w_gate = normal_values(key_of[5], (D, FF), D ** -0.5, 0.1875, ((1, 4),))
    w_up = normal_values(key_of[6], (D, FF), D ** -0.5, 0.1875, ((1, 4),))
    w_down = normal_values(key_of[7], (FF, D), FF ** -0.5, 0.109375, ((0, 4),))
    gain_attn = jnp.clip(1.0 + 0.18 * jax.random.normal(key_of[8], (D,), jnp.float32), 0.1, 1.9)
    gain_mlp = jnp.clip(1.0 + 0.18 * jax.random.normal(key_of[9], (D,), jnp.float32), 0.1, 1.9)
    cache_keys = normal_values(key_of[10], (DOCS, H, MEM, HD), 1.0, 6.0, ((0, 8), (1, 4)))
    cache_values = normal_values(key_of[11], (DOCS, H, MEM, HD), 1.0, 6.0, ((0, 8), (1, 4)))
    knn_index = draw_knn_index(jax.random.fold_in(key_of[16], 71), 0)
    memory_flag = draw_memory_flag(jax.random.fold_in(key_of[16], 71), 0)
    pairing = draw_pairing(jax.random.fold_in(key_of[16], 71), 0)
    cotangent = normal_values(key_of[15], (TOKENS, D), 1.0, 6.0, ((0, 8),))
    return dict(tokens=tokens, w_query=w_query, w_key=w_key, w_value=w_value, w_output=w_output, w_gate=w_gate, w_up=w_up, w_down=w_down, gain_attn=gain_attn, gain_mlp=gain_mlp, cache_keys=cache_keys, cache_values=cache_values, knn_index=knn_index, memory_flag=memory_flag, pairing=pairing, cotangent=cotangent)


epsilon = 1e-05
negative_big = -1e+30
largest_value = lax.Precision.HIGHEST

@jax.custom_vjp
def low(v):
    return lax.optimization_barrier(v.astype(jnp.bfloat16)).astype(jnp.float32)

@jax.custom_vjp
def low_back(v):
    return v

def low_keep(v):
    return (low(v), None)

def low_pass(kept, grad):
    return (grad,)

def back_keep(v):
    return (v, None)

def back_low(kept, grad):
    return (low(grad),)
low.defvjp(low_keep, low_pass)
low_back.defvjp(back_keep, back_low)

def rms_norm(values, gain):
    factor = lax.rsqrt(lax.optimization_barrier(jnp.mean(values * values, axis=-1, keepdims=True)) + epsilon)
    return values * factor * gain

def rotary(values):
    head_dim = values.shape[-1]
    half_dim = head_dim // 2
    position = jnp.arange(values.shape[0], dtype=jnp.float32)
    inverse = jnp.exp(-jnp.log(10000.0) * jnp.arange(half_dim, dtype=jnp.float32) * 2.0 / head_dim)
    angles = position[:, None] * inverse[None, :]
    cos_table = jnp.cos(angles)[:, None, :]
    sin_table = jnp.sin(angles)[:, None, :]
    front = values[..., :half_dim]
    back_part = values[..., half_dim:]
    return jnp.concatenate([front * cos_table - back_part * sin_table, back_part * cos_table + front * sin_table], axis=-1)

def block_attend(row_start, queries, keys, values, stored_keys, stored_values, knn_rows, flag_on):
    sequence_length = keys.shape[0]
    width = min(512, sequence_length)
    query_matrix = lax.dynamic_slice_in_dim(queries, row_start, width, 0)
    index_rows = lax.dynamic_slice_in_dim(knn_rows, row_start, width, 0)
    scale_factor = queries.shape[-1] ** (-0.5)
    local_raw = low_back(jnp.einsum('qhd,khd->hqk', query_matrix, keys, precision=largest_value) * scale_factor)
    memory_logits = low_back(jnp.einsum('lsc,sac->sla', query_matrix, stored_keys, precision=largest_value) * scale_factor)
    positions = row_start + jnp.arange(width, dtype=jnp.int32)
    causal = positions[:, None] >= jnp.arange(sequence_length, dtype=jnp.int32)[None, :]
    chosen = jnp.zeros((width, stored_keys.shape[1]), bool).at[jnp.arange(width, dtype=jnp.int32)[:, None], index_rows].set(True)
    chosen = jnp.logical_and(chosen, flag_on > 0)
    scores = jnp.concatenate([jnp.where(causal[None], local_raw, negative_big), jnp.where(chosen[None], memory_logits, negative_big)], axis=-1)
    probabilities = low(jax.nn.softmax(scores, axis=-1))
    local_out = jnp.einsum('hqk,khd->qhd', probabilities[:, :, :sequence_length], values, precision=largest_value)
    memory_output = jnp.einsum('oux,oxa->uoa', probabilities[:, :, sequence_length:], stored_values, precision=largest_value)
    return local_out + memory_output

def layer(doc_tokens, w_query, w_key, w_value, w_output, w_gate, w_up, w_down, gain_attn, gain_mlp, stored_keys, stored_values, knn_rows, flag_on):
    sequence_length = doc_tokens.shape[0]
    heads = stored_keys.shape[0]
    head_dim = stored_keys.shape[2]
    normed = low(rms_norm(doc_tokens, gain_attn))
    queries = low(rotary(low_back(jnp.dot(normed, w_query, precision=largest_value)).reshape(sequence_length, heads, head_dim)))
    keys = low(rotary(low_back(jnp.dot(normed, w_key, precision=largest_value)).reshape(sequence_length, heads, head_dim)))
    values = low(low_back(jnp.dot(normed, w_value, precision=largest_value))).reshape(sequence_length, heads, head_dim)
    width = min(512, sequence_length)
    starts = jnp.arange(sequence_length // width, dtype=jnp.int32) * width
    attend = jax.checkpoint(block_attend)
    pieces = lax.map(lambda row_start: attend(row_start, queries, keys, values, stored_keys, stored_values, knn_rows, flag_on), starts)
    attended = low(low_back(pieces.reshape(sequence_length, heads * head_dim)))
    middle = doc_tokens + low_back(jnp.dot(attended, w_output, precision=largest_value))
    normed_mlp = low(rms_norm(middle, gain_mlp))
    gate = low_back(jnp.dot(normed_mlp, w_gate, precision=largest_value))
    upper = low_back(jnp.dot(normed_mlp, w_up, precision=largest_value))
    hidden = low(jax.nn.silu(gate) * upper)
    return middle + low_back(jnp.dot(hidden, w_down, precision=largest_value))

def reference(tokens, w_query, w_key, w_value, w_output, w_gate, w_up, w_down, gain_attn, gain_mlp, cache_keys, cache_values, knn_index, memory_flag, pairing, cotangent):
    weights = tuple((matrix.astype(jnp.float32) for matrix in (w_query, w_key, w_value, w_output, w_gate, w_up, w_down, gain_attn, gain_mlp)))
    docs = memory_flag.shape[0]
    sequence_length = tokens.shape[0] // docs

    def one_doc(totals, doc):
        doc_tokens = lax.dynamic_slice_in_dim(tokens, doc * sequence_length, sequence_length, 0).astype(jnp.float32)
        doc_grad = lax.dynamic_slice_in_dim(cotangent, doc * sequence_length, sequence_length, 0).astype(jnp.float32)
        knn_rows = lax.dynamic_slice_in_dim(knn_index, doc * sequence_length, sequence_length, 0).astype(jnp.int32)
        partner = pairing[doc].astype(jnp.int32)
        stored_keys = jnp.concatenate([cache_keys[doc], cache_keys[partner]], axis=1).astype(jnp.float32)
        stored_values = jnp.concatenate([cache_values[doc], cache_values[partner]], axis=1).astype(jnp.float32)
        flag_on = memory_flag[doc]

        def forward(doc_input, *params):
            return layer(doc_input, *params, stored_keys, stored_values, knn_rows, flag_on)
        result, pullback = jax.vjp(forward, doc_tokens, *weights)
        grads = pullback(doc_grad)
        totals = tuple((total + grad_part for total, grad_part in zip(totals, grads[1:])))
        return (totals, (result.astype(jnp.bfloat16), grads[0].astype(jnp.bfloat16)))
    start_totals = tuple((jnp.zeros(matrix.shape, jnp.float32) for matrix in weights))
    totals, (outputs, gradient_rows) = lax.scan(one_doc, start_totals, jnp.arange(docs, dtype=jnp.int32))
    return (outputs.reshape(tokens.shape), gradient_rows.reshape(tokens.shape), totals[0], totals[1], totals[2], totals[3], totals[4], totals[5], totals[6], totals[7], totals[8])
```

```python
import functools

import jax
import jax.numpy as jnp
import numpy as np
from jax import lax
from jax.experimental import pallas as pl
from jax.experimental.pallas import tpu as pltpu
from jax.sharding import PartitionSpec as P

epsilon = 1e-05
negative_big = -1e30
F = jnp.float32
B = jnp.bfloat16
GROUP_BLOCK = 16


def dot(a, b, da, db):
    return lax.dot_general(a, b, (((da,), (db,)), ((), ())), preferred_element_type=F)


def swap(array, axis, bit):
    return lax.ppermute(array, axis, [(i, i ^ bit) for i in range(lax.axis_size(axis))])


def axis_bits(axis):
    return lax.axis_size(axis).bit_length() - 1


def pick(block_scores, offsets, heads, spread, gb):
    picked = [s[:gb] for s in block_scores]
    for t in range(1, spread):
        here = offsets == float(t)
        for h in range(heads):
            picked[h] = jnp.where(here, block_scores[h][t * gb : (t + 1) * gb], picked[h])
    return picked


def expand(picked, offsets, spread):
    zero = jnp.zeros_like(picked)
    return jnp.concatenate(
        [jnp.where(offsets == jnp.asarray(t, B), picked, zero) for t in range(spread)], axis=0
    )


def spread_dot(rows_ref, h, picked, offsets, spread, gb):
    rows = gb * spread
    total = None
    for b in range(offsets.shape[0] // gb):
        wide = expand(picked[b * gb : (b + 1) * gb], offsets[b * gb : (b + 1) * gb], spread)
        part = dot(rows_ref[h, b * rows : (b + 1) * rows, :], wide, 0, 0)
        total = part if total is None else total + part
    return total


def memory_forward_body(
    flag_ref, q_ref, off_ref, k_ref, v_ref, o_ref, lse_ref, sel_ref, *, heads, hd, spread, gb
):
    scale = hd**-0.5
    groups = off_ref.shape[0]
    rows = gb * spread

    @pl.when(flag_ref[0] > 0)
    def _():
        offs = off_ref[...]
        wide_offs = offs.astype(F)
        for b in range(groups // gb):
            scores = [
                dot(
                    k_ref[h, b * rows : (b + 1) * rows, :],
                    q_ref[:, h * hd : (h + 1) * hd],
                    1,
                    1,
                )
                for h in range(heads)
            ]
            picked = pick(scores, wide_offs[b * gb : (b + 1) * gb], heads, spread, gb)
            for h in range(heads):
                sel_ref[h, b * gb : (b + 1) * gb, :] = picked[h] * scale
        for h in range(heads):
            x = sel_ref[h]
            peak = jnp.max(x, axis=0, keepdims=True)
            p = jnp.exp(x - peak)
            total = jnp.sum(p, axis=0, keepdims=True)
            lse_ref[h : h + 1, :] = peak + jnp.log(total)
            out = spread_dot(v_ref, h, p.astype(B), offs, spread, gb)
            o_ref[:, h * hd : (h + 1) * hd] = (out / total).T.astype(B)

    @pl.when(flag_ref[0] <= 0)
    def _():
        o_ref[...] = jnp.zeros_like(o_ref)
        lse_ref[...] = jnp.full_like(lse_ref, negative_big)
        sel_ref[...] = jnp.full_like(sel_ref, negative_big)


def memory_backward_body(
    flag_ref, g_ref, st_ref, sel_ref, off_ref, k_ref, v_ref, dq_ref, *, heads, hd, spread, gb
):
    scale = hd**-0.5
    groups = off_ref.shape[0]
    rows = gb * spread

    @pl.when(flag_ref[0] > 0)
    def _():
        offs = off_ref[...]
        wide_offs = offs.astype(F)
        grads = [[] for _ in range(heads)]
        for b in range(groups // gb):
            dprobs = [
                dot(
                    v_ref[h, b * rows : (b + 1) * rows, :],
                    g_ref[:, h * hd : (h + 1) * hd],
                    1,
                    1,
                )
                for h in range(heads)
            ]
            picked = pick(dprobs, wide_offs[b * gb : (b + 1) * gb], heads, spread, gb)
            for h in range(heads):
                p = jnp.exp(sel_ref[h, b * gb : (b + 1) * gb, :] - st_ref[h : h + 1, :])
                delta = st_ref[heads + h : heads + h + 1, :]
                grads[h].append((p * (picked[h] - delta)).astype(B))
        for h in range(heads):
            out = spread_dot(k_ref, h, jnp.concatenate(grads[h], axis=0), offs, spread, gb)
            dq_ref[:, h * hd : (h + 1) * hd] = (out * scale).T.astype(dq_ref.dtype)

    @pl.when(flag_ref[0] <= 0)
    def _():
        dq_ref[...] = jnp.zeros_like(dq_ref)


def row_block(length):
    return min(512, length)


def memory_forward(flag, q, off, k, v, spread):
    length = q.shape[0]
    heads, rows, hd = k.shape
    groups = off.shape[0]
    tq = row_block(length)
    return pl.pallas_call(
        functools.partial(memory_forward_body, heads=heads, hd=hd, spread=spread, gb=GROUP_BLOCK),
        grid=(length // tq,),
        in_specs=[
            pl.BlockSpec(memory_space=pltpu.SMEM),
            pl.BlockSpec((tq, heads * hd), lambda i: (i, 0)),
            pl.BlockSpec((groups, tq), lambda i: (0, i)),
            pl.BlockSpec((heads, rows, hd), lambda i: (0, 0, 0)),
            pl.BlockSpec((heads, rows, hd), lambda i: (0, 0, 0)),
        ],
        out_specs=[
            pl.BlockSpec((tq, heads * hd), lambda i: (i, 0)),
            pl.BlockSpec((heads, tq), lambda i: (0, i)),
            pl.BlockSpec((heads, groups, tq), lambda i: (0, 0, i)),
        ],
        out_shape=[
            jax.ShapeDtypeStruct((length, heads * hd), B),
            jax.ShapeDtypeStruct((heads, length), F),
            jax.ShapeDtypeStruct((heads, groups, length), F),
        ],
        cost_estimate=pl.CostEstimate(
            flops=8 * length * heads * rows * hd,
            transcendentals=0,
            bytes_accessed=4 * heads * rows * hd,
        ),
        name="memory_forward",
    )(flag, q, off, k, v)


def memory_backward(flag, g, stats, sel, off, k, v, spread, dtype):
    length = g.shape[0]
    heads, rows, hd = k.shape
    groups = off.shape[0]
    tq = row_block(length)
    return pl.pallas_call(
        functools.partial(memory_backward_body, heads=heads, hd=hd, spread=spread, gb=GROUP_BLOCK),
        grid=(length // tq,),
        in_specs=[
            pl.BlockSpec(memory_space=pltpu.SMEM),
            pl.BlockSpec((tq, heads * hd), lambda i: (i, 0)),
            pl.BlockSpec((2 * heads, tq), lambda i: (0, i)),
            pl.BlockSpec((heads, groups, tq), lambda i: (0, 0, i)),
            pl.BlockSpec((groups, tq), lambda i: (0, i)),
            pl.BlockSpec((heads, rows, hd), lambda i: (0, 0, 0)),
            pl.BlockSpec((heads, rows, hd), lambda i: (0, 0, 0)),
        ],
        out_specs=pl.BlockSpec((tq, heads * hd), lambda i: (i, 0)),
        out_shape=jax.ShapeDtypeStruct((length, heads * hd), dtype),
        cost_estimate=pl.CostEstimate(
            flops=8 * length * heads * rows * hd,
            transcendentals=0,
            bytes_accessed=4 * heads * rows * hd,
        ),
        name="memory_backward",
    )(flag, g, stats, sel, off, k, v)


def causal_scores(k, q, w, scale):
    s = dot(k, q, 1, 1) * scale
    n = k.shape[0]
    key = lax.broadcasted_iota(jnp.int32, (w, w), 0)
    query = lax.broadcasted_iota(jnp.int32, (w, w), 1)
    diagonal = jnp.where(key <= query, s[n - w :], negative_big)
    return diagonal if n == w else jnp.concatenate([s[: n - w], diagonal], axis=0)


def local_forward_body(q_ref, k_ref, v_ref, o_ref, lse_ref, *, heads, hd, w):
    scale = hd**-0.5
    for h in range(heads):
        c = slice(h * hd, (h + 1) * hd)
        for i in range(q_ref.shape[0] // w):
            n = (i + 1) * w
            r = slice(i * w, n)
            s = causal_scores(k_ref[:n, c], q_ref[r, c], w, scale)
            peak = jnp.max(s, axis=0, keepdims=True)
            p = jnp.exp(s - peak)
            total = jnp.sum(p, axis=0, keepdims=True)
            lse_ref[h : h + 1, r] = peak + jnp.log(total)
            out = dot(v_ref[:n, c], p.astype(B), 0, 0)
            o_ref[r, c] = (out / total).T.astype(B)


def local_forward(q, k, v, heads):
    length, columns = q.shape
    return pl.pallas_call(
        functools.partial(
            local_forward_body, heads=heads, hd=columns // heads, w=min(256, length)
        ),
        out_shape=[
            jax.ShapeDtypeStruct((length, columns), B),
            jax.ShapeDtypeStruct((heads, length), F),
        ],
        name="local_forward",
    )(q, k, v)


def local_backward_body(
    q_ref, k_ref, v_ref, g_ref, st_ref, dq_ref, dk_ref, dv_ref, *, heads, hd, w
):
    scale = hd**-0.5
    for h in range(heads):
        c = slice(h * hd, (h + 1) * hd)
        count = q_ref.shape[0] // w
        for i in reversed(range(count)):
            n = (i + 1) * w
            r = slice(i * w, n)
            s = causal_scores(k_ref[:n, c], q_ref[r, c], w, scale)
            p = jnp.exp(s - st_ref[h : h + 1, r])
            dp = dot(v_ref[:n, c], g_ref[r, c], 1, 1)
            ds = (p * (dp - st_ref[heads + h : heads + h + 1, r])).astype(B)
            dq_ref[r, c] = (dot(k_ref[:n, c], ds, 0, 0) * scale).T
            dk = dot(ds, q_ref[r, c], 1, 0) * scale
            dv = dot(p.astype(B), g_ref[r, c], 1, 0)
            if i == count - 1:
                dk_ref[:n, c] = dk
                dv_ref[:n, c] = dv
            else:
                dk_ref[:n, c] += dk
                dv_ref[:n, c] += dv


def local_backward(q, k, v, g, stats, heads):
    length, columns = q.shape
    return pl.pallas_call(
        functools.partial(
            local_backward_body, heads=heads, hd=columns // heads, w=min(256, length)
        ),
        out_shape=[jax.ShapeDtypeStruct((length, columns), F)] * 3,
        name="local_backward",
    )(q, k, v, g, stats)


def norm_forward(values, gain):
    factor = lax.rsqrt(jnp.mean(values * values, axis=-1, keepdims=True) + epsilon)
    return (values * factor * gain, factor)


def norm_backward(values, factor, gain, grad_normed):
    scaled = gain * grad_normed
    return factor * scaled - values * (factor * factor * factor) * jnp.mean(
        values * scaled, axis=-1, keepdims=True
    )


def rotate_tables(length, hd, heads):
    half = hd // 2
    position = np.arange(length, dtype=np.float32)
    inverse = np.exp(
        -np.log(np.float32(10000.0)) * np.arange(half, dtype=np.float32) * np.float32(2.0) / hd
    ).astype(np.float32)
    angles = position[:, None] * inverse[None, :]
    cos = np.cos(angles)
    sin = np.sin(angles)
    return (
        jnp.asarray(np.concatenate([cos, cos], axis=1)[:, None, :]),
        jnp.asarray(np.concatenate([-sin, sin], axis=1)[:, None, :]),
    )


def rotate(values, heads, tables, direction):
    length, columns = values.shape
    hd = columns // heads
    x = values.reshape(length, heads, hd)
    flipped = jnp.concatenate([x[..., hd // 2 :], x[..., : hd // 2]], axis=-1)
    return (x * tables[0] + direction * flipped * tables[1]).reshape(length, columns).astype(B)


def to_partner(arrays, chosen):
    got = [[swap(a, "dp", 1 << b) for a in arrays] for b in reversed(range(len(chosen)))]
    got.reverse()
    out = []
    for j in range(len(arrays)):
        value = got[0][j]
        for b in range(1, len(chosen)):
            value = jnp.where(chosen[b], got[b][j], value)
        out.append(value)
    return out


def gather_tensor(value):
    pieces, offsets = [value], [0]
    for b in reversed(range(axis_bits("tensor"))):
        pieces = pieces + [swap(p, "tensor", 1 << b) for p in pieces]
        offsets = offsets + [k ^ (1 << b) for k in offsets]
    return pieces, offsets


def in_order(pieces, offsets, me):
    share = pieces[0].shape[0]
    out = jnp.zeros((len(pieces) * share,) + pieces[0].shape[1:], pieces[0].dtype)
    for piece, k in zip(pieces, offsets):
        out = lax.dynamic_update_slice_in_dim(out, piece, (me ^ k) * share, 0)
    return out


def scatter_sum(value, axis, bit_order):
    me = lax.axis_index(axis)
    bits = axis_bits(axis)
    tail = value.shape[1:]
    value = value.reshape((2,) * bits + tail)
    alive = list(reversed(range(bits)))
    for b in bit_order:
        where = alive.index(b)
        mine = (me >> b) & 1
        keep = lax.dynamic_index_in_dim(value, mine, where, keepdims=False)
        send = lax.dynamic_index_in_dim(value, 1 - mine, where, keepdims=False)
        value = keep.astype(F) + swap(send.astype(B), axis, 1 << b).astype(F)
        alive.pop(where)
    return value


def per_device(
    tokens,
    w_query,
    w_key,
    w_value,
    w_output,
    w_gate,
    w_up,
    w_down,
    gain_attn,
    gain_mlp,
    cache_keys,
    cache_values,
    knn_index,
    memory_flag,
    pairing,
    cotangent,
):
    length, width = tokens.shape
    parts = lax.axis_size("tensor")
    docs = lax.axis_size("dp")
    share = length // parts
    me = lax.axis_index("tensor")
    row_offset = me * share
    heads = cache_keys.shape[1]
    rows = cache_keys.shape[2]
    hd = cache_keys.shape[3]
    columns = heads * hd
    topk = knn_index.shape[1]
    groups = topk // 2
    spread = rows // groups
    flag = memory_flag[:1].astype(jnp.int32)
    difference = jnp.bitwise_xor(pairing[0], lax.axis_index("dp"))
    chosen = [difference == (1 << b) for b in range(axis_bits("dp"))]
    dp_order = list(range(axis_bits("dp")))
    tensor_order = list(range(axis_bits("tensor")))

    offsets = (knn_index - jnp.arange(topk, dtype=jnp.int32)[None, :] * spread).T.astype(B)
    own_off = offsets[:groups]
    far_off = jnp.where(flag[0] > 0, offsets[groups:], jnp.asarray(-1, B))
    (their_off,) = to_partner([far_off], chosen)
    their_flag = (their_off[0, :1].astype(F) >= 0).astype(jnp.int32)
    out_weights, weight_offsets = gather_tensor(w_output)

    def ordered_rows(cache):
        return (
            cache.reshape(heads, groups // GROUP_BLOCK, GROUP_BLOCK, spread, hd)
            .transpose(0, 1, 3, 2, 4)
            .reshape(heads, rows, hd)
        )

    tokens_full = tokens.astype(F)
    normed_attn, factor_attn = norm_forward(tokens_full, gain_attn)
    normed_low = normed_attn.astype(B)
    tables = rotate_tables(length, hd, heads)
    queries = rotate(dot(normed_low, w_query, 1, 0), heads, tables, 1.0)
    (their_queries,) = to_partner([queries], chosen)
    keys = rotate(dot(normed_low, w_key, 1, 0), heads, tables, 1.0)
    values = dot(normed_low, w_value, 1, 0).astype(B)
    stored_keys = ordered_rows(cache_keys[0])
    stored_values = ordered_rows(cache_values[0])
    own_out, own_lse, own_sel = memory_forward(
        flag, queries, own_off, stored_keys, stored_values, spread
    )
    local_out, local_lse = local_forward(queries, keys, values, heads)
    their_out, their_lse, their_sel = memory_forward(
        their_flag, their_queries, their_off, stored_keys, stored_values, spread
    )
    far_out, far_lse = to_partner([their_out, their_lse], chosen)
    log_total = jnp.logaddexp(jnp.logaddexp(local_lse, own_lse), far_lse)

    def weighted(out, lse):
        weight = jnp.exp(lse - log_total).T
        return out.reshape(length, heads, hd).astype(F) * weight[:, :, None]

    attended = (
        weighted(local_out, local_lse) + weighted(own_out, own_lse) + weighted(far_out, far_lse)
    )
    attended_low = attended.reshape(length, columns).astype(B)

    pieces, _ = gather_tensor(attended_low)
    middle = tokens_full
    for piece, weight in zip(pieces, out_weights):
        middle = middle + dot(piece, weight, 1, 0)
    normed, factor = norm_forward(middle, gain_mlp)
    normed_mlp = normed.astype(B)
    gate = dot(normed_mlp, w_gate, 1, 0)
    upper = dot(normed_mlp, w_up, 1, 0)
    sigmoid_gate = jax.nn.sigmoid(gate)
    silu_gate = gate * sigmoid_gate
    hidden = (silu_gate * upper).astype(B)
    grad_hidden = dot(cotangent, w_down, 1, 1)
    grad_gate = (grad_hidden * upper * sigmoid_gate * (1.0 + gate * (1.0 - sigmoid_gate))).astype(B)
    grad_upper = (grad_hidden * silu_gate).astype(B)
    grad_normed_part = dot(grad_gate, w_gate, 1, 1) + dot(grad_upper, w_up, 1, 1)
    middle_rows = lax.dynamic_slice_in_dim(middle, row_offset, share, 0)
    factor_rows = lax.dynamic_slice_in_dim(factor, row_offset, share, 0)
    grad_normed_rows = scatter_sum(
        grad_normed_part.reshape(parts, share, width), "tensor", tensor_order
    )
    grad_middle_rows = lax.dynamic_slice_in_dim(cotangent, row_offset, share, 0).astype(
        F
    ) + norm_backward(middle_rows, factor_rows, gain_mlp, grad_normed_rows)
    gain_mlp_part = jnp.sum(grad_normed_rows * middle_rows * factor_rows, axis=0)
    branch_pieces, branch_offsets = gather_tensor(grad_middle_rows.astype(B))
    grad_branch = in_order(branch_pieces, branch_offsets, me)

    grad_attended = dot(grad_branch, w_output, 1, 1).astype(B)
    delta = jnp.sum(
        (grad_attended.astype(F) * attended_low.astype(F)).reshape(length, heads, hd), axis=-1
    ).T
    stats = jnp.concatenate([log_total, delta], axis=0)
    their_grad, their_stats = to_partner([grad_attended, stats], chosen)
    local_dq, grad_keys, grad_values = local_backward(
        queries, keys, values, grad_attended, stats, heads
    )
    own_dq = memory_backward(
        flag, grad_attended, stats, own_sel, own_off, stored_keys, stored_values, spread, F
    )
    their_dq = memory_backward(
        their_flag, their_grad, their_stats, their_sel, their_off, stored_keys, stored_values,
        spread, B
    )
    (far_dq,) = to_partner([their_dq], chosen)

    mlp_grads = jnp.concatenate(
        [
            dot(normed_mlp, grad_gate, 0, 0),
            dot(normed_mlp, grad_upper, 0, 0),
            dot(cotangent, hidden, 0, 0),
            dot(grad_branch, attended_low, 0, 0),
        ],
        axis=1,
    )
    mlp_sum = scatter_sum(mlp_grads.reshape(docs, width // docs, -1), "dp", dp_order)
    ff = w_gate.shape[1]
    grad_w_gate = mlp_sum[:, :ff]
    grad_w_up = mlp_sum[:, ff : 2 * ff]
    grad_w_down = mlp_sum[:, 2 * ff : 3 * ff].T
    grad_w_output = mlp_sum[:, 3 * ff :].T

    down_part = dot(hidden, w_down, 1, 0).reshape(parts, share, width)
    output_rows = middle_rows + scatter_sum(down_part, "tensor", tensor_order)

    grad_key_low = rotate(grad_keys, heads, tables, -1.0)
    grad_value_low = grad_values.astype(B)
    grad_query_low = rotate(local_dq + own_dq + far_dq.astype(F), heads, tables, -1.0)
    grad_normed_attn = (
        dot(grad_key_low, w_key, 1, 1)
        + dot(grad_value_low, w_value, 1, 1)
        + dot(grad_query_low, w_query, 1, 1)
    )
    attn_grads = jnp.concatenate(
        [
            dot(normed_low, grad_query_low, 0, 0),
            dot(normed_low, grad_key_low, 0, 0),
            dot(normed_low, grad_value_low, 0, 0),
        ],
        axis=1,
    )
    attn_sum = scatter_sum(attn_grads.reshape(docs, width // docs, -1), "dp", dp_order)
    grad_attn_rows = scatter_sum(
        grad_normed_attn.reshape(parts, share, width), "tensor", tensor_order
    )
    tokens_rows = lax.dynamic_slice_in_dim(tokens, row_offset, share, 0).astype(F)
    factor_attn_rows = lax.dynamic_slice_in_dim(factor_attn, row_offset, share, 0)
    grad_tokens_rows = grad_middle_rows + norm_backward(
        tokens_rows, factor_attn_rows, gain_attn, grad_attn_rows
    )
    gain_attn_part = jnp.sum(grad_attn_rows * tokens_rows * factor_attn_rows, axis=0)
    gains = jnp.stack([gain_attn_part, gain_mlp_part], axis=0)
    for b in tensor_order:
        gains = gains + swap(gains, "tensor", 1 << b)
    gains = gains.reshape(2, docs, width // docs).transpose(1, 0, 2)
    gains = gain_scatter(gains, dp_order)
    return (
        output_rows.astype(B),
        grad_tokens_rows.astype(B),
        attn_sum[:, :columns],
        attn_sum[:, columns : 2 * columns],
        attn_sum[:, 2 * columns :],
        grad_w_output,
        grad_w_gate,
        grad_w_up,
        grad_w_down,
        gains[0],
        gains[1],
    )


def gain_scatter(gains, order):
    me = lax.axis_index("dp")
    total = gains
    for b in order:
        total = total + swap(total, "dp", 1 << b)
    return lax.dynamic_index_in_dim(total, me, 0, keepdims=False)


def solution(mesh):
    placed = (
        P("dp", None),
        P(None, "tensor"),
        P(None, "tensor"),
        P(None, "tensor"),
        P("tensor", None),
        P(None, "tensor"),
        P(None, "tensor"),
        P("tensor", None),
        P(),
        P(),
        P("dp", "tensor", None, None),
        P("dp", "tensor", None, None),
        P("dp", None),
        P("dp"),
        P("dp"),
        P("dp", None),
    )
    return jax.shard_map(
        per_device,
        mesh=mesh,
        in_specs=placed,
        out_specs=(
            P(("dp", "tensor"), None),
            P(("dp", "tensor"), None),
            P("dp", "tensor"),
            P("dp", "tensor"),
            P("dp", "tensor"),
            P("tensor", "dp"),
            P("dp", "tensor"),
            P("dp", "tensor"),
            P("tensor", "dp"),
            P("dp"),
            P("dp"),
        ),
        check_vma=False,
    )
```

```python
import functools

import jax
import jax.numpy as jnp
import numpy as np
from jax import lax
from jax.experimental import pallas as pl
from jax.experimental.pallas import tpu as pltpu
from jax.sharding import PartitionSpec as P

epsilon = 1e-05
negative_big = -1e30
F = jnp.float32
B = jnp.bfloat16
GROUP_BLOCK = 16


def dot(a, b, da, db):
    return lax.dot_general(a, b, (((da,), (db,)), ((), ())), preferred_element_type=F)


def swap(array, axis, bit):
    return lax.ppermute(array, axis, [(i, i ^ bit) for i in range(lax.axis_size(axis))])


def axis_bits(axis):
    return lax.axis_size(axis).bit_length() - 1


def call(body, out_shape, name, flops=0, **options):
    return pl.pallas_call(
        body,
        out_shape=out_shape,
        name=name,
        cost_estimate=pl.CostEstimate(flops=flops, transcendentals=0, bytes_accessed=flops // 400),
        **options,
    )


def shape(dims, dtype):
    return jax.ShapeDtypeStruct(dims, dtype)


def whole():
    return pl.BlockSpec(memory_space=pltpu.VMEM)


def scalars():
    return pl.BlockSpec(memory_space=pltpu.SMEM)


def slot_place(difference, order):
    place = 0
    for b in order:
        place = place * 2 + ((difference >> b) & 1)
    return place


def choose(refs, index, chosen):
    value = refs[0][index]
    for b in range(1, len(refs)):
        value = jnp.where(chosen == b, refs[b][index], value)
    return value


def split_terms(x):
    first = x.astype(B).astype(F)
    second = (x - first).astype(B).astype(F)
    third = (x - first - second).astype(B).astype(F)
    return [first, second, third]


def pack_rows(x, lanes, total):
    rows = []
    terms = split_terms(x)
    for b in range(x.shape[1] // lanes):
        rows += [t[:, b * lanes : (b + 1) * lanes] for t in terms]
    used = sum(r.shape[0] for r in rows)
    if total > used:
        rows.append(jnp.zeros((total - used, lanes), F))
    return jnp.concatenate(rows, axis=0).astype(B)


def unpack_rows(packed, n, blocks):
    packed = packed.astype(F)
    out = []
    for b in range(blocks):
        base = b * 3 * n
        out.append(
            packed[base : base + n]
            + packed[base + n : base + 2 * n]
            + packed[base + 2 * n : base + 3 * n]
        )
    return jnp.concatenate(out, axis=1)


def rope(x, table, direction):
    half = x.shape[1] // 2
    other = pltpu.roll(table, half, 1)
    front = lax.broadcasted_iota(jnp.int32, x.shape, 1) < half
    cos = jnp.where(front, table, other)
    sin = jnp.where(front, -other, table) * direction
    return x * cos + pltpu.roll(x, half, 1) * sin


def project_body(
    flag_ref, x_ref, knn_ref, gain_ref, wq_ref, wk_ref, wv_ref, table_ref,
    ship_ref, q_ref, k_ref, v_ref, normed_ref, off_ref, *, parts, heads, hd, spread,
):
    length = x_ref.shape[0]
    share = length // parts
    piece = share // 2
    chunk = length // 2
    columns = heads * hd
    groups = knn_ref.shape[1] // 2
    gain = gain_ref[...]
    for j in range(parts):
        r = slice(j * share, (j + 1) * share)
        x = x_ref[r, :].astype(F)
        factor = lax.rsqrt(jnp.mean(x * x, axis=1, keepdims=True) + epsilon)
        normed = (x * factor * gain).astype(B)
        table = table_ref[r, :]
        q = dot(normed, wq_ref[...], 1, 0)
        k = dot(normed, wk_ref[...], 1, 0)
        v_ref[r, :] = dot(normed, wv_ref[...], 1, 0).astype(B)
        q = jnp.concatenate(
            [rope(q[:, h * hd : (h + 1) * hd], table, 1.0) for h in range(heads)], axis=1
        ).astype(B)
        q_ref[r, :] = q
        k_ref[r, :] = jnp.concatenate(
            [rope(k[:, h * hd : (h + 1) * hd], table, 1.0) for h in range(heads)], axis=1
        ).astype(B)
        knn = knn_ref[r, :]
        start = lax.broadcasted_iota(jnp.int32, knn.shape, 1) * spread
        off = (knn - start).astype(F).T
        far = jnp.where(flag_ref[0] > 0, off[groups:], -1.0).astype(B)
        off = off[:groups].astype(B)
        for c in range(2):
            p = slice(c * piece, (c + 1) * piece)
            t = slice(j * piece, (j + 1) * piece)
            normed_ref[c, t, :] = normed[p]
            ship_ref[c, t, :] = q[p]
            off_ref[c, :, t] = off[:, p]
            lane = j * piece
            row = chunk + lane // columns * groups
            lane = lane % columns
            ship_ref[c, row : row + groups, lane : lane + piece] = far[:, p]


def project(flag, tokens, knn, gain, wq, wk, wv, table, parts, heads, spread):
    length, width = tokens.shape
    columns = wq.shape[1]
    groups = knn.shape[1] // 2
    chunk = length // 2
    body = functools.partial(
        project_body, parts=parts, heads=heads, hd=columns // heads, spread=spread
    )
    return call(
        body,
        [
            shape((2, chunk + chunk // columns * groups, columns), B),
            shape((length, columns), B),
            shape((length, columns), B),
            shape((length, columns), B),
            shape((2, chunk, width), B),
            shape((2, groups, chunk), B),
        ],
        "project",
        6 * length * width * columns,
        in_specs=[scalars()] + [whole()] * 7,
    )(flag, tokens, knn, gain, wq, wk, wv, table)


def pick(block_scores, offsets, heads, spread, gb):
    picked = [s[:gb] for s in block_scores]
    for t in range(1, spread):
        here = offsets == float(t)
        for h in range(heads):
            picked[h] = jnp.where(here, block_scores[h][t * gb : (t + 1) * gb], picked[h])
    return picked


def picked_scores(rows_ref, values, offs, heads, hd, spread, gb):
    rows = gb * spread
    wide = offs.astype(F)
    out = [[] for _ in range(heads)]
    for b in range(offs.shape[0] // gb):
        scores = [
            dot(
                rows_ref[h, b * rows : (b + 1) * rows, :], values[:, h * hd : (h + 1) * hd], 1, 1
            )
            for h in range(heads)
        ]
        picked = pick(scores, wide[b * gb : (b + 1) * gb], heads, spread, gb)
        for h in range(heads):
            out[h].append(picked[h])
    return [jnp.concatenate(o, axis=0) for o in out]


def spread_dot(rows_ref, h, picked, offs, spread, gb):
    rows = gb * spread
    total = None
    zero = jnp.zeros((gb, picked.shape[1]), B)
    for b in range(offs.shape[0] // gb):
        p = picked[b * gb : (b + 1) * gb]
        o = offs[b * gb : (b + 1) * gb]
        wide = jnp.concatenate(
            [jnp.where(o == jnp.asarray(t, B), p, zero) for t in range(spread)], axis=0
        )
        part = dot(rows_ref[h, b * rows : (b + 1) * rows, :], wide, 0, 0)
        total = part if total is None else total + part
    return total


def attend(q, offs, k_ref, v_ref, sel_ref, heads, hd, spread):
    outs, sums = [], []
    picked = picked_scores(k_ref, q, offs, heads, hd, spread, GROUP_BLOCK)
    for h in range(heads):
        x = picked[h] * hd**-0.5
        sel_ref[h] = x
        peak = jnp.max(x, axis=0, keepdims=True)
        p = jnp.exp(x - peak)
        total = jnp.sum(p, axis=0, keepdims=True)
        sums.append(peak + jnp.log(total))
        out = spread_dot(v_ref, h, p.astype(B), offs, spread, GROUP_BLOCK)
        outs.append((out / total).T.astype(B))
    return outs, sums


def own_attend_body(flag_ref, ship_ref, off_ref, k_ref, v_ref, o_ref, lse_ref, sel_ref, *, spread):
    heads, _, hd = k_ref.shape
    chunk = o_ref.shape[1]

    @pl.when(flag_ref[0] > 0)
    def _():
        outs, sums = attend(
            ship_ref[0, :chunk, :], off_ref[0], k_ref, v_ref, sel_ref.at[0], heads, hd, spread
        )
        for h in range(heads):
            o_ref[0, :, h * hd : (h + 1) * hd] = outs[h]
            lse_ref[0, h : h + 1, :] = sums[h]

    @pl.when(flag_ref[0] <= 0)
    def _():
        o_ref[...] = jnp.zeros_like(o_ref)
        lse_ref[...] = jnp.full_like(lse_ref, negative_big)


def resident(dims):
    return pl.BlockSpec(dims, lambda *i: (0,) * len(dims))


def own_attend(flag, ship, off, k, v, spread):
    heads, rows, hd = k.shape
    chunk = off.shape[2]
    groups = off.shape[1]
    columns = heads * hd
    by_chunk = lambda c: (c, 0, 0)
    return call(
        functools.partial(own_attend_body, spread=spread),
        [
            shape((2, chunk, columns), B),
            shape((2, heads, chunk), F),
            shape((2, heads, groups, chunk), F),
        ],
        "own_attend",
        16 * chunk * columns * rows,
        grid=(2,),
        in_specs=[
            scalars(),
            pl.BlockSpec((1,) + ship.shape[1:], by_chunk),
            pl.BlockSpec((1, groups, chunk), by_chunk),
            resident(k.shape),
            resident(v.shape),
        ],
        out_specs=[
            pl.BlockSpec((1, chunk, columns), by_chunk),
            pl.BlockSpec((1, heads, chunk), by_chunk),
            pl.BlockSpec((1, heads, groups, chunk), lambda c: (c, 0, 0, 0)),
        ],
    )(flag, ship, off, k, v)


def shipped_offsets(refs, chosen, chunk, groups, columns):
    blocks = chunk // columns
    index = (0, slice(chunk, chunk + blocks * groups), slice(None))
    packed = choose(refs, index, chosen)
    return jnp.concatenate([packed[b * groups : (b + 1) * groups] for b in range(blocks)], axis=1)


def their_attend_body(chosen_ref, *refs, count, spread, chunk, groups):
    ships = refs[:count]
    k_ref, v_ref, o_ref, sel_ref, off_ref, flag_ref = refs[count:]
    heads, _, hd = k_ref.shape
    columns = heads * hd
    chosen = chosen_ref[0]
    offs = shipped_offsets(ships, chosen, chunk, groups, columns)
    off_ref[...] = offs
    on = jnp.max(offs[:1, :128].astype(F)) >= 0
    flag_ref[0] = on.astype(jnp.int32)

    @pl.when(on)
    def _():
        q = choose(ships, (0, slice(0, chunk), slice(None)), chosen)
        outs, sums = attend(q, offs, k_ref, v_ref, sel_ref, heads, hd, spread)
        for h in range(heads):
            o_ref[:chunk, h * hd : (h + 1) * hd] = outs[h]
        o_ref[chunk:, :] = pack_rows(
            jnp.concatenate(sums, axis=0), columns, o_ref.shape[0] - chunk
        )

    @pl.when(jnp.logical_not(on))
    def _():
        o_ref[:chunk, :] = jnp.zeros((chunk, columns), B)
        o_ref[chunk:, :] = pack_rows(
            jnp.full((heads, chunk), negative_big, F), columns, o_ref.shape[0] - chunk
        )


def padded_rows(n):
    return -(-n // 16) * 16


def their_attend(c, chosen, ships, k, v, spread, groups):
    heads, rows, hd = k.shape
    columns = heads * hd
    chunk = ships[0].shape[1] * columns // (columns + groups)
    extra = padded_rows(3 * heads * chunk // columns)
    return call(
        functools.partial(
            their_attend_body, count=len(ships), spread=spread, chunk=chunk, groups=groups
        ),
        [
            shape((chunk + extra, columns), B),
            shape((heads, groups, chunk), F),
            shape((groups, chunk), B),
            shape((1,), jnp.int32),
        ],
        "their_attend",
        8 * chunk * columns * rows,
        grid=(1,),
        in_specs=[scalars()]
        + [pl.BlockSpec((1,) + s.shape[1:], lambda i: (c, 0, 0)) for s in ships]
        + [resident(k.shape), resident(v.shape)],
        out_specs=[
            resident((chunk + extra, columns)),
            resident((heads, groups, chunk)),
            resident((groups, chunk)),
            scalars(),
        ],
    )(chosen, *ships, k, v)


def score_gradients(g, offs, log_total, delta, sel_ref, v_ref, heads, hd, spread):
    picked = picked_scores(v_ref, g, offs, heads, hd, spread, GROUP_BLOCK)
    return [
        (jnp.exp(sel_ref[h] - log_total[h : h + 1]) * (picked[h] - delta[h : h + 1])).astype(B)
        for h in range(heads)
    ]


def own_backward_body(
    flag_ref, ship_ref, st_ref, sel_ref, off_ref, k_ref, v_ref, local_ref, dq_ref, *, spread
):
    heads, _, hd = k_ref.shape

    @pl.when(flag_ref[0] > 0)
    def _():
        offs = off_ref[0]
        stats = st_ref[0]
        ds = score_gradients(
            ship_ref[...], offs, stats[:heads], stats[heads:], sel_ref.at[0], v_ref, heads, hd,
            spread
        )
        for h in range(heads):
            c = slice(h * hd, (h + 1) * hd)
            out = spread_dot(k_ref, h, ds[h], offs, spread, GROUP_BLOCK)
            dq_ref[0, :, c] = local_ref[0, :, c] + (out * hd**-0.5).T

    @pl.when(flag_ref[0] <= 0)
    def _():
        dq_ref[...] = local_ref[...]


def own_backward(flag, ship, stats, sel, off, k, v, local, spread):
    heads, rows, hd = k.shape
    chunk = off.shape[2]
    groups = off.shape[1]
    columns = heads * hd
    by_chunk = lambda c: (c, 0, 0)
    return call(
        functools.partial(own_backward_body, spread=spread),
        shape((2, chunk, columns), F),
        "own_backward",
        16 * chunk * columns * rows,
        grid=(2,),
        in_specs=[
            scalars(),
            pl.BlockSpec((chunk, columns), lambda c: (c, 0)),
            pl.BlockSpec((1, 2 * heads, chunk), by_chunk),
            pl.BlockSpec((1, heads, groups, chunk), lambda c: (c, 0, 0, 0)),
            pl.BlockSpec((1, groups, chunk), by_chunk),
            resident(k.shape),
            resident(v.shape),
            pl.BlockSpec((1, chunk, columns), by_chunk),
        ],
        out_specs=pl.BlockSpec((1, chunk, columns), by_chunk),
    )(flag, ship, stats, sel, off, k, v, local)


def their_backward_body(chosen_ref, flag_ref, *refs, count, spread, chunk):
    ships = refs[:count]
    sel0, sel1, off0, off1, k_ref, v_ref, dq_ref = refs[count:]
    heads, _, hd = k_ref.shape
    columns = heads * hd
    blocks = chunk // columns
    extra = padded_rows(6 * heads * blocks)
    chosen = chosen_ref[0]
    on = flag_ref[0] > 0

    @pl.when(on)
    def _():
        for c, (sel_ref, off_ref) in enumerate(((sel0, off0), (sel1, off1))):
            offs = off_ref[...]
            g = choose(ships, (slice(c * chunk, (c + 1) * chunk), slice(None)), chosen)
            row = 2 * chunk + c * extra
            stats = unpack_rows(
                choose(ships, (slice(row, row + extra), slice(None)), chosen), 2 * heads, blocks
            )
            ds = score_gradients(
                g, offs, stats[:heads], stats[heads:], sel_ref, v_ref, heads, hd, spread
            )
            for h in range(heads):
                out = spread_dot(k_ref, h, ds[h], offs, spread, GROUP_BLOCK)
                dq_ref[c * chunk : (c + 1) * chunk, h * hd : (h + 1) * hd] = (
                    (out * hd**-0.5).T.astype(B)
                )

    @pl.when(jnp.logical_not(on))
    def _():
        dq_ref[...] = jnp.zeros_like(dq_ref)


def their_backward(chosen, flag, ships, sels, offs, k, v, spread):
    heads, rows, hd = k.shape
    columns = heads * hd
    chunk = offs[0].shape[1]
    return call(
        functools.partial(their_backward_body, count=len(ships), spread=spread, chunk=chunk),
        shape((2 * chunk, columns), B),
        "their_backward",
        16 * chunk * columns * rows,
        in_specs=[scalars(), scalars()] + [whole()] * (len(ships) + 6),
    )(chosen, flag, *ships, *sels, *offs, k, v)


def causal_scores(k, q, w, scale):
    s = dot(k, q, 1, 1) * scale
    n = k.shape[0]
    key = lax.broadcasted_iota(jnp.int32, (w, w), 0)
    query = lax.broadcasted_iota(jnp.int32, (w, w), 1)
    diagonal = jnp.where(key <= query, s[n - w :], negative_big)
    return diagonal if n == w else jnp.concatenate([s[: n - w], diagonal], axis=0)


def local_forward_body(q_ref, k_ref, v_ref, o_ref, lse_ref, *, heads, parts):
    length, columns = q_ref.shape
    hd = columns // heads
    w = length // parts
    piece = w // 2
    for h in range(heads):
        c = slice(h * hd, (h + 1) * hd)
        for i in range(parts):
            n = (i + 1) * w
            s = causal_scores(k_ref[:n, c], q_ref[i * w : n, c], w, hd**-0.5)
            peak = jnp.max(s, axis=0, keepdims=True)
            p = jnp.exp(s - peak)
            total = jnp.sum(p, axis=0, keepdims=True)
            lse = peak + jnp.log(total)
            out = (dot(v_ref[:n, c], p.astype(B), 0, 0) / total).T.astype(B)
            t = slice(i * piece, (i + 1) * piece)
            for a in range(2):
                o_ref[a, t, c] = out[a * piece : (a + 1) * piece]
                lse_ref[a, h : h + 1, t] = lse[:, a * piece : (a + 1) * piece]


def local_forward(q, k, v, heads, parts):
    length, columns = q.shape
    return call(
        functools.partial(local_forward_body, heads=heads, parts=parts),
        [shape((2, length // 2, columns), B), shape((2, heads, length // 2), F)],
        "local_forward",
        4 * length * length * columns,
        in_specs=[whole()] * 3,
    )(q, k, v)


def local_backward_body(
    q_ref, k_ref, v_ref, ship_ref, st_ref, table_ref, dq_ref, dkv_ref, dk_ref, dv_ref,
    *, heads, parts
):
    length, columns = q_ref.shape
    hd = columns // heads
    w = length // parts
    piece = w // 2
    chunk = length // 2
    scale = hd**-0.5
    for h in range(heads):
        c = slice(h * hd, (h + 1) * hd)
        for i in reversed(range(parts)):
            n = (i + 1) * w
            r = slice(i * w, n)
            t = slice(i * piece, (i + 1) * piece)
            g = jnp.concatenate(
                [ship_ref[a * chunk + i * piece : a * chunk + (i + 1) * piece, c] for a in range(2)],
                axis=0,
            )
            stats = jnp.concatenate([st_ref[a, :, t] for a in range(2)], axis=1)
            s = causal_scores(k_ref[:n, c], q_ref[r, c], w, scale)
            p = jnp.exp(s - stats[h : h + 1])
            dp = dot(v_ref[:n, c], g, 1, 1)
            ds = (p * (dp - stats[heads + h : heads + h + 1])).astype(B)
            dq = (dot(k_ref[:n, c], ds, 0, 0) * scale).T
            for a in range(2):
                dq_ref[a, t, c] = dq[a * piece : (a + 1) * piece]
            dk = dot(ds, q_ref[r, c], 1, 0) * scale
            dv = dot(p.astype(B), g, 1, 0)
            if i == parts - 1:
                dk_ref[:n, :] = dk
                dv_ref[:n, :] = dv
            else:
                dk_ref[:n, :] += dk
                dv_ref[:n, :] += dv
        dk = rope(dk_ref[...], table_ref[...], -1.0).astype(B)
        dv = dv_ref[...].astype(B)
        for i in range(parts):
            t = slice(i * piece, (i + 1) * piece)
            for a in range(2):
                r = slice(i * w + a * piece, i * w + (a + 1) * piece)
                dkv_ref[a, t, c] = dk[r]
                dkv_ref[a, t, columns + h * hd : columns + (h + 1) * hd] = dv[r]


def local_backward(q, k, v, ship, stats, table, heads, parts):
    length, columns = q.shape
    hd = columns // heads
    return call(
        functools.partial(local_backward_body, heads=heads, parts=parts),
        [shape((2, length // 2, columns), F), shape((2, length // 2, 2 * columns), B)],
        "local_backward",
        10 * length * length * columns,
        in_specs=[whole()] * 6,
        scratch_shapes=[pltpu.VMEM((length, hd), F)] * 2,
    )(q, k, v, ship, stats, table)


def merge_body(
    chosen_ref, lo_ref, ll_ref, oo_ref, ol_ref, *refs, count, heads
):
    ships = refs[:count]
    att_ref, total_ref = refs[count:]
    chunk, columns = att_ref.shape
    hd = columns // heads
    chosen = chosen_ref[0]
    far = choose(ships, (slice(0, chunk), slice(None)), chosen).astype(F)
    packed = choose(ships, (slice(chunk, ships[0].shape[0]), slice(None)), chosen)
    far_lse = unpack_rows(packed, heads, chunk // columns)
    local_lse = ll_ref[0]
    own_lse = ol_ref[0]
    peak = jnp.maximum(jnp.maximum(local_lse, own_lse), far_lse)
    weights = [jnp.exp(l - peak) for l in (local_lse, own_lse, far_lse)]
    total = weights[0] + weights[1] + weights[2]
    total_ref[...] = peak + jnp.log(total)
    weights = [x / total for x in weights]
    stacked = jnp.concatenate(weights + [jnp.zeros((8 - 3 * heads % 8, chunk), F)], axis=0).T
    for h in range(heads):
        c = slice(h * hd, (h + 1) * hd)
        att_ref[:, c] = (
            lo_ref[0, :, c].astype(F) * stacked[:, h : h + 1]
            + oo_ref[0, :, c].astype(F) * stacked[:, heads + h : heads + h + 1]
            + far[:, c] * stacked[:, 2 * heads + h : 2 * heads + h + 1]
        ).astype(B)


def merge(c, chosen, local, own, ships, heads):
    _, chunk, columns = local[0].shape
    part = pl.BlockSpec((1, chunk, columns), lambda i: (c, 0, 0))
    row = pl.BlockSpec((1, heads, chunk), lambda i: (c, 0, 0))
    return call(
        functools.partial(merge_body, count=len(ships), heads=heads),
        [shape((chunk, columns), B), shape((heads, chunk), F)],
        "merge",
        grid=(1,),
        in_specs=[scalars(), part, row, part, row] + [resident(s.shape) for s in ships],
        out_specs=[resident((chunk, columns)), resident((heads, chunk))],
    )(chosen, *local, *own, *ships)


def feed_body(me_ref, *refs, parts):
    pieces = refs[:parts]
    outs = refs[parts : 2 * parts]
    (x_ref, g_ref, gain_ref, wg_ref, wu_ref, wd_ref) = refs[2 * parts : 2 * parts + 6]
    (normed_ref, gu_ref, hidden_ref, gn_ref, down_ref, own_ref) = refs[2 * parts + 6 :]
    me = me_ref[0]
    piece = x_ref.shape[2]
    width = x_ref.shape[3]
    ff = wg_ref.shape[1]
    order = list(range(parts.bit_length() - 1))
    for half in range(2):
        js = range(half * parts // 2, (half + 1) * parts // 2)
        r = slice(half * parts // 2 * piece, (half + 1) * parts // 2 * piece)
        middle = x_ref[js[0] : js[-1] + 1, 0].reshape(-1, width).astype(F)
        for p, w in zip(pieces, outs):
            middle = middle + dot(p[r, :], w[...], 1, 0)
        for a, j in enumerate(js):
            @pl.when(me == j)
            def _(a=a):
                own_ref[...] = middle[a * piece : (a + 1) * piece]
        factor = lax.rsqrt(jnp.mean(middle * middle, axis=1, keepdims=True) + epsilon)
        normed = (middle * factor * gain_ref[...]).astype(B)
        normed_ref[r, :] = normed
        gate = dot(normed, wg_ref[...], 1, 0)
        upper = dot(normed, wu_ref[...], 1, 0)
        s = jax.nn.sigmoid(gate)
        silu = gate * s
        hidden = (silu * upper).astype(B)
        hidden_ref[r, :] = hidden
        grad_hidden = dot(g_ref[js[0] : js[-1] + 1, 0].reshape(-1, width), wd_ref[...], 1, 1)
        grad_gate = (grad_hidden * upper * s * (1.0 + gate * (1.0 - s))).astype(B)
        grad_upper = (grad_hidden * silu).astype(B)
        gu_ref[r, :ff] = grad_gate
        gu_ref[r, ff:] = grad_upper
        grad_normed = dot(grad_gate, wg_ref[...], 1, 1) + dot(grad_upper, wu_ref[...], 1, 1)
        down = dot(hidden, wd_ref[...], 1, 0)
        for a, j in enumerate(js):
            place = slot_place(jnp.bitwise_xor(me, j), order)
            gn_ref[place] = grad_normed[a * piece : (a + 1) * piece].astype(B)
            down_ref[place] = down[a * piece : (a + 1) * piece].astype(B)


def feed(c, me, pieces, outs, tokens, cotangent, gain, wg, wu, wd):
    parts, _, piece, width = tokens.shape
    chunk = parts * piece
    ff = wg.shape[1]
    part = pl.BlockSpec((parts, 1, piece, width), lambda i: (0, c, 0, 0))
    results = [
        shape((chunk, width), B),
        shape((chunk, 2 * ff), B),
        shape((chunk, ff), B),
        shape((parts, piece, width), B),
        shape((parts, piece, width), B),
        shape((piece, width), F),
    ]
    return call(
        functools.partial(feed_body, parts=parts),
        results,
        "feed",
        2 * chunk * width * (width + 6 * ff),
        grid=(1,),
        in_specs=[scalars()]
        + [resident(p.shape) for p in pieces]
        + [resident(w.shape) for w in outs]
        + [part, part]
        + [resident(a.shape) for a in (gain, wg, wu, wd)],
        out_specs=[resident(r.shape) for r in results],
    )(me, *pieces, *outs, tokens, cotangent, gain, wg, wu, wd)


def middle_back_body(me_ref, gn_ref, r1_ref, r2_ref, m_ref, g_ref, gain_ref, gm_ref, gb_ref, ga_ref):
    total = gn_ref[0].astype(F) + r1_ref[0].astype(F) + r2_ref[...].astype(F)
    middle = m_ref[...]
    factor = lax.rsqrt(jnp.mean(middle * middle, axis=1, keepdims=True) + epsilon)
    scaled = total * gain_ref[...]
    grad = (
        g_ref[0, 0].astype(F)
        + factor * scaled
        - middle * (factor * factor * factor) * jnp.mean(middle * scaled, axis=1, keepdims=True)
    )
    gm_ref[...] = grad
    gb_ref[...] = grad.astype(B)
    ga_ref[...] = jnp.sum(total * middle * factor, axis=0, keepdims=True)


def middle_back(c, me, gn, r1, r2, middle, cotangent, gain):
    piece, width = middle.shape
    fixed = lambda dims: pl.BlockSpec(dims, lambda i, m: (0,) * len(dims))
    results = [shape((piece, width), F), shape((piece, width), B), shape((1, width), F)]
    return call(
        middle_back_body,
        results,
        "middle_back",
        grid_spec=pltpu.PrefetchScalarGridSpec(
            num_scalar_prefetch=1,
            grid=(1,),
            in_specs=[
                fixed((1, piece, width)),
                fixed((1, piece, width)),
                fixed((piece, width)),
                fixed((piece, width)),
                pl.BlockSpec((1, 1, piece, width), lambda i, m: (m[0], c, 0, 0)),
                fixed((1, width)),
            ],
            out_specs=[fixed(r.shape) for r in results],
        ),
    )(me, gn, r1, r2, middle, cotangent, gain)


def branch_body(me_ref, *refs, parts, heads, distances):
    pieces = refs[: 2 * parts]
    w_ref, att0, att1, lse0, lse1, gb_ref, ship_ref, st_ref = refs[2 * parts :]
    me = me_ref[0]
    piece = pieces[0].shape[0]
    chunk = parts * piece
    columns = w_ref.shape[0]
    hd = columns // heads
    extra = padded_rows(6 * heads * (chunk // columns))
    for c, (att, lse) in enumerate(((att0, lse0), (att1, lse1))):
        for a, k in enumerate(distances):
            start = pl.multiple_of(jnp.bitwise_xor(me, k) * piece, piece)
            gb_ref[c, pl.ds(start, piece), :] = pieces[c * parts + a][...]
        grad = dot(gb_ref[c], w_ref[...], 1, 1).astype(B)
        ship_ref[c * chunk : (c + 1) * chunk, :] = grad
        product = grad.astype(F) * att[...].astype(F)
        rows = [lse[...]]
        for h in range(heads):
            rows.append(
                jnp.sum(product[:, h * hd : (h + 1) * hd].T, axis=0, keepdims=True)
            )
        stats = jnp.concatenate(rows, axis=0)
        st_ref[c] = stats
        row = 2 * chunk + c * extra
        ship_ref[row : row + extra, :] = pack_rows(stats, columns, extra)


def branch(me, pieces, distances, w_output, att, lse, heads):
    parts = len(distances)
    piece, width = pieces[0].shape
    chunk = parts * piece
    columns = w_output.shape[0]
    extra = padded_rows(6 * heads * (chunk // columns))
    return call(
        functools.partial(branch_body, parts=parts, heads=heads, distances=tuple(distances)),
        [
            shape((2, chunk, width), B),
            shape((2 * (chunk + extra), columns), B),
            shape((2, 2 * heads, chunk), F),
        ],
        "branch",
        4 * chunk * width * columns,
        in_specs=[scalars()] + [whole()] * (2 * parts + 5),
    )(me, *pieces, w_output, *att, *lse)


def store_slots(place_ref, out_ref, first, value, c):
    rows = out_ref.shape[1]
    for a in range(value.shape[0] // rows):
        out_ref[place_ref[first + a], :, c] = value[a * rows : (a + 1) * rows].astype(B)


def feed_grads_body(place_ref, n0, n1, gu0, gu1, h0, h1, g_ref, out_ref):
    block = n0.shape[1]
    per = block // out_ref.shape[1]
    first = pl.program_id(0) * per
    gu_width = gu0.shape[1]
    store_slots(
        place_ref, out_ref, first,
        dot(n0[...], gu0[...], 0, 0) + dot(n1[...], gu1[...], 0, 0), slice(0, gu_width),
    )
    g0 = g_ref[:, 0].reshape(-1, block)
    g1 = g_ref[:, 1].reshape(-1, block)
    store_slots(
        place_ref, out_ref, first,
        dot(g0, h0[...], 0, 0) + dot(g1, h1[...], 0, 0), slice(gu_width, out_ref.shape[2]),
    )


def feed_grads(place, normed, gu, hidden, cotangent, docs):
    chunk, width = normed[0].shape
    total = gu[0].shape[1] + hidden[0].shape[1]
    block = max(width // docs, 256)
    parts, _, piece, _ = cotangent.shape
    column = pl.BlockSpec((chunk, block), lambda i: (0, i))
    return call(
        feed_grads_body,
        shape((docs, width // docs, total), B),
        "feed_grads",
        4 * chunk * width * total,
        grid=(width // block,),
        in_specs=[scalars(), column, column]
        + [resident(a.shape) for a in (*gu, *hidden)]
        + [pl.BlockSpec((parts, 2, piece, block), lambda i: (0, 0, 0, i))],
        out_specs=resident((docs, width // docs, total)),
    )(place, *normed, *gu, *hidden, cotangent)


def key_grads_body(place_ref, n_ref, dkv_ref, gb_ref, att0, att1, wk_ref, wv_ref, out_ref, gn_ref):
    columns = wk_ref.shape[1]
    for c in range(2):
        gn_ref[c] = (
            dot(dkv_ref[c, :, :columns], wk_ref[...], 1, 1)
            + dot(dkv_ref[c, :, columns:], wv_ref[...], 1, 1)
        ).astype(B)
    store_slots(
        place_ref, out_ref, 0,
        dot(n_ref[0], dkv_ref[0], 0, 0) + dot(n_ref[1], dkv_ref[1], 0, 0), slice(0, 2 * columns),
    )
    store_slots(
        place_ref, out_ref, 0,
        dot(gb_ref[0], att0[...], 0, 0) + dot(gb_ref[1], att1[...], 0, 0),
        slice(2 * columns, 3 * columns),
    )


def key_grads(place, normed, dkv, gb, att, wk, wv, docs):
    _, chunk, width = normed.shape
    columns = wk.shape[1]
    return call(
        key_grads_body,
        [shape((docs, width // docs, 3 * columns), B), shape((2, chunk, width), B)],
        "key_grads",
        20 * chunk * width * columns,
        in_specs=[scalars()] + [whole()] * 7,
    )(place, normed, dkv, gb, *att, wk, wv)


def query_grads_body(
    chosen_ref, me_ref, place_ref, dq_ref, *refs, count, parts, heads
):
    ships = refs[:count]
    n_ref, part_ref, wq_ref, table_ref, x_ref = refs[count : count + 5]
    out_ref, gn_ref, gain_ref = refs[count + 5 :]
    chosen = chosen_ref[0]
    me = me_ref[0]
    _, chunk, columns = dq_ref.shape
    piece = chunk // parts
    hd = columns // heads
    width = wq_ref.shape[0]
    order = list(range(parts.bit_length() - 1))
    grads = None
    gain = None
    for c in range(2):
        far = choose(ships, (slice(c * chunk, (c + 1) * chunk), slice(None)), chosen)
        dq = dq_ref[c] + far.astype(F)
        table = table_ref[:, c].reshape(chunk, hd)
        low = jnp.concatenate(
            [rope(dq[:, h * hd : (h + 1) * hd], table, -1.0) for h in range(heads)], axis=1
        ).astype(B)
        gn = dot(low, wq_ref[...], 1, 1) + part_ref[c].astype(F)
        for j in range(parts):
            place = slot_place(jnp.bitwise_xor(me, j), order)
            gn_ref[place, c * piece : (c + 1) * piece, :] = gn[j * piece : (j + 1) * piece].astype(
                B
            )
        x = x_ref[:, c].reshape(chunk, width).astype(F)
        factor = lax.rsqrt(jnp.mean(x * x, axis=1, keepdims=True) + epsilon)
        part = jnp.sum(gn * x * factor, axis=0, keepdims=True)
        gain = part if gain is None else gain + part
        part = dot(n_ref[c], low, 0, 0)
        grads = part if grads is None else grads + part
    gain_ref[...] = gain
    store_slots(place_ref, out_ref, 0, grads, slice(0, columns))


def query_grads(chosen, me, place, dq, ships, normed, part, wq, table, tokens, docs, heads):
    _, chunk, width = normed.shape
    columns = wq.shape[1]
    parts = tokens.shape[0]
    return call(
        functools.partial(query_grads_body, count=len(ships), parts=parts, heads=heads),
        [
            shape((docs, width // docs, columns), B),
            shape((parts, 2 * chunk // parts, width), B),
            shape((1, width), F),
        ],
        "query_grads",
        8 * chunk * width * columns,
        in_specs=[scalars()] * 3 + [whole()] * (len(ships) + 6),
    )(chosen, me, place, dq, *ships, normed, part, wq, table, tokens)


def tokens_back_body(me_ref, gn_ref, r1_ref, r2_ref, x_ref, gm0, gm1, gain_ref, out_ref):
    total = gn_ref[0].astype(F) + r1_ref[0].astype(F) + r2_ref[...].astype(F)
    x = x_ref[...].astype(F)
    factor = lax.rsqrt(jnp.mean(x * x, axis=1, keepdims=True) + epsilon)
    scaled = total * gain_ref[...]
    grad = factor * scaled - x * (factor * factor * factor) * jnp.mean(
        x * scaled, axis=1, keepdims=True
    )
    piece = gm0.shape[0]
    out_ref[:piece, :] = (gm0[...] + grad[:piece]).astype(B)
    out_ref[piece:, :] = (gm1[...] + grad[piece:]).astype(B)


def tokens_back(me, gn, r1, r2, tokens, gm, gain):
    _, share, width = gn.shape
    fixed = lambda dims: pl.BlockSpec(dims, lambda i, m: (0,) * len(dims))
    return call(
        tokens_back_body,
        shape((share, width), B),
        "tokens_back",
        grid_spec=pltpu.PrefetchScalarGridSpec(
            num_scalar_prefetch=1,
            grid=(1,),
            in_specs=[
                fixed((1, share, width)),
                fixed((1, share, width)),
                fixed((share, width)),
                pl.BlockSpec((share, width), lambda i, m: (m[0], 0)),
                fixed(gm[0].shape),
                fixed(gm[1].shape),
                fixed((1, width)),
            ],
            out_specs=fixed((share, width)),
        ),
    )(me, gn, r1, r2, tokens, *gm, gain)


def rotate_table(length, hd):
    half = hd // 2
    position = np.arange(length, dtype=np.float32)
    inverse = np.exp(
        -np.log(np.float32(10000.0)) * np.arange(half, dtype=np.float32) * np.float32(2.0) / hd
    ).astype(np.float32)
    angles = position[:, None] * inverse[None, :]
    return jnp.asarray(np.concatenate([np.cos(angles), np.sin(angles)], axis=1).astype(np.float32))


def to_all(array):
    bits = axis_bits("dp")
    got = {b: swap(array, "dp", 1 << b) for b in reversed(range(bits))}
    return [got[b] for b in range(bits)]


def gather_tensor(value):
    pieces, distances = [value], [0]
    for b in reversed(range(axis_bits("tensor"))):
        pieces = pieces + [swap(p, "tensor", 1 << b) for p in pieces]
        distances = distances + [k ^ (1 << b) for k in distances]
    return pieces, distances


def halve(value, axis, bit):
    half = value.shape[0] // 2
    return swap(value[half:], axis, 1 << bit)


def add_low(a, b):
    return (a.astype(F) + b.astype(F)).astype(B)


def scatter_slots(value, axis, order):
    for b in order:
        half = value.shape[0] // 2
        got = halve(value, axis, b)
        if half == 1:
            return value[0].astype(F) + got[0].astype(F)
        value = add_low(value[:half], got)
    return value[0].astype(F)


def scatter_two(value):
    first = halve(value, "tensor", 0)
    second = swap(add_low(value[1], first[1]), "tensor", 2)
    return first, second


def per_device(
    tokens,
    w_query,
    w_key,
    w_value,
    w_output,
    w_gate,
    w_up,
    w_down,
    gain_attn,
    gain_mlp,
    cache_keys,
    cache_values,
    knn_index,
    memory_flag,
    pairing,
    cotangent,
):
    length, width = tokens.shape
    parts = lax.axis_size("tensor")
    docs = lax.axis_size("dp")
    piece = length // parts // 2
    me = lax.axis_index("tensor").astype(jnp.int32).reshape(1)
    heads = cache_keys.shape[1]
    rows = cache_keys.shape[2]
    hd = cache_keys.shape[3]
    columns = heads * hd
    groups = knn_index.shape[1] // 2
    spread = rows // groups
    ff = w_gate.shape[1]
    flag = memory_flag[:1].astype(jnp.int32)
    my_doc = lax.axis_index("dp").astype(jnp.int32)
    difference = jnp.bitwise_xor(pairing[0].astype(jnp.int32), my_doc)
    chosen = jnp.zeros((), jnp.int32)
    for b in range(1, axis_bits("dp")):
        chosen = jnp.where(difference == (1 << b), b, chosen)
    chosen = chosen.reshape(1)
    dp_order = list(range(axis_bits("dp")))
    place = slot_place(jnp.bitwise_xor(jnp.arange(docs, dtype=jnp.int32), my_doc), dp_order)
    place = place.astype(jnp.int32)
    table = rotate_table(length, hd)
    gain_a = gain_attn.reshape(1, width)
    gain_m = gain_mlp.reshape(1, width)
    tokens_view = tokens.reshape(parts, 2, piece, width)
    cotangent_view = cotangent.reshape(parts, 2, piece, width)
    table_view = table.reshape(parts, 2, piece, hd)

    def ordered_rows(cache):
        return (
            cache.reshape(heads, groups // GROUP_BLOCK, GROUP_BLOCK, spread, hd)
            .transpose(0, 1, 3, 2, 4)
            .reshape(heads, rows, hd)
        )

    ship, q, k, v, normed_low, own_off = project(
        flag, tokens, knn_index, gain_a, w_query, w_key, w_value, table, parts, heads, spread
    )
    ships = to_all(ship)
    out_weights, distances = gather_tensor(w_output)
    stored_keys = ordered_rows(cache_keys[0])
    stored_values = ordered_rows(cache_values[0])
    local = local_forward(q, k, v, heads, parts)
    own_out, own_lse, own_sel = own_attend(
        flag, ship, own_off, stored_keys, stored_values, spread
    )
    att, lse, their_sel, their_off, feeds = [], [], [], [], []
    gm, gb_pieces, gain_parts = [], [], []
    returned = []
    for c in range(2):
        packed, sel, off, their_flag = their_attend(
            c, chosen, ships, stored_keys, stored_values, spread, groups
        )
        their_sel.append(sel)
        their_off.append(off)
        returned.append(to_all(packed))
    for c in range(2):
        a, total = merge(c, chosen, local, (own_out, own_lse), returned[c], heads)
        att.append(a)
        lse.append(total)

        pieces, _ = gather_tensor(a)
        feeds.append(
            feed(
                c, me, pieces, out_weights, tokens_view, cotangent_view, gain_m, w_gate, w_up,
                w_down,
            )
        )
    for c in range(2):
        gn, middle = feeds[c][3], feeds[c][5]
        first, second = scatter_two(gn)
        grad_middle, low, gain_part = middle_back(
            c, me, gn, first, second, middle, cotangent_view, gain_m
        )
        gm.append(grad_middle)
        gain_parts.append(gain_part)
        gb_pieces += gather_tensor(low)[0]

    grad_branch, back_ship, stats = branch(me, gb_pieces, distances, w_output, att, lse, heads)
    back_ships = to_all(back_ship)
    local_dq, dkv = local_backward(q, k, v, back_ship, stats, table, heads, parts)
    dq = own_backward(
        flag, back_ship, stats, own_sel, own_off, stored_keys, stored_values, local_dq, spread
    )
    their_dq = their_backward(
        chosen, their_flag, back_ships, their_sel, their_off, stored_keys, stored_values, spread
    )
    dq_ships = to_all(their_dq)

    feed_sum = scatter_slots(
        feed_grads(
            place,
            [f[0] for f in feeds],
            [f[1] for f in feeds],
            [f[2] for f in feeds],
            cotangent_view,
            docs,
        ),
        "dp",
        dp_order,
    )
    output = []
    for c in range(2):
        down = feeds[c][4]
        first, second = scatter_two(down)
        output.append(
            feeds[c][5] + down[0].astype(F) + first[0].astype(F) + second.astype(F)
        )

    key_slots, gn_part = key_grads(
        place, normed_low, dkv, grad_branch, att, w_key, w_value, docs
    )
    key_sum = scatter_slots(key_slots, "dp", dp_order)
    query_slots, gn, gain_part = query_grads(
        chosen, me, place, dq, dq_ships, normed_low, gn_part, w_query, table_view, tokens_view,
        docs, heads
    )
    query_sum = scatter_slots(query_slots, "dp", dp_order)
    first, second = scatter_two(gn)
    grad_tokens = tokens_back(me, gn, first, second, tokens, gm, gain_a)
    gains = jnp.concatenate([gain_part, gain_parts[0] + gain_parts[1]], axis=0)
    gains = gains + sum(swap(gains, "tensor", t) for t in range(1, parts))
    for b in dp_order:
        gains = gains + swap(gains, "dp", 1 << b)
    gains = lax.dynamic_slice_in_dim(gains, my_doc * (width // docs), width // docs, 1)
    return (
        jnp.concatenate(output, axis=0).astype(B),
        grad_tokens,
        query_sum,
        key_sum[:, :columns],
        key_sum[:, columns : 2 * columns],
        key_sum[:, 2 * columns :].T,
        feed_sum[:, :ff],
        feed_sum[:, ff : 2 * ff],
        feed_sum[:, 2 * ff :].T,
        gains[0],
        gains[1],
    )


def solution(mesh):
    placed = (
        P("dp", None),
        P(None, "tensor"),
        P(None, "tensor"),
        P(None, "tensor"),
        P("tensor", None),
        P(None, "tensor"),
        P(None, "tensor"),
        P("tensor", None),
        P(),
        P(),
        P("dp", "tensor", None, None),
        P("dp", "tensor", None, None),
        P("dp", None),
        P("dp"),
        P("dp"),
        P("dp", None),
    )
    return jax.shard_map(
        per_device,
        mesh=mesh,
        in_specs=placed,
        out_specs=(
            P(("dp", "tensor"), None),
            P(("dp", "tensor"), None),
            P("dp", "tensor"),
            P("dp", "tensor"),
            P("dp", "tensor"),
            P("tensor", "dp"),
            P("dp", "tensor"),
            P("dp", "tensor"),
            P("tensor", "dp"),
            P("dp"),
            P("dp"),
        ),
        check_vma=False,
    )
```

```python
import functools

import jax
import jax.numpy as jnp
import numpy as np
from jax import lax
from jax.experimental import pallas as pl
from jax.experimental.pallas import tpu as pltpu
from jax.sharding import PartitionSpec as P

epsilon = 1e-05
negative_big = -1e30
F = jnp.float32
B = jnp.bfloat16
GROUP_BLOCK = 16


def dot(a, b, da, db):
    return lax.dot_general(a, b, (((da,), (db,)), ((), ())), preferred_element_type=F)


def swap(array, axis, bit):
    return lax.ppermute(array, axis, [(i, i ^ bit) for i in range(lax.axis_size(axis))])


def axis_bits(axis):
    return lax.axis_size(axis).bit_length() - 1


def call(body, out_shape, name, flops=0, limit=28, **options):
    kernel = pl.pallas_call(
        body,
        out_shape=out_shape,
        name=name,
        cost_estimate=pl.CostEstimate(flops=0, transcendentals=0, bytes_accessed=0),
        compiler_params=pltpu.CompilerParams(vmem_limit_bytes=limit << 20),
        **options,
    )
    specs = options.get("in_specs")

    def run(*args):
        if specs is not None:
            args = [
                pltpu.with_memory_space_constraint(a, pltpu.VMEM)
                if s.block_shape is None and s.memory_space is pltpu.VMEM
                else a
                for a, s in zip(args, specs)
            ]
        return kernel(*args)

    return run


def shape(dims, dtype):
    return jax.ShapeDtypeStruct(dims, dtype)


def whole():
    return pl.BlockSpec(memory_space=pltpu.VMEM)


def scalars():
    return pl.BlockSpec(memory_space=pltpu.SMEM)


def slot_place(difference, order):
    place = 0
    for b in order:
        place = place * 2 + ((difference >> b) & 1)
    return place


def store_half(refs, place, c, value, rows=slice(None)):
    half = refs[0].shape[0]
    value = value.astype(B)

    @pl.when(place < half)
    def _():
        refs[0][place, rows, c] = value

    @pl.when(place >= half)
    def _():
        refs[1][place - half, rows, c] = value


def choose(refs, index, chosen):
    value = refs[0][index]
    for b in range(1, len(refs)):
        value = jnp.where(chosen == b, refs[b][index], value)
    return value


def split_terms(x):
    first = x.astype(B).astype(F)
    second = (x - first).astype(B).astype(F)
    third = (x - first - second).astype(B).astype(F)
    return [first, second, third]


def pack_rows(x, lanes, total):
    rows = []
    terms = split_terms(x)
    for b in range(x.shape[1] // lanes):
        rows += [t[:, b * lanes : (b + 1) * lanes] for t in terms]
    used = sum(r.shape[0] for r in rows)
    if total > used:
        rows.append(jnp.zeros((total - used, lanes), F))
    return jnp.concatenate(rows, axis=0).astype(B)


def unpack_rows(packed, n, blocks):
    packed = packed.astype(F)
    out = []
    for b in range(blocks):
        base = b * 3 * n
        out.append(
            packed[base : base + n]
            + packed[base + n : base + 2 * n]
            + packed[base + 2 * n : base + 3 * n]
        )
    return jnp.concatenate(out, axis=1)


def rope(x, table, direction):
    half = x.shape[1] // 2
    other = pltpu.roll(table, half, 1)
    front = lax.broadcasted_iota(jnp.int32, x.shape, 1) < half
    cos = jnp.where(front, table, other)
    sin = jnp.where(front, -other, table) * direction
    return x * cos + pltpu.roll(x, half, 1) * sin


def project_body(
    flag_ref, x_ref, knn_ref, gain_ref, wq_ref, wk_ref, wv_ref, table_ref,
    ship_ref, q_ref, k_ref, v_ref, normed_ref, off_ref, *, parts, heads, hd, spread,
):
    length = x_ref.shape[0]
    share = length // parts
    piece = share // 2
    chunk = length // 2
    columns = heads * hd
    groups = knn_ref.shape[1] // 2
    gain = gain_ref[...]
    for j in range(parts):
        r = slice(j * share, (j + 1) * share)
        x = x_ref[r, :].astype(F)
        factor = lax.rsqrt(jnp.mean(x * x, axis=1, keepdims=True) + epsilon)
        normed = (x * factor * gain).astype(B)
        table = table_ref[r, :]
        q = dot(normed, wq_ref[...], 1, 0)
        k = dot(normed, wk_ref[...], 1, 0)
        v_ref[r, :] = dot(normed, wv_ref[...], 1, 0).astype(B)
        q = jnp.concatenate(
            [rope(q[:, h * hd : (h + 1) * hd], table, 1.0) for h in range(heads)], axis=1
        ).astype(B)
        q_ref[r, :] = q
        k_ref[r, :] = jnp.concatenate(
            [rope(k[:, h * hd : (h + 1) * hd], table, 1.0) for h in range(heads)], axis=1
        ).astype(B)
        knn = knn_ref[r, :]
        start = lax.broadcasted_iota(jnp.int32, knn.shape, 1) * spread
        off = (knn - start).astype(F).T
        far = jnp.where(flag_ref[0] > 0, off[groups:], -1.0).astype(B)
        off = off[:groups].astype(B)
        for c in range(2):
            p = slice(c * piece, (c + 1) * piece)
            t = slice(j * piece, (j + 1) * piece)
            normed_ref[c, t, :] = normed[p]
            ship_ref[c, t, :] = q[p]
            off_ref[c, :, t] = off[:, p]
            lane = j * piece
            row = chunk + lane // columns * groups
            lane = lane % columns
            ship_ref[c, row : row + groups, lane : lane + piece] = far[:, p]


def project(flag, tokens, knn, gain, wq, wk, wv, table, parts, heads, spread):
    length, width = tokens.shape
    columns = wq.shape[1]
    groups = knn.shape[1] // 2
    chunk = length // 2
    body = functools.partial(
        project_body, parts=parts, heads=heads, hd=columns // heads, spread=spread
    )
    return call(
        body,
        [
            shape((2, chunk + chunk // columns * groups, columns), B),
            shape((length, columns), B),
            shape((length, columns), B),
            shape((length, columns), B),
            shape((2, chunk, width), B),
            shape((2, groups, chunk), B),
        ],
        "project",
        6 * length * width * columns,
        in_specs=[scalars()] + [whole()] * 7,
    )(flag, tokens, knn, gain, wq, wk, wv, table)


def pick(block_scores, offsets, heads, spread, gb):
    picked = [s[:gb] for s in block_scores]
    for t in range(1, spread):
        here = offsets == float(t)
        for h in range(heads):
            picked[h] = jnp.where(here, block_scores[h][t * gb : (t + 1) * gb], picked[h])
    return picked


def picked_scores(rows_ref, values, offs, heads, hd, spread, gb):
    rows = gb * spread
    wide = offs.astype(F)
    out = [[] for _ in range(heads)]
    for b in range(offs.shape[0] // gb):
        scores = [
            dot(
                rows_ref[h, b * rows : (b + 1) * rows, :], values[:, h * hd : (h + 1) * hd], 1, 1
            )
            for h in range(heads)
        ]
        picked = pick(scores, wide[b * gb : (b + 1) * gb], heads, spread, gb)
        for h in range(heads):
            out[h].append(picked[h])
    return [jnp.concatenate(o, axis=0) for o in out]


def spread_dot(rows_ref, h, picked, offs, spread, gb):
    rows = gb * spread
    total = None
    zero = jnp.zeros((gb, picked.shape[1]), B)
    for b in range(offs.shape[0] // gb):
        p = picked[b * gb : (b + 1) * gb]
        o = offs[b * gb : (b + 1) * gb]
        wide = jnp.concatenate(
            [jnp.where(o == jnp.asarray(t, B), p, zero) for t in range(spread)], axis=0
        )
        part = dot(rows_ref[h, b * rows : (b + 1) * rows, :], wide, 0, 0)
        total = part if total is None else total + part
    return total


def attend(q, offs, k_ref, v_ref, sel_ref, heads, hd, spread):
    outs, sums = [], []
    picked = picked_scores(k_ref, q, offs, heads, hd, spread, GROUP_BLOCK)
    for h in range(heads):
        x = picked[h] * hd**-0.5
        sel_ref[h] = x
        peak = jnp.max(x, axis=0, keepdims=True)
        p = jnp.exp(x - peak)
        total = jnp.sum(p, axis=0, keepdims=True)
        sums.append(peak + jnp.log(total))
        out = spread_dot(v_ref, h, p.astype(B), offs, spread, GROUP_BLOCK)
        outs.append((out / total).T.astype(B))
    return outs, sums


def own_attend_body(flag_ref, ship_ref, off_ref, k_ref, v_ref, o_ref, lse_ref, sel_ref, *, spread):
    heads, _, hd = k_ref.shape
    chunk = o_ref.shape[1]

    @pl.when(flag_ref[0] > 0)
    def _():
        outs, sums = attend(
            ship_ref[0, :chunk, :], off_ref[0], k_ref, v_ref, sel_ref.at[0], heads, hd, spread
        )
        for h in range(heads):
            o_ref[0, :, h * hd : (h + 1) * hd] = outs[h]
            lse_ref[0, h : h + 1, :] = sums[h]

    @pl.when(flag_ref[0] <= 0)
    def _():
        o_ref[...] = jnp.zeros_like(o_ref)
        lse_ref[...] = jnp.full_like(lse_ref, negative_big)


def resident(dims):
    return pl.BlockSpec(dims, lambda *i: (0,) * len(dims))


def own_attend(flag, ship, off, k, v, spread):
    heads, rows, hd = k.shape
    chunk = off.shape[2]
    groups = off.shape[1]
    columns = heads * hd
    by_chunk = lambda c: (c, 0, 0)
    return call(
        functools.partial(own_attend_body, spread=spread),
        [
            shape((2, chunk, columns), B),
            shape((2, heads, chunk), F),
            shape((2, heads, groups, chunk), F),
        ],
        "own_attend",
        16 * chunk * columns * rows,
        grid=(2,),
        in_specs=[
            scalars(),
            pl.BlockSpec((1,) + ship.shape[1:], by_chunk),
            pl.BlockSpec((1, groups, chunk), by_chunk),
            resident(k.shape),
            resident(v.shape),
        ],
        out_specs=[
            pl.BlockSpec((1, chunk, columns), by_chunk),
            pl.BlockSpec((1, heads, chunk), by_chunk),
            pl.BlockSpec((1, heads, groups, chunk), lambda c: (c, 0, 0, 0)),
        ],
    )(flag, ship, off, k, v)


def shipped_offsets(refs, chosen, chunk, groups, columns):
    blocks = chunk // columns
    index = (0, slice(chunk, chunk + blocks * groups), slice(None))
    packed = choose(refs, index, chosen)
    return jnp.concatenate([packed[b * groups : (b + 1) * groups] for b in range(blocks)], axis=1)


def their_attend_body(chosen_ref, *refs, count, spread, chunk, groups):
    ships = refs[:count]
    k_ref, v_ref, o_ref, sel_ref, off_ref, flag_ref = refs[count:]
    heads, _, hd = k_ref.shape
    columns = heads * hd
    chosen = chosen_ref[0]
    offs = shipped_offsets(ships, chosen, chunk, groups, columns)
    off_ref[...] = offs
    on = jnp.max(offs[:1, :128].astype(F)) >= 0
    flag_ref[0] = on.astype(jnp.int32)

    @pl.when(on)
    def _():
        q = choose(ships, (0, slice(0, chunk), slice(None)), chosen)
        outs, sums = attend(q, offs, k_ref, v_ref, sel_ref, heads, hd, spread)
        for h in range(heads):
            o_ref[:chunk, h * hd : (h + 1) * hd] = outs[h]
        o_ref[chunk:, :] = pack_rows(
            jnp.concatenate(sums, axis=0), columns, o_ref.shape[0] - chunk
        )

    @pl.when(jnp.logical_not(on))
    def _():
        o_ref[:chunk, :] = jnp.zeros((chunk, columns), B)
        o_ref[chunk:, :] = pack_rows(
            jnp.full((heads, chunk), negative_big, F), columns, o_ref.shape[0] - chunk
        )


def padded_rows(n):
    return -(-n // 16) * 16


def their_attend(c, chosen, ships, k, v, spread, groups):
    heads, rows, hd = k.shape
    columns = heads * hd
    chunk = ships[0].shape[1] * columns // (columns + groups)
    extra = padded_rows(3 * heads * chunk // columns)
    return call(
        functools.partial(
            their_attend_body, count=len(ships), spread=spread, chunk=chunk, groups=groups
        ),
        [
            shape((chunk + extra, columns), B),
            shape((heads, groups, chunk), F),
            shape((groups, chunk), B),
            shape((1,), jnp.int32),
        ],
        "their_attend",
        8 * chunk * columns * rows,
        grid=(1,),
        in_specs=[scalars()]
        + [pl.BlockSpec((1,) + s.shape[1:], lambda i: (c, 0, 0)) for s in ships]
        + [resident(k.shape), resident(v.shape)],
        out_specs=[
            resident((chunk + extra, columns)),
            resident((heads, groups, chunk)),
            resident((groups, chunk)),
            scalars(),
        ],
    )(chosen, *ships, k, v)


def score_gradients(g, offs, log_total, delta, sel_ref, v_ref, heads, hd, spread):
    picked = picked_scores(v_ref, g, offs, heads, hd, spread, GROUP_BLOCK)
    return [
        (jnp.exp(sel_ref[h] - log_total[h : h + 1]) * (picked[h] - delta[h : h + 1])).astype(B)
        for h in range(heads)
    ]


def own_backward_body(
    flag_ref, ship_ref, st_ref, sel_ref, off_ref, k_ref, v_ref, local_ref, dq_ref, *, spread
):
    heads, _, hd = k_ref.shape

    @pl.when(flag_ref[0] > 0)
    def _():
        offs = off_ref[0]
        stats = st_ref[0]
        ds = score_gradients(
            ship_ref[...], offs, stats[:heads], stats[heads:], sel_ref.at[0], v_ref, heads, hd,
            spread
        )
        for h in range(heads):
            c = slice(h * hd, (h + 1) * hd)
            out = spread_dot(k_ref, h, ds[h], offs, spread, GROUP_BLOCK)
            dq_ref[0, :, c] = local_ref[0, :, c] + (out * hd**-0.5).T

    @pl.when(flag_ref[0] <= 0)
    def _():
        dq_ref[...] = local_ref[...]


def own_backward(flag, ship, stats, sel, off, k, v, local, spread):
    heads, rows, hd = k.shape
    chunk = off.shape[2]
    groups = off.shape[1]
    columns = heads * hd
    by_chunk = lambda c: (c, 0, 0)
    return call(
        functools.partial(own_backward_body, spread=spread),
        shape((2, chunk, columns), F),
        "own_backward",
        16 * chunk * columns * rows,
        grid=(2,),
        in_specs=[
            scalars(),
            pl.BlockSpec((chunk, columns), lambda c: (c, 0)),
            pl.BlockSpec((1, 2 * heads, chunk), by_chunk),
            pl.BlockSpec((1, heads, groups, chunk), lambda c: (c, 0, 0, 0)),
            pl.BlockSpec((1, groups, chunk), by_chunk),
            resident(k.shape),
            resident(v.shape),
            pl.BlockSpec((1, chunk, columns), by_chunk),
        ],
        out_specs=pl.BlockSpec((1, chunk, columns), by_chunk),
    )(flag, ship, stats, sel, off, k, v, local)


def their_backward_body(chosen_ref, flag_ref, *refs, count, spread, chunk):
    ships = refs[:count]
    sel0, sel1, off0, off1, k_ref, v_ref, dq_ref = refs[count:]
    heads, _, hd = k_ref.shape
    columns = heads * hd
    blocks = chunk // columns
    extra = padded_rows(6 * heads * blocks)
    chosen = chosen_ref[0]
    on = flag_ref[0] > 0

    @pl.when(on)
    def _():
        for c, (sel_ref, off_ref) in enumerate(((sel0, off0), (sel1, off1))):
            offs = off_ref[...]
            g = choose(ships, (slice(c * chunk, (c + 1) * chunk), slice(None)), chosen)
            row = 2 * chunk + c * extra
            stats = unpack_rows(
                choose(ships, (slice(row, row + extra), slice(None)), chosen), 2 * heads, blocks
            )
            ds = score_gradients(
                g, offs, stats[:heads], stats[heads:], sel_ref, v_ref, heads, hd, spread
            )
            for h in range(heads):
                out = spread_dot(k_ref, h, ds[h], offs, spread, GROUP_BLOCK)
                dq_ref[c * chunk : (c + 1) * chunk, h * hd : (h + 1) * hd] = (
                    (out * hd**-0.5).T.astype(B)
                )

    @pl.when(jnp.logical_not(on))
    def _():
        dq_ref[...] = jnp.zeros_like(dq_ref)


def their_backward(chosen, flag, ships, sels, offs, k, v, spread):
    heads, rows, hd = k.shape
    columns = heads * hd
    chunk = offs[0].shape[1]
    return call(
        functools.partial(their_backward_body, count=len(ships), spread=spread, chunk=chunk),
        shape((2 * chunk, columns), B),
        "their_backward",
        16 * chunk * columns * rows,
        in_specs=[scalars(), scalars()] + [whole()] * (len(ships) + 6),
    )(chosen, flag, *ships, *sels, *offs, k, v)


def causal_scores(k, q, w, scale):
    s = dot(k, q, 1, 1) * scale
    n = k.shape[0]
    key = lax.broadcasted_iota(jnp.int32, (w, w), 0)
    query = lax.broadcasted_iota(jnp.int32, (w, w), 1)
    diagonal = jnp.where(key <= query, s[n - w :], negative_big)
    return diagonal if n == w else jnp.concatenate([s[: n - w], diagonal], axis=0)


def local_forward_body(q_ref, k_ref, v_ref, o_ref, lse_ref, *, heads, parts):
    length, columns = q_ref.shape
    hd = columns // heads
    w = length // parts
    piece = w // 2
    for h in range(heads):
        c = slice(h * hd, (h + 1) * hd)
        for i in range(parts):
            n = (i + 1) * w
            s = causal_scores(k_ref[:n, c], q_ref[i * w : n, c], w, hd**-0.5)
            peak = jnp.max(s, axis=0, keepdims=True)
            p = jnp.exp(s - peak)
            total = jnp.sum(p, axis=0, keepdims=True)
            lse = peak + jnp.log(total)
            out = (dot(v_ref[:n, c], p.astype(B), 0, 0) / total).T.astype(B)
            t = slice(i * piece, (i + 1) * piece)
            for a in range(2):
                o_ref[a, t, c] = out[a * piece : (a + 1) * piece]
                lse_ref[a, h : h + 1, t] = lse[:, a * piece : (a + 1) * piece]


def local_forward(q, k, v, heads, parts):
    length, columns = q.shape
    return call(
        functools.partial(local_forward_body, heads=heads, parts=parts),
        [shape((2, length // 2, columns), B), shape((2, heads, length // 2), F)],
        "local_forward",
        4 * length * length * columns,
        in_specs=[whole()] * 3,
    )(q, k, v)


def local_backward_body(
    q_ref, k_ref, v_ref, ship_ref, st_ref, table_ref, dq_ref, dkv_ref, dk_ref, dv_ref,
    *, heads, parts
):
    length, columns = q_ref.shape
    hd = columns // heads
    w = length // parts
    piece = w // 2
    chunk = length // 2
    scale = hd**-0.5
    for h in range(heads):
        c = slice(h * hd, (h + 1) * hd)
        for i in reversed(range(parts)):
            n = (i + 1) * w
            r = slice(i * w, n)
            t = slice(i * piece, (i + 1) * piece)
            g = jnp.concatenate(
                [ship_ref[a * chunk + i * piece : a * chunk + (i + 1) * piece, c] for a in range(2)],
                axis=0,
            )
            stats = jnp.concatenate([st_ref[a, :, t] for a in range(2)], axis=1)
            s = causal_scores(k_ref[:n, c], q_ref[r, c], w, scale)
            p = jnp.exp(s - stats[h : h + 1])
            dp = dot(v_ref[:n, c], g, 1, 1)
            ds = (p * (dp - stats[heads + h : heads + h + 1])).astype(B)
            dq = (dot(k_ref[:n, c], ds, 0, 0) * scale).T
            for a in range(2):
                dq_ref[a, t, c] = dq[a * piece : (a + 1) * piece]
            dk = dot(ds, q_ref[r, c], 1, 0) * scale
            dv = dot(p.astype(B), g, 1, 0)
            if i == parts - 1:
                dk_ref[:n, :] = dk
                dv_ref[:n, :] = dv
            else:
                dk_ref[:n, :] += dk
                dv_ref[:n, :] += dv
        dk = rope(dk_ref[...], table_ref[...], -1.0).astype(B)
        dv = dv_ref[...].astype(B)
        for i in range(parts):
            t = slice(i * piece, (i + 1) * piece)
            for a in range(2):
                r = slice(i * w + a * piece, i * w + (a + 1) * piece)
                dkv_ref[a, t, c] = dk[r]
                dkv_ref[a, t, columns + h * hd : columns + (h + 1) * hd] = dv[r]


def local_backward(q, k, v, ship, stats, table, heads, parts):
    length, columns = q.shape
    hd = columns // heads
    return call(
        functools.partial(local_backward_body, heads=heads, parts=parts),
        [shape((2, length // 2, columns), F), shape((2, length // 2, 2 * columns), B)],
        "local_backward",
        10 * length * length * columns,
        in_specs=[whole()] * 6,
        scratch_shapes=[pltpu.VMEM((length, hd), F)] * 2,
    )(q, k, v, ship, stats, table)


def merge_body(
    chosen_ref, lo_ref, ll_ref, oo_ref, ol_ref, *refs, count, heads
):
    ships = refs[:count]
    att_ref, total_ref = refs[count:]
    chunk, columns = att_ref.shape
    hd = columns // heads
    chosen = chosen_ref[0]
    far = choose(ships, (slice(0, chunk), slice(None)), chosen).astype(F)
    packed = choose(ships, (slice(chunk, ships[0].shape[0]), slice(None)), chosen)
    far_lse = unpack_rows(packed, heads, chunk // columns)
    local_lse = ll_ref[0]
    own_lse = ol_ref[0]
    peak = jnp.maximum(jnp.maximum(local_lse, own_lse), far_lse)
    weights = [jnp.exp(l - peak) for l in (local_lse, own_lse, far_lse)]
    total = weights[0] + weights[1] + weights[2]
    total_ref[...] = peak + jnp.log(total)
    weights = [x / total for x in weights]
    stacked = jnp.concatenate(weights + [jnp.zeros((8 - 3 * heads % 8, chunk), F)], axis=0).T
    for h in range(heads):
        c = slice(h * hd, (h + 1) * hd)
        att_ref[:, c] = (
            lo_ref[0, :, c].astype(F) * stacked[:, h : h + 1]
            + oo_ref[0, :, c].astype(F) * stacked[:, heads + h : heads + h + 1]
            + far[:, c] * stacked[:, 2 * heads + h : 2 * heads + h + 1]
        ).astype(B)


def merge(c, chosen, local, own, ships, heads):
    _, chunk, columns = local[0].shape
    part = pl.BlockSpec((1, chunk, columns), lambda i: (c, 0, 0))
    row = pl.BlockSpec((1, heads, chunk), lambda i: (c, 0, 0))
    return call(
        functools.partial(merge_body, count=len(ships), heads=heads),
        [shape((chunk, columns), B), shape((heads, chunk), F)],
        "merge",
        grid=(1,),
        in_specs=[scalars(), part, row, part, row] + [resident(s.shape) for s in ships],
        out_specs=[resident((chunk, columns)), resident((heads, chunk))],
    )(chosen, *local, *own, *ships)


def feed_body(me_ref, *refs, parts):
    pieces = refs[:parts]
    outs = refs[parts : 2 * parts]
    (x_ref, g_ref, gain_ref, wg_ref, wu_ref, wd_ref) = refs[2 * parts : 2 * parts + 6]
    normed_ref, gu_ref, hidden_ref = refs[2 * parts + 6 : 2 * parts + 9]
    gn_refs = refs[2 * parts + 9 : 2 * parts + 11]
    down_refs = refs[2 * parts + 11 : 2 * parts + 13]
    own_ref = refs[2 * parts + 13]
    me = me_ref[0]
    piece = x_ref.shape[2]
    width = x_ref.shape[3]
    ff = wg_ref.shape[0]
    order = list(range(parts.bit_length() - 1))
    for half in range(2):
        js = range(half * parts // 2, (half + 1) * parts // 2)
        r = slice(half * parts // 2 * piece, (half + 1) * parts // 2 * piece)
        middle = x_ref[js[0] : js[-1] + 1, 0].reshape(-1, width).astype(F)
        for p, w in zip(pieces, outs):
            middle = middle + dot(p[r, :], w[...], 1, 0)
        for a, j in enumerate(js):
            @pl.when(me == j)
            def _(a=a):
                own_ref[...] = middle[a * piece : (a + 1) * piece]
        factor = lax.rsqrt(jnp.mean(middle * middle, axis=1, keepdims=True) + epsilon)
        normed = (middle * factor * gain_ref[...]).astype(B)
        normed_ref[r, :] = normed
        gate = dot(normed, wg_ref[...], 1, 1)
        upper = dot(normed, wu_ref[...], 1, 1)
        s = jax.nn.sigmoid(gate)
        silu = gate * s
        hidden = (silu * upper).astype(B)
        hidden_ref[r, :] = hidden
        grad_hidden = dot(g_ref[js[0] : js[-1] + 1, 0].reshape(-1, width), wd_ref[...], 1, 1)
        grad_gate = (grad_hidden * upper * s * (1.0 + gate * (1.0 - s))).astype(B)
        grad_upper = (grad_hidden * silu).astype(B)
        gu_ref[r, :ff] = grad_gate
        gu_ref[r, ff:] = grad_upper
        grad_normed = dot(grad_gate, wg_ref[...], 1, 0) + dot(grad_upper, wu_ref[...], 1, 0)
        down = dot(hidden, wd_ref[...], 1, 0)
        for a, j in enumerate(js):
            place = slot_place(jnp.bitwise_xor(me, j), order)
            store_half(gn_refs, place, slice(None), grad_normed[a * piece : (a + 1) * piece])
            store_half(down_refs, place, slice(None), down[a * piece : (a + 1) * piece])


def feed(c, me, pieces, outs, tokens, cotangent, gain, wg, wu, wd):
    parts, _, piece, width = tokens.shape
    chunk = parts * piece
    ff = wg.shape[0]
    part = pl.BlockSpec((parts, 1, piece, width), lambda i: (0, c, 0, 0))
    results = [
        shape((chunk, width), B),
        shape((chunk, 2 * ff), B),
        shape((chunk, ff), B),
        shape((parts // 2, piece, width), B),
        shape((parts // 2, piece, width), B),
        shape((parts // 2, piece, width), B),
        shape((parts // 2, piece, width), B),
        shape((piece, width), F),
    ]
    return call(
        functools.partial(feed_body, parts=parts),
        results,
        "feed",
        2 * chunk * width * (width + 6 * ff),
        grid=(1,),
        in_specs=[scalars()]
        + [resident(p.shape) for p in pieces]
        + [resident(w.shape) for w in outs]
        + [part, part]
        + [resident(a.shape) for a in (gain, wg, wu, wd)],
        out_specs=[resident(r.shape) for r in results],
    )(me, *pieces, *outs, tokens, cotangent, gain, wg, wu, wd)


def middle_back_body(me_ref, gn_ref, r1_ref, r2_ref, m_ref, g_ref, gain_ref, gm_ref, gb_ref, ga_ref):
    total = gn_ref[0].astype(F) + r1_ref[0].astype(F) + r2_ref[...].astype(F)
    middle = m_ref[...]
    factor = lax.rsqrt(jnp.mean(middle * middle, axis=1, keepdims=True) + epsilon)
    scaled = total * gain_ref[...]
    grad = (
        g_ref[0, 0].astype(F)
        + factor * scaled
        - middle * (factor * factor * factor) * jnp.mean(middle * scaled, axis=1, keepdims=True)
    )
    gm_ref[...] = grad
    gb_ref[...] = grad.astype(B)
    ga_ref[...] = jnp.sum(total * middle * factor, axis=0, keepdims=True)


def middle_back(c, me, gn, r1, r2, middle, cotangent, gain):
    piece, width = middle.shape
    fixed = lambda dims: pl.BlockSpec(dims, lambda i, m: (0,) * len(dims))
    results = [shape((piece, width), F), shape((piece, width), B), shape((1, width), F)]
    return call(
        middle_back_body,
        results,
        "middle_back",
        grid_spec=pltpu.PrefetchScalarGridSpec(
            num_scalar_prefetch=1,
            grid=(1,),
            in_specs=[
                fixed((1, piece, width)),
                fixed((1, piece, width)),
                fixed((piece, width)),
                fixed((piece, width)),
                pl.BlockSpec((1, 1, piece, width), lambda i, m: (m[0], c, 0, 0)),
                fixed((1, width)),
            ],
            out_specs=[fixed(r.shape) for r in results],
        ),
    )(me, gn, r1, r2, middle, cotangent, gain)


def branch_body(me_ref, *refs, parts, heads, distances):
    pieces = refs[: 2 * parts]
    w_ref, att0, att1, lse0, lse1, gb_ref, ship_ref, st_ref = refs[2 * parts :]
    me = me_ref[0]
    piece = pieces[0].shape[0]
    chunk = parts * piece
    columns = w_ref.shape[0]
    hd = columns // heads
    extra = padded_rows(6 * heads * (chunk // columns))
    for c, (att, lse) in enumerate(((att0, lse0), (att1, lse1))):
        for a, k in enumerate(distances):
            start = pl.multiple_of(jnp.bitwise_xor(me, k) * piece, piece)
            gb_ref[c, pl.ds(start, piece), :] = pieces[c * parts + a][...]
        grad = dot(gb_ref[c], w_ref[...], 1, 1).astype(B)
        ship_ref[c * chunk : (c + 1) * chunk, :] = grad
        product = grad.astype(F) * att[...].astype(F)
        rows = [lse[...]]
        for h in range(heads):
            rows.append(
                jnp.sum(product[:, h * hd : (h + 1) * hd].T, axis=0, keepdims=True)
            )
        stats = jnp.concatenate(rows, axis=0)
        st_ref[c] = stats
        row = 2 * chunk + c * extra
        ship_ref[row : row + extra, :] = pack_rows(stats, columns, extra)


def branch(me, pieces, distances, w_output, att, lse, heads):
    parts = len(distances)
    piece, width = pieces[0].shape
    chunk = parts * piece
    columns = w_output.shape[0]
    extra = padded_rows(6 * heads * (chunk // columns))
    return call(
        functools.partial(branch_body, parts=parts, heads=heads, distances=tuple(distances)),
        [
            shape((2, chunk, width), B),
            shape((2 * (chunk + extra), columns), B),
            shape((2, 2 * heads, chunk), F),
        ],
        "branch",
        4 * chunk * width * columns,
        in_specs=[scalars()] + [whole()] * (2 * parts + 5),
    )(me, *pieces, w_output, *att, *lse)


def store_slots(place_ref, outs, first, value, c):
    rows = outs[0].shape[1]
    for a in range(value.shape[0] // rows):
        store_half(outs, place_ref[first + a], c, value[a * rows : (a + 1) * rows])


def columns_body(place_ref, a0, a1, r_ref, keep_ref, send_ref, *, view):
    if view:
        r0 = r_ref[:, 0].reshape(a0.shape[0], -1)
        r1 = r_ref[:, 1].reshape(a0.shape[0], -1)
    else:
        r0 = r_ref[0]
        r1 = r_ref[1]
    value = dot(a0[...], r0, 0, 0) + dot(a1[...], r1, 0, 0)
    lanes = keep_ref.shape[2]
    per = value.shape[1] // lanes
    first = pl.program_id(0) * per
    for a in range(per):
        store_half(
            (keep_ref, send_ref), place_ref[first + a], slice(None),
            value[:, a * lanes : (a + 1) * lanes],
        )


def column_grads(place, left, right, docs, name):
    chunk, features = left[0].shape
    width = right.shape[-1]
    block = max(width // docs, 256)
    view = right.ndim == 4
    rows = right.shape[:-1]
    out = shape((docs // 2, features, width // docs), B)
    return call(
        functools.partial(columns_body, view=view),
        [out, out],
        name,
        grid=(width // block,),
        in_specs=[scalars()]
        + [resident(a.shape) for a in left]
        + [pl.BlockSpec(rows + (block,), lambda i: (0,) * len(rows) + (i,))],
        out_specs=[resident(out.shape)] * 2,
    )(place, *left, right)


def two_columns_body(place_ref, a0, a1, r0, r1, keep_ref, send_ref):
    value = dot(a0[...], r0[...], 0, 0) + dot(a1[...], r1[...], 0, 0)
    lanes = keep_ref.shape[2]
    per = value.shape[1] // lanes
    first = pl.program_id(0) * per
    for a in range(per):
        store_half(
            (keep_ref, send_ref), place_ref[first + a], slice(None),
            value[:, a * lanes : (a + 1) * lanes],
        )


def two_column_grads(place, left, right, docs, name):
    chunk, features = left[0].shape
    width = right[0].shape[1]
    block = max(width // docs, 256)
    out = shape((docs // 2, features, width // docs), B)
    column = pl.BlockSpec((chunk, block), lambda i: (0, i))
    return call(
        two_columns_body,
        [out, out],
        name,
        grid=(width // block,),
        in_specs=[scalars()] + [resident(a.shape) for a in left] + [column, column],
        out_specs=[resident(out.shape)] * 2,
    )(place, *left, *right)


def key_grads_body(
    place_ref, n_ref, dkv_ref, gb_ref, att0, att1, wk_ref, wv_ref, keep_ref, send_ref, gn_ref
):
    out_ref = (keep_ref, send_ref)
    columns = wk_ref.shape[1]
    for c in range(2):
        gn_ref[c] = (
            dot(dkv_ref[c, :, :columns], wk_ref[...], 1, 1)
            + dot(dkv_ref[c, :, columns:], wv_ref[...], 1, 1)
        ).astype(B)
    store_slots(
        place_ref, out_ref, 0,
        dot(n_ref[0], dkv_ref[0], 0, 0) + dot(n_ref[1], dkv_ref[1], 0, 0), slice(0, 2 * columns),
    )
    store_slots(
        place_ref, out_ref, 0,
        dot(gb_ref[0], att0[...], 0, 0) + dot(gb_ref[1], att1[...], 0, 0),
        slice(2 * columns, 3 * columns),
    )


def key_grads(place, normed, dkv, gb, att, wk, wv, docs):
    _, chunk, width = normed.shape
    columns = wk.shape[1]
    return call(
        key_grads_body,
        [shape((docs // 2, width // docs, 3 * columns), B)] * 2 + [shape((2, chunk, width), B)],
        "key_grads",
        20 * chunk * width * columns,
        in_specs=[scalars()] + [whole()] * 7,
    )(place, normed, dkv, gb, *att, wk, wv)


def query_grads_body(
    chosen_ref, me_ref, place_ref, dq_ref, *refs, count, parts, heads
):
    ships = refs[:count]
    n_ref, part_ref, wq_ref, table_ref, x_ref = refs[count : count + 5]
    out_ref = refs[count + 5 : count + 7]
    gn_refs = refs[count + 7 : count + 9]
    gain_ref = refs[count + 9]
    chosen = chosen_ref[0]
    me = me_ref[0]
    _, chunk, columns = dq_ref.shape
    piece = chunk // parts
    hd = columns // heads
    width = wq_ref.shape[0]
    order = list(range(parts.bit_length() - 1))
    grads = None
    gain = None
    for c in range(2):
        far = choose(ships, (slice(c * chunk, (c + 1) * chunk), slice(None)), chosen)
        dq = dq_ref[c] + far.astype(F)
        table = table_ref[:, c].reshape(chunk, hd)
        low = jnp.concatenate(
            [rope(dq[:, h * hd : (h + 1) * hd], table, -1.0) for h in range(heads)], axis=1
        ).astype(B)
        gn = dot(low, wq_ref[...], 1, 1) + part_ref[c].astype(F)
        for j in range(parts):
            place = slot_place(jnp.bitwise_xor(me, j), order)
            store_half(
                gn_refs, place, slice(None), gn[j * piece : (j + 1) * piece],
                slice(c * piece, (c + 1) * piece),
            )
        x = x_ref[:, c].reshape(chunk, width).astype(F)
        factor = lax.rsqrt(jnp.mean(x * x, axis=1, keepdims=True) + epsilon)
        part = jnp.sum(gn * x * factor, axis=0, keepdims=True)
        gain = part if gain is None else gain + part
        part = dot(n_ref[c], low, 0, 0)
        grads = part if grads is None else grads + part
    gain_ref[...] = gain
    store_slots(place_ref, out_ref, 0, grads, slice(0, columns))


def query_grads(chosen, me, place, dq, ships, normed, part, wq, table, tokens, docs, heads):
    _, chunk, width = normed.shape
    columns = wq.shape[1]
    parts = tokens.shape[0]
    return call(
        functools.partial(query_grads_body, count=len(ships), parts=parts, heads=heads),
        [shape((docs // 2, width // docs, columns), B)] * 2
        + [shape((parts // 2, 2 * chunk // parts, width), B)] * 2
        + [shape((1, width), F)],
        "query_grads",
        8 * chunk * width * columns,
        in_specs=[scalars()] * 3 + [whole()] * (len(ships) + 6),
    )(chosen, me, place, dq, *ships, normed, part, wq, table, tokens)


def tokens_back_body(me_ref, gn_ref, r1_ref, r2_ref, x_ref, gm0, gm1, gain_ref, out_ref):
    total = gn_ref[0].astype(F) + r1_ref[0].astype(F) + r2_ref[...].astype(F)
    x = x_ref[...].astype(F)
    factor = lax.rsqrt(jnp.mean(x * x, axis=1, keepdims=True) + epsilon)
    scaled = total * gain_ref[...]
    grad = factor * scaled - x * (factor * factor * factor) * jnp.mean(
        x * scaled, axis=1, keepdims=True
    )
    piece = gm0.shape[0]
    out_ref[:piece, :] = (gm0[...] + grad[:piece]).astype(B)
    out_ref[piece:, :] = (gm1[...] + grad[piece:]).astype(B)


def tokens_back(me, gn, r1, r2, tokens, gm, gain):
    _, share, width = gn.shape
    fixed = lambda dims: pl.BlockSpec(dims, lambda i, m: (0,) * len(dims))
    return call(
        tokens_back_body,
        shape((share, width), B),
        "tokens_back",
        grid_spec=pltpu.PrefetchScalarGridSpec(
            num_scalar_prefetch=1,
            grid=(1,),
            in_specs=[
                fixed((1, share, width)),
                fixed((1, share, width)),
                fixed((share, width)),
                pl.BlockSpec((share, width), lambda i, m: (m[0], 0)),
                fixed(gm[0].shape),
                fixed(gm[1].shape),
                fixed((1, width)),
            ],
            out_specs=fixed((share, width)),
        ),
    )(me, gn, r1, r2, tokens, *gm, gain)


def rotate_table(length, hd):
    half = hd // 2
    position = np.arange(length, dtype=np.float32)
    inverse = np.exp(
        -np.log(np.float32(10000.0)) * np.arange(half, dtype=np.float32) * np.float32(2.0) / hd
    ).astype(np.float32)
    angles = position[:, None] * inverse[None, :]
    return jnp.asarray(np.concatenate([np.cos(angles), np.sin(angles)], axis=1).astype(np.float32))


def to_all(array):
    bits = axis_bits("dp")
    got = {b: swap(array, "dp", 1 << b) for b in reversed(range(bits))}
    return [got[b] for b in range(bits)]


def gather_tensor(value):
    pieces, distances = [value], [0]
    for b in reversed(range(axis_bits("tensor"))):
        pieces = pieces + [swap(p, "tensor", 1 << b) for p in pieces]
        distances = distances + [k ^ (1 << b) for k in distances]
    return pieces, distances


def after(value, *others):
    return lax.optimization_barrier((value,) + others)[0]


def add_low(a, b):
    return (a.astype(F) + b.astype(F)).astype(B)


def fold(keep, send, bit, *others):
    got = swap(after(send, *others) if others else send, "dp", 1 << bit)
    half = keep.shape[0] // 2
    if half == 0:
        return keep[0], got[0]
    return add_low(keep[:half], got[:half]), add_low(keep[half:], got[half:])


def total(pair, c=slice(None)):
    return pair[0][:, c].astype(F) + pair[1][:, c].astype(F)


def per_device(
    tokens,
    w_query,
    w_key,
    w_value,
    w_output,
    w_gate,
    w_up,
    w_down,
    gain_attn,
    gain_mlp,
    cache_keys,
    cache_values,
    knn_index,
    memory_flag,
    pairing,
    cotangent,
):
    length, width = tokens.shape
    parts = lax.axis_size("tensor")
    docs = lax.axis_size("dp")
    piece = length // parts // 2
    me = lax.axis_index("tensor").astype(jnp.int32).reshape(1)
    heads = cache_keys.shape[1]
    rows = cache_keys.shape[2]
    hd = cache_keys.shape[3]
    columns = heads * hd
    groups = knn_index.shape[1] // 2
    spread = rows // groups
    ff = w_gate.shape[1]
    flag = memory_flag[:1].astype(jnp.int32)
    my_doc = lax.axis_index("dp").astype(jnp.int32)
    difference = jnp.bitwise_xor(pairing[0].astype(jnp.int32), my_doc)
    chosen = jnp.zeros((), jnp.int32)
    for b in range(1, axis_bits("dp")):
        chosen = jnp.where(difference == (1 << b), b, chosen)
    chosen = chosen.reshape(1)
    dp_order = list(range(axis_bits("dp")))
    place = slot_place(jnp.bitwise_xor(jnp.arange(docs, dtype=jnp.int32), my_doc), dp_order)
    place = place.astype(jnp.int32)
    table = rotate_table(length, hd)
    gain_a = gain_attn.reshape(1, width)
    gain_m = gain_mlp.reshape(1, width)
    tokens_view = tokens.reshape(parts, 2, piece, width)
    cotangent_view = cotangent.reshape(parts, 2, piece, width)
    table_view = table.reshape(parts, 2, piece, hd)

    def ordered_rows(cache):
        return (
            cache.reshape(heads, groups // GROUP_BLOCK, GROUP_BLOCK, spread, hd)
            .transpose(0, 1, 3, 2, 4)
            .reshape(heads, rows, hd)
        )

    ship, q, k, v, normed_low, own_off = project(
        flag, tokens, knn_index, gain_a, w_query, w_key, w_value, table, parts, heads, spread
    )
    ships = to_all(ship)
    out_weights, distances = gather_tensor(w_output)
    stored_keys = ordered_rows(cache_keys[0])
    stored_values = ordered_rows(cache_values[0])
    local = local_forward(q, k, v, heads, parts)
    own_out, own_lse, own_sel = own_attend(
        flag, ship, own_off, stored_keys, stored_values, spread
    )
    ships = list(after(tuple(ships), own_out, local[0]))
    att, lse, their_sel, their_off, returned, pieces = [], [], [], [], [], []
    for c in range(2):
        packed, sel, off, their_flag = their_attend(
            c, chosen, ships, stored_keys, stored_values, spread, groups
        )
        their_sel.append(sel)
        their_off.append(off)
        returned.append(to_all(packed))
    for c in range(2):
        a, log_total = merge(c, chosen, local, (own_out, own_lse), returned[c], heads)
        att.append(a)
        lse.append(log_total)
        pieces.append(gather_tensor(a)[0])

    feeds, back = [], []
    for c in range(2):
        if c:
            pieces[c] = list(after(tuple(pieces[c]), back[0][1]))
        feeds.append(
            feed(
                c, me, pieces[c], out_weights, tokens_view, cotangent_view, gain_m, w_gate.T,
                w_up.T, w_down,
            )
        )
        keep, send = feeds[c][3], feeds[c][4]
        first = swap(send, "tensor", 1)
        back.append((first, add_low(keep[1], first[1])))
    gm, gb_pieces, gain_parts = [], [], []
    for c in range(2):
        first, second = back[c]
        grad_middle, low, gain_part = middle_back(
            c, me, feeds[c][3], first, swap(second, "tensor", 2), feeds[c][7], cotangent_view,
            gain_m
        )
        gm.append(grad_middle)
        gain_parts.append(gain_part)
        gb_pieces += gather_tensor(low)[0]
    down_slots = column_grads(
        place, after((feeds[0][2], feeds[1][2]), back[1][1]), cotangent_view, docs, "down_grads"
    )
    down_half = fold(*down_slots, dp_order[0])
    gate_slots = two_column_grads(
        place,
        after((feeds[0][1], feeds[1][1]), gm[1], down_slots[1]),
        (feeds[0][0], feeds[1][0]),
        docs,
        "gate_grads",
    )

    grad_branch, back_ship, stats = branch(
        me, after(tuple(gb_pieces), gate_slots[0]), distances, w_output, att, lse, heads
    )
    back_ships = to_all(back_ship)
    local_dq, dkv = local_backward(q, k, v, back_ship, stats, table, heads, parts)
    gate_half = fold(*gate_slots, dp_order[0], local_dq)
    dq = own_backward(
        flag, back_ship, stats, own_sel, own_off, stored_keys, stored_values, local_dq, spread
    )
    down_half = fold(*down_half, dp_order[1], dq)
    their_dq = their_backward(
        chosen, their_flag, list(after(tuple(back_ships), dq)), their_sel, their_off, stored_keys,
        stored_values, spread
    )
    dq_ships = to_all(their_dq)

    keep, send, gn_part = key_grads(
        place, normed_low, after(dkv, their_dq), grad_branch, att, w_key, w_value, docs
    )
    down_half = fold(*down_half, dp_order[2], their_dq) if len(dp_order) > 2 else down_half
    key_half = fold(keep, send, dp_order[0])
    gate_half = fold(*gate_half, dp_order[1], their_dq)
    output = []
    for c in range(2):
        keep, send = feeds[c][5], after(feeds[c][6], their_dq)
        first = swap(send, "tensor", 1)
        second = swap(add_low(keep[1], first[1]), "tensor", 2)
        output.append(
            feeds[c][7] + keep[0].astype(F) + first[0].astype(F) + second.astype(F)
        )
    keep, send, gn_keep, gn_send, gain_part = query_grads(
        chosen, me, place, dq, dq_ships, normed_low, gn_part, w_query, table_view, tokens_view,
        docs, heads
    )
    query_half = fold(keep, send, dp_order[0])
    first = swap(gn_send, "tensor", 1)
    second = swap(add_low(gn_keep[1], first[1]), "tensor", 2)
    grad_tokens = tokens_back(me, gn_keep, first, second, tokens, gm, gain_a)
    for b in dp_order[1:]:
        query_half = fold(*query_half, b)
        key_half = fold(*key_half, b)
    for b in dp_order[2:]:
        gate_half = fold(*gate_half, b)
    for b in dp_order[3:]:
        down_half = fold(*down_half, b)
    gains = jnp.concatenate([gain_part, gain_parts[0] + gain_parts[1]], axis=0)
    gains = gains + sum(swap(gains, "tensor", t) for t in range(1, parts))
    for b in dp_order:
        gains = gains + swap(gains, "dp", 1 << b)
    gains = lax.dynamic_slice_in_dim(gains, my_doc * (width // docs), width // docs, 1)
    gate_pair = gate_half
    return (
        jnp.concatenate(output, axis=0).astype(B),
        grad_tokens,
        total(query_half),
        total(key_half, slice(0, columns)),
        total(key_half, slice(columns, 2 * columns)),
        total(key_half, slice(2 * columns, None)).T,
        (gate_pair[0][:ff].astype(F) + gate_pair[1][:ff].astype(F)).T,
        (gate_pair[0][ff:].astype(F) + gate_pair[1][ff:].astype(F)).T,
        total(down_half),
        gains[0],
        gains[1],
    )


def solution(mesh):
    placed = (
        P("dp", None),
        P(None, "tensor"),
        P(None, "tensor"),
        P(None, "tensor"),
        P("tensor", None),
        P(None, "tensor"),
        P(None, "tensor"),
        P("tensor", None),
        P(),
        P(),
        P("dp", "tensor", None, None),
        P("dp", "tensor", None, None),
        P("dp", None),
        P("dp"),
        P("dp"),
        P("dp", None),
    )
    return jax.shard_map(
        per_device,
        mesh=mesh,
        in_specs=placed,
        out_specs=(
            P(("dp", "tensor"), None),
            P(("dp", "tensor"), None),
            P("dp", "tensor"),
            P("dp", "tensor"),
            P("dp", "tensor"),
            P("tensor", "dp"),
            P("dp", "tensor"),
            P("dp", "tensor"),
            P("tensor", "dp"),
            P("dp"),
            P("dp"),
        ),
        check_vma=False,
    )
```

```python
import functools

import jax
import jax.numpy as jnp
import numpy as np
from jax import lax
from jax.experimental import pallas as pl
from jax.experimental.pallas import tpu as pltpu
from jax.sharding import PartitionSpec as P

epsilon = 1e-05
negative_big = -1e30
F = jnp.float32
B = jnp.bfloat16
GROUP_BLOCK = 16
extra_rows = 16
kernel_us = dict(
    project=3.4, own_attend=9.0, their_attend=5.3, own_backward=7.2, their_backward=8.5,
    local_forward=3.4, local_backward=4.2, merge=1.9, feed=9.8, middle_back=0.4, branch=2.3,
    down_grads=4.0, gate_grads=6.2, key_grads=5.6, query_grads=4.3, tokens_back=2.4,
)


def dot(a, b, da, db):
    return lax.dot_general(a, b, (((da,), (db,)), ((), ())), preferred_element_type=F)


def swap(array, axis, bit):
    return lax.ppermute(array, axis, [(i, i ^ bit) for i in range(lax.axis_size(axis))])


def axis_bits(axis):
    return lax.axis_size(axis).bit_length() - 1


def call(body, out_shape, name, flops=0, limit=28, **options):
    kernel = pl.pallas_call(
        body,
        out_shape=out_shape,
        name=name,
        cost_estimate=pl.CostEstimate(
            flops=int(kernel_us[name] * 1e9 * 1.15), transcendentals=0, bytes_accessed=0
        ),
        compiler_params=pltpu.CompilerParams(vmem_limit_bytes=limit << 20),
        **options,
    )
    specs = options.get("in_specs")

    def run(*args):
        if specs is not None:
            args = [
                pltpu.with_memory_space_constraint(a, pltpu.VMEM)
                if s.block_shape is None and s.memory_space is pltpu.VMEM
                else a
                for a, s in zip(args, specs)
            ]
        return kernel(*args)

    return run


def shape(dims, dtype):
    return jax.ShapeDtypeStruct(dims, dtype)


def whole():
    return pl.BlockSpec(memory_space=pltpu.VMEM)


def scalars():
    return pl.BlockSpec(memory_space=pltpu.SMEM)


def slot_place(difference, order):
    place = 0
    for b in order:
        place = place * 2 + ((difference >> b) & 1)
    return place


def store_half(refs, place, c, value, rows=slice(None)):
    half = refs[0].shape[0]
    value = value.astype(B)

    @pl.when(place < half)
    def _():
        refs[0][place, rows, c] = value

    @pl.when(place >= half)
    def _():
        refs[1][place - half, rows, c] = value


def choose(refs, index, chosen):
    value = refs[0][index]
    for b in range(1, len(refs)):
        value = jnp.where(chosen == b, refs[b][index], value)
    return value


def split_terms(x):
    first = x.astype(B).astype(F)
    second = (x - first).astype(B).astype(F)
    third = (x - first - second).astype(B).astype(F)
    return [first, second, third]


def pack_rows(x, lanes, total):
    rows = []
    terms = split_terms(x)
    for b in range(x.shape[1] // lanes):
        rows += [t[:, b * lanes : (b + 1) * lanes] for t in terms]
    used = sum(r.shape[0] for r in rows)
    if total > used:
        rows.append(jnp.zeros((total - used, lanes), F))
    return jnp.concatenate(rows, axis=0).astype(B)


def unpack_rows(packed, n, blocks):
    packed = packed.astype(F)
    out = []
    for b in range(blocks):
        base = b * 3 * n
        out.append(
            packed[base : base + n]
            + packed[base + n : base + 2 * n]
            + packed[base + 2 * n : base + 3 * n]
        )
    return jnp.concatenate(out, axis=1)


def rope(x, table, direction):
    half = x.shape[1] // 2
    other = pltpu.roll(table, half, 1)
    front = lax.broadcasted_iota(jnp.int32, x.shape, 1) < half
    cos = jnp.where(front, table, other)
    sin = jnp.where(front, -other, table) * direction
    return x * cos + pltpu.roll(x, half, 1) * sin


def project_body(
    flag_ref, x_ref, knn_ref, gain_ref, wq_ref, wk_ref, wv_ref, table_ref,
    ship_ref, q_ref, k_ref, v_ref, normed_ref, off_ref, *, parts, heads, hd, spread,
):
    length = x_ref.shape[0]
    share = length // parts
    piece = share // 2
    chunk = length // 2
    columns = heads * hd
    groups = knn_ref.shape[1] // 2
    gain = gain_ref[...]
    for j in range(parts):
        r = slice(j * share, (j + 1) * share)
        x = x_ref[r, :].astype(F)
        factor = lax.rsqrt(jnp.mean(x * x, axis=1, keepdims=True) + epsilon)
        normed = (x * factor * gain).astype(B)
        table = table_ref[r, :]
        q = dot(normed, wq_ref[...], 1, 0)
        k = dot(normed, wk_ref[...], 1, 0)
        v_ref[r, :] = dot(normed, wv_ref[...], 1, 0).astype(B)
        q = jnp.concatenate(
            [rope(q[:, h * hd : (h + 1) * hd], table, 1.0) for h in range(heads)], axis=1
        ).astype(B)
        q_ref[r, :] = q
        k_ref[r, :] = jnp.concatenate(
            [rope(k[:, h * hd : (h + 1) * hd], table, 1.0) for h in range(heads)], axis=1
        ).astype(B)
        knn = knn_ref[r, :]
        start = lax.broadcasted_iota(jnp.int32, knn.shape, 1) * spread
        off = (knn - start).astype(F).T
        far = jnp.where(flag_ref[0] > 0, off[groups:], -1.0).astype(B)
        off = off[:groups].astype(B)
        for c in range(2):
            p = slice(c * piece, (c + 1) * piece)
            t = slice(j * piece, (j + 1) * piece)
            normed_ref[c, t, :] = normed[p]
            ship_ref[c, t, :] = q[p]
            off_ref[c, :, t] = off[:, p]
            lane = j * piece
            row = chunk + lane // columns * groups
            lane = lane % columns
            ship_ref[c, row : row + groups, lane : lane + piece] = far[:, p]


def project(flag, tokens, knn, gain, wq, wk, wv, table, parts, heads, spread):
    length, width = tokens.shape
    columns = wq.shape[1]
    groups = knn.shape[1] // 2
    chunk = length // 2
    body = functools.partial(
        project_body, parts=parts, heads=heads, hd=columns // heads, spread=spread
    )
    arrays = (tokens, knn, gain, wq, wk, wv, table)
    results = [
        shape((2, chunk + chunk // columns * groups, columns), B),
        shape((length, columns), B),
        shape((length, columns), B),
        shape((length, columns), B),
        shape((2, chunk, width), B),
        shape((2, groups, chunk), B),
    ]
    return call(
        body,
        results,
        "project",
        6 * length * width * columns,
        grid=(1,),
        in_specs=[scalars()] + [resident(a.shape) for a in arrays],
        out_specs=[resident(r.shape) for r in results],
    )(flag, *[pltpu.with_memory_space_constraint(a, pltpu.HBM) for a in arrays])


def pick(block_scores, offsets, heads, spread, gb):
    picked = [s[:gb] for s in block_scores]
    for t in range(1, spread):
        here = offsets == float(t)
        for h in range(heads):
            picked[h] = jnp.where(here, block_scores[h][t * gb : (t + 1) * gb], picked[h])
    return picked


def picked_scores(rows_ref, values, offs, heads, hd, spread, gb):
    rows = gb * spread
    wide = offs.astype(F)
    out = [[] for _ in range(heads)]
    for b in range(offs.shape[0] // gb):
        scores = [
            dot(
                rows_ref[h, b * rows : (b + 1) * rows, :], values[:, h * hd : (h + 1) * hd], 1, 1
            )
            for h in range(heads)
        ]
        picked = pick(scores, wide[b * gb : (b + 1) * gb], heads, spread, gb)
        for h in range(heads):
            out[h].append(picked[h])
    return [jnp.concatenate(o, axis=0) for o in out]


def spread_dot(rows_ref, h, picked, offs, spread, gb):
    rows = gb * spread
    total = None
    zero = jnp.zeros((gb, picked.shape[1]), B)
    for b in range(offs.shape[0] // gb):
        p = picked[b * gb : (b + 1) * gb]
        o = offs[b * gb : (b + 1) * gb]
        wide = jnp.concatenate(
            [jnp.where(o == jnp.asarray(t, B), p, zero) for t in range(spread)], axis=0
        )
        part = dot(rows_ref[h, b * rows : (b + 1) * rows, :], wide, 0, 0)
        total = part if total is None else total + part
    return total


def attend(q, offs, k_ref, v_ref, sel_ref, heads, hd, spread):
    outs, sums = [], []
    picked = picked_scores(k_ref, q, offs, heads, hd, spread, GROUP_BLOCK)
    for h in range(heads):
        x = picked[h] * hd**-0.5
        sel_ref[h] = x
        peak = jnp.max(x, axis=0, keepdims=True)
        p = jnp.exp(x - peak)
        total = jnp.sum(p, axis=0, keepdims=True)
        sums.append(peak + jnp.log(total))
        out = spread_dot(v_ref, h, p.astype(B), offs, spread, GROUP_BLOCK)
        outs.append((out / total).T.astype(B))
    return outs, sums


def own_attend_body(flag_ref, ship_ref, off_ref, k_ref, v_ref, o_ref, lse_ref, sel_ref, *, spread):
    heads, _, hd = k_ref.shape
    chunk = o_ref.shape[1]

    @pl.when(flag_ref[0] > 0)
    def _():
        outs, sums = attend(
            ship_ref[0, :chunk, :], off_ref[0], k_ref, v_ref, sel_ref.at[0], heads, hd, spread
        )
        for h in range(heads):
            o_ref[0, :, h * hd : (h + 1) * hd] = outs[h]
            lse_ref[0, h : h + 1, :] = sums[h]

    @pl.when(flag_ref[0] <= 0)
    def _():
        o_ref[...] = jnp.zeros_like(o_ref)
        lse_ref[...] = jnp.full_like(lse_ref, negative_big)


def resident(dims):
    return pl.BlockSpec(dims, lambda *i: (0,) * len(dims))


def own_attend(flag, ship, off, k, v, spread):
    heads, rows, hd = k.shape
    chunk = off.shape[2]
    groups = off.shape[1]
    columns = heads * hd
    by_chunk = lambda c: (c, 0, 0)
    return call(
        functools.partial(own_attend_body, spread=spread),
        [
            shape((2, chunk, columns), B),
            shape((2, heads, chunk), F),
            shape((2, heads, groups, chunk), F),
        ],
        "own_attend",
        16 * chunk * columns * rows,
        grid=(2,),
        in_specs=[
            scalars(),
            pl.BlockSpec((1,) + ship.shape[1:], by_chunk),
            pl.BlockSpec((1, groups, chunk), by_chunk),
            resident(k.shape),
            resident(v.shape),
        ],
        out_specs=[
            pl.BlockSpec((1, chunk, columns), by_chunk),
            pl.BlockSpec((1, heads, chunk), by_chunk),
            pl.BlockSpec((1, heads, groups, chunk), lambda c: (c, 0, 0, 0)),
        ],
    )(flag, ship, off, k, v)


def shipped_offsets(refs, chosen, chunk, groups, columns):
    blocks = chunk // columns
    index = (0, slice(chunk, chunk + blocks * groups), slice(None))
    packed = choose(refs, index, chosen)
    return jnp.concatenate([packed[b * groups : (b + 1) * groups] for b in range(blocks)], axis=1)


def their_attend_body(chosen_ref, *refs, count, spread, chunk, groups):
    ships = refs[:count]
    k_ref, v_ref, o_ref, sel_ref, off_ref, flag_ref = refs[count:]
    heads, _, hd = k_ref.shape
    columns = heads * hd
    chosen = chosen_ref[0]
    offs = shipped_offsets(ships, chosen, chunk, groups, columns)
    off_ref[...] = offs
    on = jnp.max(offs[:1, :128].astype(F)) >= 0
    flag_ref[0] = on.astype(jnp.int32)

    @pl.when(on)
    def _():
        q = choose(ships, (0, slice(0, chunk), slice(None)), chosen)
        outs, sums = attend(q, offs, k_ref, v_ref, sel_ref, heads, hd, spread)
        for h in range(heads):
            o_ref[:chunk, h * hd : (h + 1) * hd] = outs[h]
        o_ref[chunk:, :] = pack_rows(
            jnp.concatenate(sums, axis=0), columns, o_ref.shape[0] - chunk
        )

    @pl.when(jnp.logical_not(on))
    def _():
        o_ref[:chunk, :] = jnp.zeros((chunk, columns), B)
        o_ref[chunk:, :] = pack_rows(
            jnp.full((heads, chunk), negative_big, F), columns, o_ref.shape[0] - chunk
        )


def padded_rows(n):
    return -(-n // 16) * 16


def their_attend(c, chosen, ships, k, v, spread, groups):
    heads, rows, hd = k.shape
    columns = heads * hd
    chunk = ships[0].shape[1] * columns // (columns + groups)
    extra = padded_rows(3 * heads * chunk // columns)
    return call(
        functools.partial(
            their_attend_body, count=len(ships), spread=spread, chunk=chunk, groups=groups
        ),
        [
            shape((chunk + extra, columns), B),
            shape((heads, groups, chunk), F),
            shape((groups, chunk), B),
            shape((1,), jnp.int32),
        ],
        "their_attend",
        8 * chunk * columns * rows,
        grid=(1,),
        in_specs=[scalars()]
        + [pl.BlockSpec((1,) + s.shape[1:], lambda i: (c, 0, 0)) for s in ships]
        + [resident(k.shape), resident(v.shape)],
        out_specs=[
            resident((chunk + extra, columns)),
            resident((heads, groups, chunk)),
            resident((groups, chunk)),
            scalars(),
        ],
    )(chosen, *ships, k, v)


def score_gradients(g, offs, log_total, delta, sel_ref, v_ref, heads, hd, spread):
    picked = picked_scores(v_ref, g, offs, heads, hd, spread, GROUP_BLOCK)
    return [
        (jnp.exp(sel_ref[h] - log_total[h : h + 1]) * (picked[h] - delta[h : h + 1])).astype(B)
        for h in range(heads)
    ]


def own_backward_body(
    flag_ref, ship_ref, st_ref, sel_ref, off_ref, k_ref, v_ref, local_ref, dq_ref, *, spread
):
    heads, _, hd = k_ref.shape

    @pl.when(flag_ref[0] > 0)
    def _():
        offs = off_ref[0]
        stats = st_ref[0]
        ds = score_gradients(
            ship_ref[...], offs, stats[:heads], stats[heads:], sel_ref.at[0], v_ref, heads, hd,
            spread
        )
        for h in range(heads):
            c = slice(h * hd, (h + 1) * hd)
            out = spread_dot(k_ref, h, ds[h], offs, spread, GROUP_BLOCK)
            dq_ref[0, :, c] = local_ref[0, :, c] + (out * hd**-0.5).T

    @pl.when(flag_ref[0] <= 0)
    def _():
        dq_ref[...] = local_ref[...]


def own_backward(flag, ship, stats, sel, off, k, v, local, spread):
    heads, rows, hd = k.shape
    chunk = off.shape[2]
    groups = off.shape[1]
    columns = heads * hd
    by_chunk = lambda c: (c, 0, 0)
    return call(
        functools.partial(own_backward_body, spread=spread),
        shape((2, chunk, columns), F),
        "own_backward",
        16 * chunk * columns * rows,
        grid=(2,),
        in_specs=[
            scalars(),
            pl.BlockSpec((chunk, columns), lambda c: (c, 0)),
            pl.BlockSpec((1, 2 * heads, chunk), by_chunk),
            pl.BlockSpec((1, heads, groups, chunk), lambda c: (c, 0, 0, 0)),
            pl.BlockSpec((1, groups, chunk), by_chunk),
            resident(k.shape),
            resident(v.shape),
            pl.BlockSpec((1, chunk, columns), by_chunk),
        ],
        out_specs=pl.BlockSpec((1, chunk, columns), by_chunk),
    )(flag, ship, stats, sel, off, k, v, local)


def their_backward_body(chosen_ref, flag_ref, *refs, count, spread, chunk):
    ships = refs[:count]
    sel0, sel1, off0, off1, k_ref, v_ref, dq_ref = refs[count:]
    heads, _, hd = k_ref.shape
    columns = heads * hd
    blocks = chunk // columns
    extra = padded_rows(6 * heads * blocks)
    chosen = chosen_ref[0]
    on = flag_ref[0] > 0

    @pl.when(on)
    def _():
        for c, (sel_ref, off_ref) in enumerate(((sel0, off0), (sel1, off1))):
            offs = off_ref[...]
            g = choose(ships, (slice(c * chunk, (c + 1) * chunk), slice(None)), chosen)
            row = 2 * chunk + c * extra
            stats = unpack_rows(
                choose(ships, (slice(row, row + extra), slice(None)), chosen), 2 * heads, blocks
            )
            ds = score_gradients(
                g, offs, stats[:heads], stats[heads:], sel_ref, v_ref, heads, hd, spread
            )
            for h in range(heads):
                out = spread_dot(k_ref, h, ds[h], offs, spread, GROUP_BLOCK)
                dq_ref[c * chunk : (c + 1) * chunk, h * hd : (h + 1) * hd] = (
                    (out * hd**-0.5).T.astype(B)
                )

    @pl.when(jnp.logical_not(on))
    def _():
        dq_ref[...] = jnp.zeros_like(dq_ref)


def their_backward(chosen, flag, ships, sels, offs, k, v, spread):
    heads, rows, hd = k.shape
    columns = heads * hd
    chunk = offs[0].shape[1]
    return call(
        functools.partial(their_backward_body, count=len(ships), spread=spread, chunk=chunk),
        shape((2 * chunk, columns), B),
        "their_backward",
        16 * chunk * columns * rows,
        in_specs=[scalars(), scalars()] + [whole()] * (len(ships) + 6),
    )(chosen, flag, *ships, *sels, *offs, k, v)


def causal_scores(k, q, w, scale):
    s = dot(k, q, 1, 1) * scale
    n = k.shape[0]
    key = lax.broadcasted_iota(jnp.int32, (w, w), 0)
    query = lax.broadcasted_iota(jnp.int32, (w, w), 1)
    diagonal = jnp.where(key <= query, s[n - w :], negative_big)
    return diagonal if n == w else jnp.concatenate([s[: n - w], diagonal], axis=0)


def local_forward_body(q_ref, k_ref, v_ref, o_ref, lse_ref, *, heads, parts):
    length, columns = q_ref.shape
    hd = columns // heads
    w = length // parts
    piece = w // 2
    for h in range(heads):
        c = slice(h * hd, (h + 1) * hd)
        for i in range(parts):
            n = (i + 1) * w
            s = causal_scores(k_ref[:n, c], q_ref[i * w : n, c], w, hd**-0.5)
            peak = jnp.max(s, axis=0, keepdims=True)
            p = jnp.exp(s - peak)
            total = jnp.sum(p, axis=0, keepdims=True)
            lse = peak + jnp.log(total)
            out = (dot(v_ref[:n, c], p.astype(B), 0, 0) / total).T.astype(B)
            t = slice(i * piece, (i + 1) * piece)
            for a in range(2):
                o_ref[a, t, c] = out[a * piece : (a + 1) * piece]
                lse_ref[a, h : h + 1, t] = lse[:, a * piece : (a + 1) * piece]


def local_forward(q, k, v, heads, parts):
    length, columns = q.shape
    return call(
        functools.partial(local_forward_body, heads=heads, parts=parts),
        [shape((2, length // 2, columns), B), shape((2, heads, length // 2), F)],
        "local_forward",
        4 * length * length * columns,
        in_specs=[whole()] * 3,
    )(q, k, v)


def local_backward_body(
    q_ref, k_ref, v_ref, ship_ref, st_ref, table_ref, dq_ref, dkv_ref, dk_ref, dv_ref,
    *, heads, parts
):
    length, columns = q_ref.shape
    hd = columns // heads
    w = length // parts
    piece = w // 2
    chunk = length // 2
    scale = hd**-0.5
    for h in range(heads):
        c = slice(h * hd, (h + 1) * hd)
        for i in reversed(range(parts)):
            n = (i + 1) * w
            r = slice(i * w, n)
            t = slice(i * piece, (i + 1) * piece)
            g = jnp.concatenate(
                [ship_ref[a * chunk + i * piece : a * chunk + (i + 1) * piece, c] for a in range(2)],
                axis=0,
            )
            stats = jnp.concatenate([st_ref[a, :, t] for a in range(2)], axis=1)
            s = causal_scores(k_ref[:n, c], q_ref[r, c], w, scale)
            p = jnp.exp(s - stats[h : h + 1])
            dp = dot(v_ref[:n, c], g, 1, 1)
            ds = (p * (dp - stats[heads + h : heads + h + 1])).astype(B)
            dq = (dot(k_ref[:n, c], ds, 0, 0) * scale).T
            for a in range(2):
                dq_ref[a, t, c] = dq[a * piece : (a + 1) * piece]
            dk = dot(ds, q_ref[r, c], 1, 0) * scale
            dv = dot(p.astype(B), g, 1, 0)
            if i == parts - 1:
                dk_ref[:n, :] = dk
                dv_ref[:n, :] = dv
            else:
                dk_ref[:n, :] += dk
                dv_ref[:n, :] += dv
        dk = rope(dk_ref[...], table_ref[...], -1.0).astype(B)
        dv = dv_ref[...].astype(B)
        for i in range(parts):
            t = slice(i * piece, (i + 1) * piece)
            for a in range(2):
                r = slice(i * w + a * piece, i * w + (a + 1) * piece)
                dkv_ref[a, t, c] = dk[r]
                dkv_ref[a, t, columns + h * hd : columns + (h + 1) * hd] = dv[r]


def local_backward(q, k, v, ship, stats, table, heads, parts):
    length, columns = q.shape
    hd = columns // heads
    return call(
        functools.partial(local_backward_body, heads=heads, parts=parts),
        [shape((2, length // 2, columns), F), shape((2, length // 2, 2 * columns), B)],
        "local_backward",
        10 * length * length * columns,
        in_specs=[whole()] * 6,
        scratch_shapes=[pltpu.VMEM((length, hd), F)] * 2,
    )(q, k, v, ship, stats, table)


def merge_body(
    chosen_ref, lo_ref, ll_ref, oo_ref, ol_ref, *refs, count, heads
):
    ships = refs[:count]
    att_ref, total_ref = refs[count:]
    chunk, columns = att_ref.shape
    hd = columns // heads
    chosen = chosen_ref[0]
    far = choose(ships, (slice(0, chunk), slice(None)), chosen).astype(F)
    packed = choose(ships, (slice(chunk, ships[0].shape[0]), slice(None)), chosen)
    far_lse = unpack_rows(packed, heads, chunk // columns)
    local_lse = ll_ref[0]
    own_lse = ol_ref[0]
    peak = jnp.maximum(jnp.maximum(local_lse, own_lse), far_lse)
    weights = [jnp.exp(l - peak) for l in (local_lse, own_lse, far_lse)]
    total = weights[0] + weights[1] + weights[2]
    total_ref[...] = peak + jnp.log(total)
    weights = [x / total for x in weights]
    stacked = jnp.concatenate(weights + [jnp.zeros((8 - 3 * heads % 8, chunk), F)], axis=0).T
    for h in range(heads):
        c = slice(h * hd, (h + 1) * hd)
        att_ref[:, c] = (
            lo_ref[0, :, c].astype(F) * stacked[:, h : h + 1]
            + oo_ref[0, :, c].astype(F) * stacked[:, heads + h : heads + h + 1]
            + far[:, c] * stacked[:, 2 * heads + h : 2 * heads + h + 1]
        ).astype(B)


def merge(c, chosen, local, own, ships, heads):
    _, chunk, columns = local[0].shape
    part = pl.BlockSpec((1, chunk, columns), lambda i: (c, 0, 0))
    row = pl.BlockSpec((1, heads, chunk), lambda i: (c, 0, 0))
    return call(
        functools.partial(merge_body, count=len(ships), heads=heads),
        [shape((chunk, columns), B), shape((heads, chunk), F)],
        "merge",
        grid=(1,),
        in_specs=[scalars(), part, row, part, row] + [resident(s.shape) for s in ships],
        out_specs=[resident((chunk, columns)), resident((heads, chunk))],
    )(chosen, *local, *own, *ships)


def feed_body(me_ref, *refs, parts):
    pieces = refs[:parts]
    outs = refs[parts : 2 * parts]
    (x_ref, g_ref, gain_ref, wg_ref, wu_ref, wd_ref) = refs[2 * parts : 2 * parts + 6]
    normed_ref, gu_ref, hidden_ref = refs[2 * parts + 6 : 2 * parts + 9]
    gn_refs = refs[2 * parts + 9 : 2 * parts + 11]
    down_refs = refs[2 * parts + 11 : 2 * parts + 13]
    own_ref = refs[2 * parts + 13]
    me = me_ref[0]
    piece = x_ref.shape[2]
    width = x_ref.shape[3]
    ff = wg_ref.shape[0]
    order = list(range(parts.bit_length() - 1))
    for half in range(2):
        js = range(half * parts // 2, (half + 1) * parts // 2)
        r = slice(half * parts // 2 * piece, (half + 1) * parts // 2 * piece)
        middle = x_ref[js[0] : js[-1] + 1, 0].reshape(-1, width).astype(F)
        for p, w in zip(pieces, outs):
            middle = middle + dot(p[r, :], w[...], 1, 0)
        for a, j in enumerate(js):
            @pl.when(me == j)
            def _(a=a):
                own_ref[...] = middle[a * piece : (a + 1) * piece]
        factor = lax.rsqrt(jnp.mean(middle * middle, axis=1, keepdims=True) + epsilon)
        normed = (middle * factor * gain_ref[...]).astype(B)
        normed_ref[r, :] = normed
        gate = dot(normed, wg_ref[...], 1, 1)
        upper = dot(normed, wu_ref[...], 1, 1)
        s = jax.nn.sigmoid(gate)
        silu = gate * s
        hidden = (silu * upper).astype(B)
        hidden_ref[r, :] = hidden
        grad_hidden = dot(g_ref[js[0] : js[-1] + 1, 0].reshape(-1, width), wd_ref[...], 1, 1)
        grad_gate = (grad_hidden * upper * s * (1.0 + gate * (1.0 - s))).astype(B)
        grad_upper = (grad_hidden * silu).astype(B)
        gu_ref[r, :ff] = grad_gate
        gu_ref[r, ff:] = grad_upper
        grad_normed = dot(grad_gate, wg_ref[...], 1, 0) + dot(grad_upper, wu_ref[...], 1, 0)
        down = dot(hidden, wd_ref[...], 1, 0)
        for a, j in enumerate(js):
            place = slot_place(jnp.bitwise_xor(me, j), order)
            store_half(gn_refs, place, slice(None), grad_normed[a * piece : (a + 1) * piece])
            store_half(down_refs, place, slice(None), down[a * piece : (a + 1) * piece])


def feed(c, me, pieces, outs, tokens, cotangent, gain, wg, wu, wd):
    parts, _, piece, width = tokens.shape
    chunk = parts * piece
    ff = wg.shape[0]
    part = pl.BlockSpec((parts, 1, piece, width), lambda i: (0, c, 0, 0))
    results = [
        shape((chunk, width), B),
        shape((chunk, 2 * ff), B),
        shape((chunk, ff), B),
        shape((parts // 2, piece, width), B),
        shape((parts // 2, piece, width), B),
        shape((parts // 2, piece, width), B),
        shape((parts // 2, piece, width), B),
        shape((piece, width), F),
    ]
    return call(
        functools.partial(feed_body, parts=parts),
        results,
        "feed",
        2 * chunk * width * (width + 6 * ff),
        grid=(1,),
        in_specs=[scalars()]
        + [resident(p.shape) for p in pieces]
        + [resident(w.shape) for w in outs]
        + [part, part]
        + [resident(a.shape) for a in (gain, wg, wu, wd)],
        out_specs=[resident(r.shape) for r in results],
    )(me, *pieces, *outs, tokens, cotangent, gain, wg, wu, wd)


def middle_back_body(me_ref, *refs):
    g_ref, gain_ref, gm_ref, gb_ref, ga_ref = refs[8:]
    gain = None
    for c in range(2):
        gn_ref, r1_ref, r2_ref, m_ref = refs[4 * c : 4 * c + 4]
        total = gn_ref[0].astype(F) + r1_ref[0].astype(F) + r2_ref[...].astype(F)
        middle = m_ref[...]
        piece = middle.shape[0]
        rows = slice(c * piece, (c + 1) * piece)
        factor = lax.rsqrt(jnp.mean(middle * middle, axis=1, keepdims=True) + epsilon)
        scaled = total * gain_ref[...]
        grad = (
            g_ref[0, c].astype(F)
            + factor * scaled
            - middle
            * (factor * factor * factor)
            * jnp.mean(middle * scaled, axis=1, keepdims=True)
        )
        gm_ref[rows, :] = grad
        gb_ref[rows, :] = grad.astype(B)
        part = jnp.sum(total * middle * factor, axis=0, keepdims=True)
        gain = part if gain is None else gain + part
    ga_ref[...] = gain


def middle_back(me, chunks, cotangent, gain):
    piece, width = chunks[0][3].shape
    fixed = lambda dims: pl.BlockSpec(dims, lambda i, m: (0,) * len(dims))
    results = [shape((2 * piece, width), F), shape((2 * piece, width), B), shape((1, width), F)]
    per_chunk = [
        fixed((1, piece, width)),
        fixed((1, piece, width)),
        fixed((piece, width)),
        fixed((piece, width)),
    ]
    return call(
        middle_back_body,
        results,
        "middle_back",
        grid_spec=pltpu.PrefetchScalarGridSpec(
            num_scalar_prefetch=1,
            grid=(1,),
            in_specs=per_chunk * 2
            + [
                pl.BlockSpec((1, 2, piece, width), lambda i, m: (m[0], 0, 0, 0)),
                fixed((1, width)),
            ],
            out_specs=[fixed(r.shape) for r in results],
        ),
    )(me, *chunks[0], *chunks[1], cotangent, gain)


def branch_body(me_ref, *refs, parts, heads, distances):
    pieces = refs[:parts]
    w_ref, att0, att1, lse0, lse1, gb_ref, ship_ref, st_ref = refs[parts:]
    me = me_ref[0]
    piece = pieces[0].shape[0] // 2
    chunk = parts * piece
    columns = w_ref.shape[0]
    hd = columns // heads
    extra = padded_rows(6 * heads * (chunk // columns))
    for c, (att, lse) in enumerate(((att0, lse0), (att1, lse1))):
        for a, k in enumerate(distances):
            start = pl.multiple_of(jnp.bitwise_xor(me, k) * piece, piece)
            gb_ref[c, pl.ds(start, piece), :] = pieces[a][c * piece : (c + 1) * piece, :]
        grad = dot(gb_ref[c], w_ref[...], 1, 1).astype(B)
        ship_ref[c * chunk : (c + 1) * chunk, :] = grad
        product = grad.astype(F) * att[...].astype(F)
        rows = [lse[...]]
        for h in range(heads):
            rows.append(
                jnp.sum(product[:, h * hd : (h + 1) * hd].T, axis=0, keepdims=True)
            )
        stats = jnp.concatenate(rows, axis=0)
        st_ref[c] = stats
        row = 2 * chunk + c * extra
        ship_ref[row : row + extra, :] = pack_rows(stats, columns, extra)


def branch(me, pieces, distances, w_output, att, lse, heads):
    parts = len(distances)
    piece, width = pieces[0].shape
    piece = piece // 2
    chunk = parts * piece
    columns = w_output.shape[0]
    extra = padded_rows(6 * heads * (chunk // columns))
    return call(
        functools.partial(branch_body, parts=parts, heads=heads, distances=tuple(distances)),
        [
            shape((2, chunk, width), B),
            shape((2 * (chunk + extra), columns), B),
            shape((2, 2 * heads, chunk), F),
        ],
        "branch",
        4 * chunk * width * columns,
        in_specs=[scalars()] + [whole()] * (parts + 5),
    )(me, *pieces, w_output, *att, *lse)


def store_slots(place_ref, outs, first, value, c):
    rows = outs[0].shape[1]
    for a in range(value.shape[0] // rows):
        store_half(outs, place_ref[first + a], c, value[a * rows : (a + 1) * rows])


def columns_body(place_ref, a0, a1, r_ref, keep_ref, send_ref, *, view):
    if view:
        r0 = r_ref[:, 0].reshape(a0.shape[0], -1)
        r1 = r_ref[:, 1].reshape(a0.shape[0], -1)
    else:
        r0 = r_ref[0]
        r1 = r_ref[1]
    value = dot(a0[...], r0, 0, 0) + dot(a1[...], r1, 0, 0)
    lanes = keep_ref.shape[2]
    per = value.shape[1] // lanes
    first = pl.program_id(0) * per
    for a in range(per):
        store_half(
            (keep_ref, send_ref), place_ref[first + a], slice(None),
            value[:, a * lanes : (a + 1) * lanes],
        )


def column_grads(place, left, right, docs, name):
    chunk, features = left[0].shape
    width = right.shape[-1]
    block = max(width // docs, 256)
    view = right.ndim == 4
    rows = right.shape[:-1]
    out = shape((docs // 2, features, width // docs), B)
    return call(
        functools.partial(columns_body, view=view),
        [out, out],
        name,
        grid=(width // block,),
        in_specs=[scalars()]
        + [resident(a.shape) for a in left]
        + [pl.BlockSpec(rows + (block,), lambda i: (0,) * len(rows) + (i,))],
        out_specs=[resident(out.shape)] * 2,
    )(place, *left, right)


def two_columns_body(first_ref, second_ref, a0, a1, r0, r1, keep0, send0, keep1, send1):
    value = dot(a0[...], r0[...], 0, 0) + dot(a1[...], r1[...], 0, 0)
    _, half, lanes = keep0.shape
    per = value.shape[1] // lanes
    first = pl.program_id(0) * per
    for a in range(per):
        c = slice(a * lanes, (a + 1) * lanes)
        store_half((keep0, send0), first_ref[first + a], slice(None), value[:half, c])
        store_half((keep1, send1), second_ref[first + a], slice(None), value[half:, c])


def two_column_grads(places, left, right, docs, name):
    chunk, features = left[0].shape
    width = right[0].shape[1]
    block = max(width // docs, 256)
    out = shape((docs // 2, features // 2, width // docs), B)
    column = pl.BlockSpec((chunk, block), lambda i: (0, i))
    return call(
        two_columns_body,
        [out] * 4,
        name,
        grid=(width // block,),
        in_specs=[scalars()] * 2 + [resident(a.shape) for a in left] + [column, column],
        out_specs=[resident(out.shape)] * 4,
    )(*places, *left, *right)


def key_grads_body(
    place_ref, n_ref, dkv_ref, gb_ref, att0, att1, wk_ref, wv_ref, keep_ref, send_ref, gn_ref
):
    out_ref = (keep_ref, send_ref)
    columns = wk_ref.shape[1]
    for c in range(2):
        gn_ref[c] = (
            dot(dkv_ref[c, :, :columns], wk_ref[...], 1, 1)
            + dot(dkv_ref[c, :, columns:], wv_ref[...], 1, 1)
        ).astype(B)
    store_slots(
        place_ref, out_ref, 0,
        dot(n_ref[0], dkv_ref[0], 0, 0) + dot(n_ref[1], dkv_ref[1], 0, 0), slice(0, 2 * columns),
    )
    store_slots(
        place_ref, out_ref, 0,
        dot(gb_ref[0], att0[...], 0, 0) + dot(gb_ref[1], att1[...], 0, 0),
        slice(2 * columns, 3 * columns),
    )


def key_grads(place, normed, dkv, gb, att, wk, wv, docs):
    _, chunk, width = normed.shape
    columns = wk.shape[1]
    return call(
        key_grads_body,
        [shape((docs // 2, width // docs, 3 * columns), B)] * 2 + [shape((2, chunk, width), B)],
        "key_grads",
        20 * chunk * width * columns,
        in_specs=[scalars()] + [whole()] * 7,
    )(place, normed, dkv, gb, *att, wk, wv)


def query_grads_body(
    chosen_ref, me_ref, place_ref, dq_ref, *refs, count, parts, heads
):
    ships = refs[:count]
    n_ref, part_ref, wq_ref, table_ref, x_ref, mlp_ref = refs[count : count + 6]
    out_ref = refs[count + 6 : count + 8]
    gn_refs = refs[count + 8 : count + 10]
    chosen = chosen_ref[0]
    me = me_ref[0]
    _, chunk, columns = dq_ref.shape
    piece = chunk // parts
    hd = columns // heads
    width = wq_ref.shape[0]
    order = list(range(parts.bit_length() - 1))
    grads = None
    gain = None
    for c in range(2):
        far = choose(ships, (slice(c * chunk, (c + 1) * chunk), slice(None)), chosen)
        dq = dq_ref[c] + far.astype(F)
        table = table_ref[:, c].reshape(chunk, hd)
        low = jnp.concatenate(
            [rope(dq[:, h * hd : (h + 1) * hd], table, -1.0) for h in range(heads)], axis=1
        ).astype(B)
        gn = dot(low, wq_ref[...], 1, 1) + part_ref[c].astype(F)
        for j in range(parts):
            place = slot_place(jnp.bitwise_xor(me, j), order)
            store_half(
                gn_refs, place, slice(None), gn[j * piece : (j + 1) * piece],
                slice(c * piece, (c + 1) * piece),
            )
        x = x_ref[:, c].reshape(chunk, width).astype(F)
        factor = lax.rsqrt(jnp.mean(x * x, axis=1, keepdims=True) + epsilon)
        part = jnp.sum(gn * x * factor, axis=0, keepdims=True)
        gain = part if gain is None else gain + part
        part = dot(n_ref[c], low, 0, 0)
        grads = part if grads is None else grads + part
    gains = jnp.concatenate([gain, mlp_ref[...]], axis=0)
    lanes = out_ref[0].shape[1] - extra_rows
    for d in range(width // lanes):
        rows = slice(d * lanes, (d + 1) * lanes)
        own = jnp.concatenate([gains[:, rows], jnp.zeros((2, columns - lanes), F)], axis=1)
        own = jnp.concatenate([own, jnp.zeros((extra_rows - 2, columns), F)], axis=0)
        store_half(
            out_ref, place_ref[d], slice(None), jnp.concatenate([grads[rows], own], axis=0)
        )


def query_grads(
    chosen, me, place, dq, ships, normed, part, wq, table, tokens, mlp_gain, docs, heads
):
    _, chunk, width = normed.shape
    columns = wq.shape[1]
    parts = tokens.shape[0]
    return call(
        functools.partial(query_grads_body, count=len(ships), parts=parts, heads=heads),
        [shape((docs // 2, width // docs + extra_rows, columns), B)] * 2
        + [shape((parts // 2, 2 * chunk // parts, width), B)] * 2,
        "query_grads",
        8 * chunk * width * columns,
        in_specs=[scalars()] * 3 + [whole()] * (len(ships) + 7),
    )(chosen, me, place, dq, *ships, normed, part, wq, table, tokens, mlp_gain)


def tokens_back_body(me_ref, gn_ref, r1_ref, r2_ref, x_ref, gm_ref, gain_ref, out_ref):
    total = gn_ref[0].astype(F) + r1_ref[0].astype(F) + r2_ref[...].astype(F)
    x = x_ref[...].astype(F)
    factor = lax.rsqrt(jnp.mean(x * x, axis=1, keepdims=True) + epsilon)
    scaled = total * gain_ref[...]
    grad = factor * scaled - x * (factor * factor * factor) * jnp.mean(
        x * scaled, axis=1, keepdims=True
    )
    out_ref[...] = (gm_ref[...] + grad).astype(B)


def tokens_back(me, gn, r1, r2, tokens, gm, gain):
    _, share, width = gn.shape
    fixed = lambda dims: pl.BlockSpec(dims, lambda i, m: (0,) * len(dims))
    return call(
        tokens_back_body,
        shape((share, width), B),
        "tokens_back",
        grid_spec=pltpu.PrefetchScalarGridSpec(
            num_scalar_prefetch=1,
            grid=(1,),
            in_specs=[
                fixed((1, share, width)),
                fixed((1, share, width)),
                fixed((share, width)),
                pl.BlockSpec((share, width), lambda i, m: (m[0], 0)),
                fixed(gm.shape),
                fixed((1, width)),
            ],
            out_specs=fixed((share, width)),
        ),
    )(me, gn, r1, r2, tokens, gm, gain)


def rotate_table(length, hd):
    half = hd // 2
    position = np.arange(length, dtype=np.float32)
    inverse = np.exp(
        -np.log(np.float32(10000.0)) * np.arange(half, dtype=np.float32) * np.float32(2.0) / hd
    ).astype(np.float32)
    angles = position[:, None] * inverse[None, :]
    return jnp.asarray(np.concatenate([np.cos(angles), np.sin(angles)], axis=1).astype(np.float32))


def to_all(array):
    bits = axis_bits("dp")
    got = {b: swap(array, "dp", 1 << b) for b in reversed(range(bits))}
    return [got[b] for b in range(bits)]


def gather_tensor(value):
    pieces, distances = [value], [0]
    for b in reversed(range(axis_bits("tensor"))):
        pieces = pieces + [swap(p, "tensor", 1 << b) for p in pieces]
        distances = distances + [k ^ (1 << b) for k in distances]
    return pieces, distances


def after(value, *others):
    return lax.optimization_barrier((value,) + others)[0]


def add_low(a, b):
    return (a.astype(F) + b.astype(F)).astype(B)


def fold(keep, send, bit, *others, hold=None):
    got = swap(after(send, *others) if others else send, "dp", 1 << bit)
    if hold is not None:
        got = after(got, hold)
    half = keep.shape[0] // 2
    if half == 0:
        return keep[0], got[0]
    return add_low(keep[:half], got[:half]), add_low(keep[half:], got[half:])


def total(pair, c=slice(None)):
    return pair[0][:, c].astype(F) + pair[1][:, c].astype(F)


def per_device(
    tokens,
    w_query,
    w_key,
    w_value,
    w_output,
    w_gate,
    w_up,
    w_down,
    gain_attn,
    gain_mlp,
    cache_keys,
    cache_values,
    knn_index,
    memory_flag,
    pairing,
    cotangent,
):
    length, width = tokens.shape
    parts = lax.axis_size("tensor")
    docs = lax.axis_size("dp")
    piece = length // parts // 2
    me = lax.axis_index("tensor").astype(jnp.int32).reshape(1)
    heads = cache_keys.shape[1]
    rows = cache_keys.shape[2]
    hd = cache_keys.shape[3]
    columns = heads * hd
    groups = knn_index.shape[1] // 2
    spread = rows // groups
    flag = memory_flag[:1].astype(jnp.int32)
    my_doc = lax.axis_index("dp").astype(jnp.int32)
    difference = jnp.bitwise_xor(pairing[0].astype(jnp.int32), my_doc)
    chosen = jnp.zeros((), jnp.int32)
    for b in range(1, axis_bits("dp")):
        chosen = jnp.where(difference == (1 << b), b, chosen)
    chosen = chosen.reshape(1)
    dp_order = list(range(axis_bits("dp")))
    other_order = [dp_order[1], dp_order[0]] + dp_order[2:]
    place, other_place = [
        slot_place(jnp.bitwise_xor(jnp.arange(docs, dtype=jnp.int32), my_doc), o).astype(jnp.int32)
        for o in (dp_order, other_order)
    ]
    table = rotate_table(length, hd)
    gain_a = gain_attn.reshape(1, width)
    gain_m = gain_mlp.reshape(1, width)
    tokens_view = tokens.reshape(parts, 2, piece, width)
    cotangent_view = cotangent.reshape(parts, 2, piece, width)
    table_view = table.reshape(parts, 2, piece, hd)

    def ordered_rows(cache):
        return (
            cache.reshape(heads, groups // GROUP_BLOCK, GROUP_BLOCK, spread, hd)
            .transpose(0, 1, 3, 2, 4)
            .reshape(heads, rows, hd)
        )

    ship, q, k, v, normed_low, own_off = project(
        flag, tokens, knn_index, gain_a, w_query, w_key, w_value, table, parts, heads, spread
    )
    ships = to_all(ship)
    out_weights, distances = gather_tensor(w_output)
    stored_keys = ordered_rows(cache_keys[0])
    stored_values = ordered_rows(cache_values[0])
    local = local_forward(q, k, v, heads, parts)
    own_out, own_lse, own_sel = own_attend(
        flag, ship, own_off, stored_keys, stored_values, spread
    )
    ships = list(after(tuple(ships), own_out, local[0], *out_weights))
    att, lse, their_sel, their_off, returned, pieces = [], [], [], [], [], []
    packs = []
    for c in range(2):
        packed, sel, off, their_flag = their_attend(
            c, chosen, ships, stored_keys, stored_values, spread, groups
        )
        their_sel.append(sel)
        their_off.append(off)
        packs.append(packed)
        returned.append(to_all(packed))
    returned[0] = list(after(tuple(returned[0]), packs[1]))
    for c in range(2):
        a, log_total = merge(c, chosen, local, (own_out, own_lse), returned[c], heads)
        att.append(a)
        lse.append(log_total)
        pieces.append(gather_tensor(a)[0])

    feeds, back = [], []
    for c in range(2):
        pieces[c] = list(after(tuple(pieces[c]), feeds[0][0] if c else att[1]))
        feeds.append(
            feed(
                c, me, pieces[c], out_weights, tokens_view, cotangent_view, gain_m, w_gate.T,
                w_up.T, w_down,
            )
        )
        keep, send = feeds[c][3], feeds[c][4]
        first = swap(send, "tensor", 1)
        back.append((first, add_low(keep[1], first[1])))
    rows_back = (back[0][1], back[1][1])
    gate_slots = two_column_grads(
        (place, other_place),
        after((feeds[0][1], feeds[1][1]), *rows_back),
        (feeds[0][0], feeds[1][0]),
        docs,
        "gate_grads",
    )
    partial, seconds = [], []
    for c in range(2):
        keep, send = feeds[c][5], after(feeds[c][6], *rows_back)
        first = swap(send, "tensor", 1)
        seconds.append(add_low(keep[1], first[1]))
        partial.append(feeds[c][7] + keep[0].astype(F) + first[0].astype(F))
    seconds = jnp.concatenate(seconds, axis=0)
    partial = jnp.concatenate(partial, axis=0)
    arrived = [swap(second, "tensor", 2) for _, second in back]
    arrived = after(tuple(arrived), gate_slots[1], seconds, partial)
    gm, low, gain_part = middle_back(
        me,
        [(feeds[c][3], back[c][0], arrived[c], feeds[c][7]) for c in range(2)],
        cotangent_view,
        gain_m,
    )
    gb_pieces, _ = gather_tensor(low)
    gate_half = fold(*gate_slots[:2], dp_order[0], hold=low)
    up_half = fold(*gate_slots[2:], other_order[0], hold=low)
    down_slots = column_grads(
        place,
        after((feeds[0][2], feeds[1][2]), low, gate_half[1], up_half[1]),
        cotangent_view,
        docs,
        "down_grads",
    )

    grad_branch, back_ship, stats = branch(
        me, after(tuple(gb_pieces), down_slots[1]), distances, w_output, att, lse, heads
    )
    gate_half = fold(*gate_half, dp_order[1], hold=back_ship)
    up_half = fold(*up_half, other_order[1], hold=back_ship)
    back_ships = to_all(back_ship)
    down_half = fold(*down_slots, dp_order[0], gate_half[1], up_half[1])
    local_dq, dkv = local_backward(q, k, v, back_ship, stats, table, heads, parts)
    dq = own_backward(
        flag, back_ship, stats, own_sel, own_off, stored_keys, stored_values, local_dq, spread
    )
    second = swap(after(seconds, back_ship), "tensor", 2)
    output = (partial + second.astype(F)).astype(B)
    back_ships = list(after(tuple(back_ships), dq, gate_half[1], up_half[1], output, down_half[1]))
    their_dq = their_backward(
        chosen, their_flag, back_ships, their_sel, their_off, stored_keys, stored_values, spread
    )
    down_half = fold(*down_half, dp_order[1], back_ships[0], hold=their_dq)
    if len(dp_order) > 2:
        gate_half = fold(*gate_half, dp_order[2], back_ships[0], hold=their_dq)
    dq_ships = to_all(their_dq)

    keep, send, gn_part = key_grads(
        place, normed_low, after(dkv, their_dq), grad_branch, att, w_key, w_value, docs
    )
    key_half = fold(keep, send, dp_order[0])
    keep, send, gn_keep, gn_send = query_grads(
        chosen, me, place, dq, dq_ships, normed_low, gn_part, w_query, table_view, tokens_view,
        gain_part, docs, heads
    )
    first = swap(gn_send, "tensor", 1)
    query_half = fold(keep, send, dp_order[0])
    second = add_low(gn_keep[1], first[1])
    last = swap(second, "tensor", 2)
    query_half = fold(*query_half, dp_order[1], second)
    key_half = fold(*key_half, dp_order[1], gn_send)
    for b in dp_order[2:]:
        key_half = fold(*key_half, b)
        query_half = fold(*query_half, b, key_half[1])
    if len(dp_order) > 2:
        up_half = fold(*up_half, other_order[2], their_dq, hold=second)
    for b in dp_order[2:]:
        down_half = fold(*down_half, b, gn_send, hold=key_half[1])
    for b in dp_order[3:]:
        gate_half = fold(*gate_half, b)
        up_half = fold(*up_half, b)
    grad_tokens = tokens_back(me, gn_keep, first, last, tokens, gm, gain_a)
    query_total = total(query_half)
    lanes = width // docs
    gains = query_total[lanes : lanes + 8, :lanes]
    gains = gains + sum(swap(gains, "tensor", t) for t in range(1, parts))
    return (
        output,
        grad_tokens,
        query_total[:lanes],
        total(key_half, slice(0, columns)),
        total(key_half, slice(columns, 2 * columns)),
        total(key_half, slice(2 * columns, None)).T,
        total(gate_half).T,
        total(up_half).T,
        total(down_half),
        gains[0],
        gains[1],
    )


def solution(mesh):
    placed = (
        P("dp", None),
        P(None, "tensor"),
        P(None, "tensor"),
        P(None, "tensor"),
        P("tensor", None),
        P(None, "tensor"),
        P(None, "tensor"),
        P("tensor", None),
        P(),
        P(),
        P("dp", "tensor", None, None),
        P("dp", "tensor", None, None),
        P("dp", None),
        P("dp"),
        P("dp"),
        P("dp", None),
    )
    return jax.shard_map(
        per_device,
        mesh=mesh,
        in_specs=placed,
        out_specs=(
            P(("dp", "tensor"), None),
            P(("dp", "tensor"), None),
            P("dp", "tensor"),
            P("dp", "tensor"),
            P("dp", "tensor"),
            P("tensor", "dp"),
            P("dp", "tensor"),
            P("dp", "tensor"),
            P("tensor", "dp"),
            P("dp"),
            P("dp"),
        ),
        check_vma=False,
    )
```

```python
import functools

import jax
import jax.numpy as jnp
import numpy as np
from jax import lax
from jax.experimental import pallas as pl
from jax.experimental.pallas import tpu as pltpu
from jax.sharding import PartitionSpec as P

epsilon = 1e-05
negative_big = -1e30
F = jnp.float32
B = jnp.bfloat16
GROUP_BLOCK = 16
extra_rows = 16
kernel_us = dict(
    project=3.4, own_attend=9.0, their_attend=5.3, own_backward=7.2, their_backward=8.5,
    local_forward=3.4, local_backward=4.2, merge=1.9, feed=9.8, middle_back=0.4, branch=2.3,
    down_grads=4.0, gate_grads=6.2, key_grads=5.6, query_grads=4.3, tokens_back=2.4,
)


def dot(a, b, da, db):
    return lax.dot_general(a, b, (((da,), (db,)), ((), ())), preferred_element_type=F)


def swap(array, axis, bit):
    return lax.ppermute(array, axis, [(i, i ^ bit) for i in range(lax.axis_size(axis))])


def axis_bits(axis):
    return lax.axis_size(axis).bit_length() - 1


def call(body, out_shape, name, flops=0, limit=28, **options):
    kernel = pl.pallas_call(
        body,
        out_shape=out_shape,
        name=name,
        cost_estimate=pl.CostEstimate(
            flops=int(kernel_us[name] * 1e9 * 1.15), transcendentals=0, bytes_accessed=0
        ),
        compiler_params=pltpu.CompilerParams(vmem_limit_bytes=limit << 20),
        **options,
    )
    specs = options.get("in_specs")

    def run(*args):
        if specs is not None:
            args = [
                pltpu.with_memory_space_constraint(a, pltpu.VMEM)
                if s.block_shape is None and s.memory_space is pltpu.VMEM
                else a
                for a, s in zip(args, specs)
            ]
        return kernel(*args)

    return run


def shape(dims, dtype):
    return jax.ShapeDtypeStruct(dims, dtype)


def whole():
    return pl.BlockSpec(memory_space=pltpu.VMEM)


def scalars():
    return pl.BlockSpec(memory_space=pltpu.SMEM)


def slot_place(difference, order):
    place = 0
    for b in order:
        place = place * 2 + ((difference >> b) & 1)
    return place


def store_half(refs, place, c, value, rows=slice(None)):
    half = refs[0].shape[0]
    value = value.astype(B)

    @pl.when(place < half)
    def _():
        refs[0][place, rows, c] = value

    @pl.when(place >= half)
    def _():
        refs[1][place - half, rows, c] = value


def choose(refs, index, chosen):
    value = refs[0][index]
    for b in range(1, len(refs)):
        value = jnp.where(chosen == b, refs[b][index], value)
    return value


def split_terms(x):
    first = x.astype(B).astype(F)
    second = (x - first).astype(B).astype(F)
    third = (x - first - second).astype(B).astype(F)
    return [first, second, third]


def pack_rows(x, lanes, total):
    rows = []
    terms = split_terms(x)
    for b in range(x.shape[1] // lanes):
        rows += [t[:, b * lanes : (b + 1) * lanes] for t in terms]
    used = sum(r.shape[0] for r in rows)
    if total > used:
        rows.append(jnp.zeros((total - used, lanes), F))
    return jnp.concatenate(rows, axis=0).astype(B)


def unpack_rows(packed, n, blocks):
    packed = packed.astype(F)
    out = []
    for b in range(blocks):
        base = b * 3 * n
        out.append(
            packed[base : base + n]
            + packed[base + n : base + 2 * n]
            + packed[base + 2 * n : base + 3 * n]
        )
    return jnp.concatenate(out, axis=1)


def rope(x, table, direction):
    half = x.shape[1] // 2
    other = pltpu.roll(table, half, 1)
    front = lax.broadcasted_iota(jnp.int32, x.shape, 1) < half
    cos = jnp.where(front, table, other)
    sin = jnp.where(front, -other, table) * direction
    return x * cos + pltpu.roll(x, half, 1) * sin


def project_body(
    flag_ref, x_ref, knn_ref, gain_ref, wq_ref, wk_ref, wv_ref, table_ref,
    ship_ref, q_ref, k_ref, v_ref, normed_ref, off_ref, *, parts, heads, hd, spread,
):
    length = x_ref.shape[0]
    share = length // parts
    piece = share // 2
    chunk = length // 2
    columns = heads * hd
    groups = knn_ref.shape[1] // 2
    gain = gain_ref[...]
    for j in range(parts):
        r = slice(j * share, (j + 1) * share)
        x = x_ref[r, :].astype(F)
        factor = lax.rsqrt(jnp.mean(x * x, axis=1, keepdims=True) + epsilon)
        normed = (x * factor * gain).astype(B)
        table = table_ref[r, :]
        q = dot(normed, wq_ref[...], 1, 0)
        k = dot(normed, wk_ref[...], 1, 0)
        v_ref[r, :] = dot(normed, wv_ref[...], 1, 0).astype(B)
        q = jnp.concatenate(
            [rope(q[:, h * hd : (h + 1) * hd], table, 1.0) for h in range(heads)], axis=1
        ).astype(B)
        q_ref[r, :] = q
        k_ref[r, :] = jnp.concatenate(
            [rope(k[:, h * hd : (h + 1) * hd], table, 1.0) for h in range(heads)], axis=1
        ).astype(B)
        knn = knn_ref[r, :]
        start = lax.broadcasted_iota(jnp.int32, knn.shape, 1) * spread
        off = (knn - start).astype(F).T
        far = jnp.where(flag_ref[0] > 0, off[groups:], -1.0).astype(B)
        off = off[:groups].astype(B)
        for c in range(2):
            p = slice(c * piece, (c + 1) * piece)
            t = slice(j * piece, (j + 1) * piece)
            normed_ref[c, t, :] = normed[p]
            ship_ref[c, t, :] = q[p]
            off_ref[c, :, t] = off[:, p]
            lane = j * piece
            row = chunk + lane // columns * groups
            lane = lane % columns
            ship_ref[c, row : row + groups, lane : lane + piece] = far[:, p]


def project(flag, tokens, knn, gain, wq, wk, wv, table, parts, heads, spread):
    length, width = tokens.shape
    columns = wq.shape[1]
    groups = knn.shape[1] // 2
    chunk = length // 2
    body = functools.partial(
        project_body, parts=parts, heads=heads, hd=columns // heads, spread=spread
    )
    arrays = (tokens, knn, gain, wq, wk, wv, table)
    results = [
        shape((2, chunk + chunk // columns * groups, columns), B),
        shape((length, columns), B),
        shape((length, columns), B),
        shape((length, columns), B),
        shape((2, chunk, width), B),
        shape((2, groups, chunk), B),
    ]
    return call(
        body,
        results,
        "project",
        6 * length * width * columns,
        grid=(1,),
        in_specs=[scalars()] + [resident(a.shape) for a in arrays],
        out_specs=[resident(r.shape) for r in results],
    )(flag, *[pltpu.with_memory_space_constraint(a, pltpu.HBM) for a in arrays])


def pick(block_scores, offsets, heads, spread, gb):
    picked = [s[:gb] for s in block_scores]
    for t in range(1, spread):
        here = offsets == float(t)
        for h in range(heads):
            picked[h] = jnp.where(here, block_scores[h][t * gb : (t + 1) * gb], picked[h])
    return picked


def picked_scores(rows_ref, values, offs, heads, hd, spread, gb):
    rows = gb * spread
    wide = offs.astype(F)
    out = [[] for _ in range(heads)]
    for b in range(offs.shape[0] // gb):
        scores = [
            dot(
                rows_ref[h, b * rows : (b + 1) * rows, :], values[:, h * hd : (h + 1) * hd], 1, 1
            )
            for h in range(heads)
        ]
        picked = pick(scores, wide[b * gb : (b + 1) * gb], heads, spread, gb)
        for h in range(heads):
            out[h].append(picked[h])
    return [jnp.concatenate(o, axis=0) for o in out]


def spread_dot(rows_ref, h, picked, offs, spread, gb):
    rows = gb * spread
    total = None
    zero = jnp.zeros((gb, picked.shape[1]), B)
    for b in range(offs.shape[0] // gb):
        p = picked[b * gb : (b + 1) * gb]
        o = offs[b * gb : (b + 1) * gb]
        wide = jnp.concatenate(
            [jnp.where(o == jnp.asarray(t, B), p, zero) for t in range(spread)], axis=0
        )
        part = dot(rows_ref[h, b * rows : (b + 1) * rows, :], wide, 0, 0)
        total = part if total is None else total + part
    return total


def attend(q, offs, k_ref, v_ref, sel_ref, heads, hd, spread):
    outs, sums = [], []
    picked = picked_scores(k_ref, q, offs, heads, hd, spread, GROUP_BLOCK)
    for h in range(heads):
        x = picked[h] * hd**-0.5
        sel_ref[h] = x
        peak = jnp.max(x, axis=0, keepdims=True)
        p = jnp.exp(x - peak)
        total = jnp.sum(p, axis=0, keepdims=True)
        sums.append(peak + jnp.log(total))
        out = spread_dot(v_ref, h, p.astype(B), offs, spread, GROUP_BLOCK)
        outs.append((out / total).T.astype(B))
    return outs, sums


def own_attend_body(flag_ref, ship_ref, off_ref, k_ref, v_ref, o_ref, lse_ref, sel_ref, *, spread):
    heads, _, hd = k_ref.shape
    chunk = o_ref.shape[1]

    @pl.when(flag_ref[0] > 0)
    def _():
        outs, sums = attend(
            ship_ref[0, :chunk, :], off_ref[0], k_ref, v_ref, sel_ref.at[0], heads, hd, spread
        )
        for h in range(heads):
            o_ref[0, :, h * hd : (h + 1) * hd] = outs[h]
            lse_ref[0, h : h + 1, :] = sums[h]

    @pl.when(flag_ref[0] <= 0)
    def _():
        o_ref[...] = jnp.zeros_like(o_ref)
        lse_ref[...] = jnp.full_like(lse_ref, negative_big)


def resident(dims):
    return pl.BlockSpec(dims, lambda *i: (0,) * len(dims))


def own_attend(flag, ship, off, k, v, spread):
    heads, rows, hd = k.shape
    chunk = off.shape[2]
    groups = off.shape[1]
    columns = heads * hd
    by_chunk = lambda c: (c, 0, 0)
    return call(
        functools.partial(own_attend_body, spread=spread),
        [
            shape((2, chunk, columns), B),
            shape((2, heads, chunk), F),
            shape((2, heads, groups, chunk), F),
        ],
        "own_attend",
        16 * chunk * columns * rows,
        grid=(2,),
        in_specs=[
            scalars(),
            pl.BlockSpec((1,) + ship.shape[1:], by_chunk),
            pl.BlockSpec((1, groups, chunk), by_chunk),
            resident(k.shape),
            resident(v.shape),
        ],
        out_specs=[
            pl.BlockSpec((1, chunk, columns), by_chunk),
            pl.BlockSpec((1, heads, chunk), by_chunk),
            pl.BlockSpec((1, heads, groups, chunk), lambda c: (c, 0, 0, 0)),
        ],
    )(flag, ship, off, k, v)


def shipped_offsets(refs, chosen, chunk, groups, columns):
    blocks = chunk // columns
    index = (0, slice(chunk, chunk + blocks * groups), slice(None))
    packed = choose(refs, index, chosen)
    return jnp.concatenate([packed[b * groups : (b + 1) * groups] for b in range(blocks)], axis=1)


def their_attend_body(chosen_ref, *refs, count, spread, chunk, groups):
    ships = refs[:count]
    k_ref, v_ref, o_ref, sel_ref, off_ref, flag_ref = refs[count:]
    heads, _, hd = k_ref.shape
    columns = heads * hd
    chosen = chosen_ref[0]
    offs = shipped_offsets(ships, chosen, chunk, groups, columns)
    off_ref[...] = offs
    on = jnp.max(offs[:1, :128].astype(F)) >= 0
    flag_ref[0] = on.astype(jnp.int32)

    @pl.when(on)
    def _():
        q = choose(ships, (0, slice(0, chunk), slice(None)), chosen)
        outs, sums = attend(q, offs, k_ref, v_ref, sel_ref, heads, hd, spread)
        for h in range(heads):
            o_ref[:chunk, h * hd : (h + 1) * hd] = outs[h]
        o_ref[chunk:, :] = pack_rows(
            jnp.concatenate(sums, axis=0), columns, o_ref.shape[0] - chunk
        )

    @pl.when(jnp.logical_not(on))
    def _():
        o_ref[:chunk, :] = jnp.zeros((chunk, columns), B)
        o_ref[chunk:, :] = pack_rows(
            jnp.full((heads, chunk), negative_big, F), columns, o_ref.shape[0] - chunk
        )


def padded_rows(n):
    return -(-n // 16) * 16


def their_attend(c, chosen, ships, k, v, spread, groups):
    heads, rows, hd = k.shape
    columns = heads * hd
    chunk = ships[0].shape[1] * columns // (columns + groups)
    extra = padded_rows(3 * heads * chunk // columns)
    return call(
        functools.partial(
            their_attend_body, count=len(ships), spread=spread, chunk=chunk, groups=groups
        ),
        [
            shape((chunk + extra, columns), B),
            shape((heads, groups, chunk), F),
            shape((groups, chunk), B),
            shape((1,), jnp.int32),
        ],
        "their_attend",
        8 * chunk * columns * rows,
        grid=(1,),
        in_specs=[scalars()]
        + [pl.BlockSpec((1,) + s.shape[1:], lambda i: (c, 0, 0)) for s in ships]
        + [resident(k.shape), resident(v.shape)],
        out_specs=[
            resident((chunk + extra, columns)),
            resident((heads, groups, chunk)),
            resident((groups, chunk)),
            scalars(),
        ],
    )(chosen, *ships, k, v)


def score_gradients(g, offs, log_total, delta, sel_ref, v_ref, heads, hd, spread):
    picked = picked_scores(v_ref, g, offs, heads, hd, spread, GROUP_BLOCK)
    return [
        (jnp.exp(sel_ref[h] - log_total[h : h + 1]) * (picked[h] - delta[h : h + 1])).astype(B)
        for h in range(heads)
    ]


def own_backward_body(
    flag_ref, ship_ref, st_ref, sel_ref, off_ref, k_ref, v_ref, local_ref, dq_ref, *, spread
):
    heads, _, hd = k_ref.shape

    @pl.when(flag_ref[0] > 0)
    def _():
        offs = off_ref[0]
        stats = st_ref[0]
        ds = score_gradients(
            ship_ref[...], offs, stats[:heads], stats[heads:], sel_ref.at[0], v_ref, heads, hd,
            spread
        )
        for h in range(heads):
            c = slice(h * hd, (h + 1) * hd)
            out = spread_dot(k_ref, h, ds[h], offs, spread, GROUP_BLOCK)
            dq_ref[0, :, c] = local_ref[0, :, c] + (out * hd**-0.5).T

    @pl.when(flag_ref[0] <= 0)
    def _():
        dq_ref[...] = local_ref[...]


def own_backward(flag, ship, stats, sel, off, k, v, local, spread):
    heads, rows, hd = k.shape
    chunk = off.shape[2]
    groups = off.shape[1]
    columns = heads * hd
    by_chunk = lambda c: (c, 0, 0)
    return call(
        functools.partial(own_backward_body, spread=spread),
        shape((2, chunk, columns), F),
        "own_backward",
        16 * chunk * columns * rows,
        grid=(2,),
        in_specs=[
            scalars(),
            pl.BlockSpec((chunk, columns), lambda c: (c, 0)),
            pl.BlockSpec((1, 2 * heads, chunk), by_chunk),
            pl.BlockSpec((1, heads, groups, chunk), lambda c: (c, 0, 0, 0)),
            pl.BlockSpec((1, groups, chunk), by_chunk),
            resident(k.shape),
            resident(v.shape),
            pl.BlockSpec((1, chunk, columns), by_chunk),
        ],
        out_specs=pl.BlockSpec((1, chunk, columns), by_chunk),
    )(flag, ship, stats, sel, off, k, v, local)


def their_backward_body(chosen_ref, flag_ref, *refs, count, spread, chunk):
    ships = refs[:count]
    sel0, sel1, off0, off1, k_ref, v_ref, dq_ref = refs[count:]
    heads, _, hd = k_ref.shape
    columns = heads * hd
    blocks = chunk // columns
    extra = padded_rows(6 * heads * blocks)
    chosen = chosen_ref[0]
    on = flag_ref[0] > 0

    @pl.when(on)
    def _():
        for c, (sel_ref, off_ref) in enumerate(((sel0, off0), (sel1, off1))):
            offs = off_ref[...]
            g = choose(ships, (slice(c * chunk, (c + 1) * chunk), slice(None)), chosen)
            row = 2 * chunk + c * extra
            stats = unpack_rows(
                choose(ships, (slice(row, row + extra), slice(None)), chosen), 2 * heads, blocks
            )
            ds = score_gradients(
                g, offs, stats[:heads], stats[heads:], sel_ref, v_ref, heads, hd, spread
            )
            for h in range(heads):
                out = spread_dot(k_ref, h, ds[h], offs, spread, GROUP_BLOCK)
                dq_ref[c * chunk : (c + 1) * chunk, h * hd : (h + 1) * hd] = (
                    (out * hd**-0.5).T.astype(B)
                )

    @pl.when(jnp.logical_not(on))
    def _():
        dq_ref[...] = jnp.zeros_like(dq_ref)


def their_backward(chosen, flag, ships, sels, offs, k, v, spread):
    heads, rows, hd = k.shape
    columns = heads * hd
    chunk = offs[0].shape[1]
    return call(
        functools.partial(their_backward_body, count=len(ships), spread=spread, chunk=chunk),
        shape((2 * chunk, columns), B),
        "their_backward",
        16 * chunk * columns * rows,
        in_specs=[scalars(), scalars()] + [whole()] * (len(ships) + 6),
    )(chosen, flag, *ships, *sels, *offs, k, v)


def causal_scores(k, q, w, scale):
    s = dot(k, q, 1, 1) * scale
    n = k.shape[0]
    key = lax.broadcasted_iota(jnp.int32, (w, w), 0)
    query = lax.broadcasted_iota(jnp.int32, (w, w), 1)
    diagonal = jnp.where(key <= query, s[n - w :], negative_big)
    return diagonal if n == w else jnp.concatenate([s[: n - w], diagonal], axis=0)


def local_forward_body(q_ref, k_ref, v_ref, o_ref, lse_ref, *, heads, parts):
    length, columns = q_ref.shape
    hd = columns // heads
    w = length // parts
    piece = w // 2
    for h in range(heads):
        c = slice(h * hd, (h + 1) * hd)
        for i in range(parts):
            n = (i + 1) * w
            s = causal_scores(k_ref[:n, c], q_ref[i * w : n, c], w, hd**-0.5)
            peak = jnp.max(s, axis=0, keepdims=True)
            p = jnp.exp(s - peak)
            total = jnp.sum(p, axis=0, keepdims=True)
            lse = peak + jnp.log(total)
            out = (dot(v_ref[:n, c], p.astype(B), 0, 0) / total).T.astype(B)
            t = slice(i * piece, (i + 1) * piece)
            for a in range(2):
                o_ref[a, t, c] = out[a * piece : (a + 1) * piece]
                lse_ref[a, h : h + 1, t] = lse[:, a * piece : (a + 1) * piece]


def local_forward(q, k, v, heads, parts):
    length, columns = q.shape
    return call(
        functools.partial(local_forward_body, heads=heads, parts=parts),
        [shape((2, length // 2, columns), B), shape((2, heads, length // 2), F)],
        "local_forward",
        4 * length * length * columns,
        in_specs=[whole()] * 3,
    )(q, k, v)


def local_backward_body(
    q_ref, k_ref, v_ref, ship_ref, st_ref, table_ref, dq_ref, dkv_ref, dk_ref, dv_ref,
    *, heads, parts
):
    length, columns = q_ref.shape
    hd = columns // heads
    w = length // parts
    piece = w // 2
    chunk = length // 2
    scale = hd**-0.5
    for h in range(heads):
        c = slice(h * hd, (h + 1) * hd)
        for i in reversed(range(parts)):
            n = (i + 1) * w
            r = slice(i * w, n)
            t = slice(i * piece, (i + 1) * piece)
            g = jnp.concatenate(
                [ship_ref[a * chunk + i * piece : a * chunk + (i + 1) * piece, c] for a in range(2)],
                axis=0,
            )
            stats = jnp.concatenate([st_ref[a, :, t] for a in range(2)], axis=1)
            s = causal_scores(k_ref[:n, c], q_ref[r, c], w, scale)
            p = jnp.exp(s - stats[h : h + 1])
            dp = dot(v_ref[:n, c], g, 1, 1)
            ds = (p * (dp - stats[heads + h : heads + h + 1])).astype(B)
            dq = (dot(k_ref[:n, c], ds, 0, 0) * scale).T
            for a in range(2):
                dq_ref[a, t, c] = dq[a * piece : (a + 1) * piece]
            dk = dot(ds, q_ref[r, c], 1, 0) * scale
            dv = dot(p.astype(B), g, 1, 0)
            if i == parts - 1:
                dk_ref[:n, :] = dk
                dv_ref[:n, :] = dv
            else:
                dk_ref[:n, :] += dk
                dv_ref[:n, :] += dv
        dk = rope(dk_ref[...], table_ref[...], -1.0).astype(B)
        dv = dv_ref[...].astype(B)
        for i in range(parts):
            t = slice(i * piece, (i + 1) * piece)
            for a in range(2):
                r = slice(i * w + a * piece, i * w + (a + 1) * piece)
                dkv_ref[a, t, c] = dk[r]
                dkv_ref[a, t, columns + h * hd : columns + (h + 1) * hd] = dv[r]


def local_backward(q, k, v, ship, stats, table, heads, parts):
    length, columns = q.shape
    hd = columns // heads
    return call(
        functools.partial(local_backward_body, heads=heads, parts=parts),
        [shape((2, length // 2, columns), F), shape((2, length // 2, 2 * columns), B)],
        "local_backward",
        10 * length * length * columns,
        in_specs=[whole()] * 6,
        scratch_shapes=[pltpu.VMEM((length, hd), F)] * 2,
    )(q, k, v, ship, stats, table)


def merge_body(
    chosen_ref, lo_ref, ll_ref, oo_ref, ol_ref, *refs, count, heads
):
    ships = refs[:count]
    att_ref, total_ref = refs[count:]
    chunk, columns = att_ref.shape
    hd = columns // heads
    chosen = chosen_ref[0]
    far = choose(ships, (slice(0, chunk), slice(None)), chosen).astype(F)
    packed = choose(ships, (slice(chunk, ships[0].shape[0]), slice(None)), chosen)
    far_lse = unpack_rows(packed, heads, chunk // columns)
    local_lse = ll_ref[0]
    own_lse = ol_ref[0]
    peak = jnp.maximum(jnp.maximum(local_lse, own_lse), far_lse)
    weights = [jnp.exp(l - peak) for l in (local_lse, own_lse, far_lse)]
    total = weights[0] + weights[1] + weights[2]
    total_ref[...] = peak + jnp.log(total)
    weights = [x / total for x in weights]
    stacked = jnp.concatenate(weights + [jnp.zeros((8 - 3 * heads % 8, chunk), F)], axis=0).T
    for h in range(heads):
        c = slice(h * hd, (h + 1) * hd)
        att_ref[:, c] = (
            lo_ref[0, :, c].astype(F) * stacked[:, h : h + 1]
            + oo_ref[0, :, c].astype(F) * stacked[:, heads + h : heads + h + 1]
            + far[:, c] * stacked[:, 2 * heads + h : 2 * heads + h + 1]
        ).astype(B)


def merge(c, chosen, local, own, ships, heads):
    _, chunk, columns = local[0].shape
    part = pl.BlockSpec((1, chunk, columns), lambda i: (c, 0, 0))
    row = pl.BlockSpec((1, heads, chunk), lambda i: (c, 0, 0))
    return call(
        functools.partial(merge_body, count=len(ships), heads=heads),
        [shape((chunk, columns), B), shape((heads, chunk), F)],
        "merge",
        grid=(1,),
        in_specs=[scalars(), part, row, part, row] + [resident(s.shape) for s in ships],
        out_specs=[resident((chunk, columns)), resident((heads, chunk))],
    )(chosen, *local, *own, *ships)


def feed_body(me_ref, *refs, parts):
    pieces = refs[:parts]
    outs = refs[parts : 2 * parts]
    (x_ref, g_ref, gain_ref, wg_ref, wu_ref, wd_ref) = refs[2 * parts : 2 * parts + 6]
    normed_ref, gu_ref, hidden_ref = refs[2 * parts + 6 : 2 * parts + 9]
    gn_refs = refs[2 * parts + 9 : 2 * parts + 11]
    down_refs = refs[2 * parts + 11 : 2 * parts + 13]
    own_ref = refs[2 * parts + 13]
    me = me_ref[0]
    piece = x_ref.shape[2]
    width = x_ref.shape[3]
    ff = wg_ref.shape[0]
    order = list(range(parts.bit_length() - 1))
    for half in range(2):
        js = range(half * parts // 2, (half + 1) * parts // 2)
        r = slice(half * parts // 2 * piece, (half + 1) * parts // 2 * piece)
        middle = x_ref[js[0] : js[-1] + 1, 0].reshape(-1, width).astype(F)
        for p, w in zip(pieces, outs):
            middle = middle + dot(p[r, :], w[...], 1, 0)
        for a, j in enumerate(js):
            @pl.when(me == j)
            def _(a=a):
                own_ref[...] = middle[a * piece : (a + 1) * piece]
        factor = lax.rsqrt(jnp.mean(middle * middle, axis=1, keepdims=True) + epsilon)
        normed = (middle * factor * gain_ref[...]).astype(B)
        normed_ref[r, :] = normed
        gate = dot(normed, wg_ref[...], 1, 1)
        upper = dot(normed, wu_ref[...], 1, 1)
        s = jax.nn.sigmoid(gate)
        silu = gate * s
        hidden = (silu * upper).astype(B)
        hidden_ref[r, :] = hidden
        grad_hidden = dot(g_ref[js[0] : js[-1] + 1, 0].reshape(-1, width), wd_ref[...], 1, 1)
        grad_gate = (grad_hidden * upper * s * (1.0 + gate * (1.0 - s))).astype(B)
        grad_upper = (grad_hidden * silu).astype(B)
        gu_ref[r, :ff] = grad_gate
        gu_ref[r, ff:] = grad_upper
        grad_normed = dot(grad_gate, wg_ref[...], 1, 0) + dot(grad_upper, wu_ref[...], 1, 0)
        down = dot(hidden, wd_ref[...], 1, 0)
        for a, j in enumerate(js):
            place = slot_place(jnp.bitwise_xor(me, j), order)
            store_half(gn_refs, place, slice(None), grad_normed[a * piece : (a + 1) * piece])
            store_half(down_refs, place, slice(None), down[a * piece : (a + 1) * piece])


def feed(c, me, pieces, outs, tokens, cotangent, gain, wg, wu, wd):
    parts, _, piece, width = tokens.shape
    chunk = parts * piece
    ff = wg.shape[0]
    part = pl.BlockSpec((parts, 1, piece, width), lambda i: (0, c, 0, 0))
    results = [
        shape((chunk, width), B),
        shape((chunk, 2 * ff), B),
        shape((chunk, ff), B),
        shape((parts // 2, piece, width), B),
        shape((parts // 2, piece, width), B),
        shape((parts // 2, piece, width), B),
        shape((parts // 2, piece, width), B),
        shape((piece, width), F),
    ]
    return call(
        functools.partial(feed_body, parts=parts),
        results,
        "feed",
        2 * chunk * width * (width + 6 * ff),
        grid=(1,),
        in_specs=[scalars()]
        + [resident(p.shape) for p in pieces]
        + [resident(w.shape) for w in outs]
        + [part, part]
        + [resident(a.shape) for a in (gain, wg, wu, wd)],
        out_specs=[resident(r.shape) for r in results],
    )(me, *pieces, *outs, tokens, cotangent, gain, wg, wu, wd)


def middle_back_body(me_ref, *refs):
    g_ref, gain_ref, gm_ref, gb_ref, ga_ref = refs[8:]
    gain = None
    for c in range(2):
        gn_ref, r1_ref, r2_ref, m_ref = refs[4 * c : 4 * c + 4]
        total = gn_ref[0].astype(F) + r1_ref[0].astype(F) + r2_ref[...].astype(F)
        middle = m_ref[...]
        piece = middle.shape[0]
        rows = slice(c * piece, (c + 1) * piece)
        factor = lax.rsqrt(jnp.mean(middle * middle, axis=1, keepdims=True) + epsilon)
        scaled = total * gain_ref[...]
        grad = (
            g_ref[0, c].astype(F)
            + factor * scaled
            - middle
            * (factor * factor * factor)
            * jnp.mean(middle * scaled, axis=1, keepdims=True)
        )
        gm_ref[rows, :] = grad
        gb_ref[rows, :] = grad.astype(B)
        part = jnp.sum(total * middle * factor, axis=0, keepdims=True)
        gain = part if gain is None else gain + part
    ga_ref[...] = gain


def middle_back(me, chunks, cotangent, gain):
    piece, width = chunks[0][3].shape
    fixed = lambda dims: pl.BlockSpec(dims, lambda i, m: (0,) * len(dims))
    results = [shape((2 * piece, width), F), shape((2 * piece, width), B), shape((1, width), F)]
    per_chunk = [
        fixed((1, piece, width)),
        fixed((1, piece, width)),
        fixed((piece, width)),
        fixed((piece, width)),
    ]
    return call(
        middle_back_body,
        results,
        "middle_back",
        grid_spec=pltpu.PrefetchScalarGridSpec(
            num_scalar_prefetch=1,
            grid=(1,),
            in_specs=per_chunk * 2
            + [
                pl.BlockSpec((1, 2, piece, width), lambda i, m: (m[0], 0, 0, 0)),
                fixed((1, width)),
            ],
            out_specs=[fixed(r.shape) for r in results],
        ),
    )(me, *chunks[0], *chunks[1], cotangent, gain)


def branch_body(me_ref, *refs, parts, heads, distances):
    pieces = refs[:parts]
    w_ref, att0, att1, lse0, lse1, gb_ref, ship_ref, st_ref = refs[parts:]
    me = me_ref[0]
    piece = pieces[0].shape[0] // 2
    chunk = parts * piece
    columns = w_ref.shape[0]
    hd = columns // heads
    extra = padded_rows(6 * heads * (chunk // columns))
    for c, (att, lse) in enumerate(((att0, lse0), (att1, lse1))):
        for a, k in enumerate(distances):
            start = pl.multiple_of(jnp.bitwise_xor(me, k) * piece, piece)
            gb_ref[c, pl.ds(start, piece), :] = pieces[a][c * piece : (c + 1) * piece, :]
        grad = dot(gb_ref[c], w_ref[...], 1, 1).astype(B)
        ship_ref[c * chunk : (c + 1) * chunk, :] = grad
        product = grad.astype(F) * att[...].astype(F)
        rows = [lse[...]]
        for h in range(heads):
            rows.append(
                jnp.sum(product[:, h * hd : (h + 1) * hd].T, axis=0, keepdims=True)
            )
        stats = jnp.concatenate(rows, axis=0)
        st_ref[c] = stats
        row = 2 * chunk + c * extra
        ship_ref[row : row + extra, :] = pack_rows(stats, columns, extra)


def branch(me, pieces, distances, w_output, att, lse, heads):
    parts = len(distances)
    piece, width = pieces[0].shape
    piece = piece // 2
    chunk = parts * piece
    columns = w_output.shape[0]
    extra = padded_rows(6 * heads * (chunk // columns))
    return call(
        functools.partial(branch_body, parts=parts, heads=heads, distances=tuple(distances)),
        [
            shape((2, chunk, width), B),
            shape((2 * (chunk + extra), columns), B),
            shape((2, 2 * heads, chunk), F),
        ],
        "branch",
        4 * chunk * width * columns,
        in_specs=[scalars()] + [whole()] * (parts + 5),
    )(me, *pieces, w_output, *att, *lse)


def store_slots(place_ref, outs, first, value, c):
    rows = outs[0].shape[1]
    for a in range(value.shape[0] // rows):
        store_half(outs, place_ref[first + a], c, value[a * rows : (a + 1) * rows])


def columns_body(place_ref, a0, a1, r_ref, keep_ref, send_ref, *, view):
    if view:
        r0 = r_ref[:, 0].reshape(a0.shape[0], -1)
        r1 = r_ref[:, 1].reshape(a0.shape[0], -1)
    else:
        r0 = r_ref[0]
        r1 = r_ref[1]
    value = dot(a0[...], r0, 0, 0) + dot(a1[...], r1, 0, 0)
    lanes = keep_ref.shape[2]
    per = value.shape[1] // lanes
    first = pl.program_id(0) * per
    for a in range(per):
        store_half(
            (keep_ref, send_ref), place_ref[first + a], slice(None),
            value[:, a * lanes : (a + 1) * lanes],
        )


def column_grads(place, left, right, docs, name):
    chunk, features = left[0].shape
    width = right.shape[-1]
    block = max(width // docs, 256)
    view = right.ndim == 4
    rows = right.shape[:-1]
    out = shape((docs // 2, features, width // docs), B)
    return call(
        functools.partial(columns_body, view=view),
        [out, out],
        name,
        grid=(width // block,),
        in_specs=[scalars()]
        + [resident(a.shape) for a in left]
        + [pl.BlockSpec(rows + (block,), lambda i: (0,) * len(rows) + (i,))],
        out_specs=[resident(out.shape)] * 2,
    )(place, *left, right)


def two_columns_body(first_ref, second_ref, a0, a1, r0, r1, keep0, send0, keep1, send1):
    value = dot(a0[...], r0[...], 0, 0) + dot(a1[...], r1[...], 0, 0)
    _, half, lanes = keep0.shape
    per = value.shape[1] // lanes
    first = pl.program_id(0) * per
    for a in range(per):
        c = slice(a * lanes, (a + 1) * lanes)
        store_half((keep0, send0), first_ref[first + a], slice(None), value[:half, c])
        store_half((keep1, send1), second_ref[first + a], slice(None), value[half:, c])


def two_column_grads(places, left, right, docs, name):
    chunk, features = left[0].shape
    width = right[0].shape[1]
    block = max(width // docs, 256)
    out = shape((docs // 2, features // 2, width // docs), B)
    column = pl.BlockSpec((chunk, block), lambda i: (0, i))
    return call(
        two_columns_body,
        [out] * 4,
        name,
        grid=(width // block,),
        in_specs=[scalars()] * 2 + [resident(a.shape) for a in left] + [column, column],
        out_specs=[resident(out.shape)] * 4,
    )(*places, *left, *right)


def key_grads_body(
    place_ref, n_ref, dkv_ref, gb_ref, att0, att1, wk_ref, wv_ref, keep_ref, send_ref, gn_ref
):
    out_ref = (keep_ref, send_ref)
    columns = wk_ref.shape[1]
    for c in range(2):
        gn_ref[c] = (
            dot(dkv_ref[c, :, :columns], wk_ref[...], 1, 1)
            + dot(dkv_ref[c, :, columns:], wv_ref[...], 1, 1)
        ).astype(B)
    store_slots(
        place_ref, out_ref, 0,
        dot(n_ref[0], dkv_ref[0], 0, 0) + dot(n_ref[1], dkv_ref[1], 0, 0), slice(0, 2 * columns),
    )
    store_slots(
        place_ref, out_ref, 0,
        dot(gb_ref[0], att0[...], 0, 0) + dot(gb_ref[1], att1[...], 0, 0),
        slice(2 * columns, 3 * columns),
    )


def key_grads(place, normed, dkv, gb, att, wk, wv, docs):
    _, chunk, width = normed.shape
    columns = wk.shape[1]
    return call(
        key_grads_body,
        [shape((docs // 2, width // docs, 3 * columns), B)] * 2 + [shape((2, chunk, width), B)],
        "key_grads",
        20 * chunk * width * columns,
        in_specs=[scalars()] + [whole()] * 7,
    )(place, normed, dkv, gb, *att, wk, wv)


def query_grads_body(
    chosen_ref, me_ref, place_ref, dq_ref, *refs, count, parts, heads
):
    ships = refs[:count]
    n_ref, part_ref, wq_ref, table_ref, x_ref, mlp_ref = refs[count : count + 6]
    out_ref = refs[count + 6 : count + 8]
    gn_refs = refs[count + 8 : count + 10]
    chosen = chosen_ref[0]
    me = me_ref[0]
    _, chunk, columns = dq_ref.shape
    piece = chunk // parts
    hd = columns // heads
    width = wq_ref.shape[0]
    order = list(range(parts.bit_length() - 1))
    grads = None
    gain = None
    for c in range(2):
        far = choose(ships, (slice(c * chunk, (c + 1) * chunk), slice(None)), chosen)
        dq = dq_ref[c] + far.astype(F)
        table = table_ref[:, c].reshape(chunk, hd)
        low = jnp.concatenate(
            [rope(dq[:, h * hd : (h + 1) * hd], table, -1.0) for h in range(heads)], axis=1
        ).astype(B)
        gn = dot(low, wq_ref[...], 1, 1) + part_ref[c].astype(F)
        for j in range(parts):
            place = slot_place(jnp.bitwise_xor(me, j), order)
            store_half(
                gn_refs, place, slice(None), gn[j * piece : (j + 1) * piece],
                slice(c * piece, (c + 1) * piece),
            )
        x = x_ref[:, c].reshape(chunk, width).astype(F)
        factor = lax.rsqrt(jnp.mean(x * x, axis=1, keepdims=True) + epsilon)
        part = jnp.sum(gn * x * factor, axis=0, keepdims=True)
        gain = part if gain is None else gain + part
        part = dot(n_ref[c], low, 0, 0)
        grads = part if grads is None else grads + part
    gains = jnp.concatenate([gain, mlp_ref[...]], axis=0)
    lanes = out_ref[0].shape[1] - extra_rows
    for d in range(width // lanes):
        rows = slice(d * lanes, (d + 1) * lanes)
        own = jnp.concatenate([gains[:, rows], jnp.zeros((2, columns - lanes), F)], axis=1)
        own = jnp.concatenate([own, jnp.zeros((extra_rows - 2, columns), F)], axis=0)
        store_half(
            out_ref, place_ref[d], slice(None), jnp.concatenate([grads[rows], own], axis=0)
        )


def query_grads(
    chosen, me, place, dq, ships, normed, part, wq, table, tokens, mlp_gain, docs, heads
):
    _, chunk, width = normed.shape
    columns = wq.shape[1]
    parts = tokens.shape[0]
    return call(
        functools.partial(query_grads_body, count=len(ships), parts=parts, heads=heads),
        [shape((docs // 2, width // docs + extra_rows, columns), B)] * 2
        + [shape((parts // 2, 2 * chunk // parts, width), B)] * 2,
        "query_grads",
        8 * chunk * width * columns,
        in_specs=[scalars()] * 3 + [whole()] * (len(ships) + 7),
    )(chosen, me, place, dq, *ships, normed, part, wq, table, tokens, mlp_gain)


def tokens_back_body(me_ref, gn_ref, r1_ref, r2_ref, x_ref, gm_ref, gain_ref, out_ref):
    total = gn_ref[0].astype(F) + r1_ref[0].astype(F) + r2_ref[...].astype(F)
    x = x_ref[...].astype(F)
    factor = lax.rsqrt(jnp.mean(x * x, axis=1, keepdims=True) + epsilon)
    scaled = total * gain_ref[...]
    grad = factor * scaled - x * (factor * factor * factor) * jnp.mean(
        x * scaled, axis=1, keepdims=True
    )
    out_ref[...] = (gm_ref[...] + grad).astype(B)


def tokens_back(me, gn, r1, r2, tokens, gm, gain):
    _, share, width = gn.shape
    fixed = lambda dims: pl.BlockSpec(dims, lambda i, m: (0,) * len(dims))
    return call(
        tokens_back_body,
        shape((share, width), B),
        "tokens_back",
        grid_spec=pltpu.PrefetchScalarGridSpec(
            num_scalar_prefetch=1,
            grid=(1,),
            in_specs=[
                fixed((1, share, width)),
                fixed((1, share, width)),
                fixed((share, width)),
                pl.BlockSpec((share, width), lambda i, m: (m[0], 0)),
                fixed(gm.shape),
                fixed((1, width)),
            ],
            out_specs=fixed((share, width)),
        ),
    )(me, gn, r1, r2, tokens, gm, gain)


def rotate_table(length, hd):
    half = hd // 2
    position = np.arange(length, dtype=np.float32)
    inverse = np.exp(
        -np.log(np.float32(10000.0)) * np.arange(half, dtype=np.float32) * np.float32(2.0) / hd
    ).astype(np.float32)
    angles = position[:, None] * inverse[None, :]
    return jnp.asarray(np.concatenate([np.cos(angles), np.sin(angles)], axis=1).astype(np.float32))


def to_all(array):
    bits = axis_bits("dp")
    got = {b: swap(array, "dp", 1 << b) for b in reversed(range(bits))}
    return [got[b] for b in range(bits)]


def gather_tensor(value):
    pieces, distances = [value], [0]
    for b in reversed(range(axis_bits("tensor"))):
        pieces = pieces + [swap(p, "tensor", 1 << b) for p in pieces]
        distances = distances + [k ^ (1 << b) for k in distances]
    return pieces, distances


def after(value, *others):
    return lax.optimization_barrier((value,) + others)[0]


def add_low(a, b):
    return (a.astype(F) + b.astype(F)).astype(B)


def fold(keep, send, bit, *others, hold=None):
    got = swap(after(send, *others) if others else send, "dp", 1 << bit)
    if hold is not None:
        got = after(got, hold)
    half = keep.shape[0] // 2
    if half == 0:
        return keep[0], got[0]
    return add_low(keep[:half], got[:half]), add_low(keep[half:], got[half:])


def total(pair, c=slice(None)):
    return pair[0][:, c].astype(F) + pair[1][:, c].astype(F)


def per_device(
    tokens,
    w_query,
    w_key,
    w_value,
    w_output,
    w_gate,
    w_up,
    w_down,
    gain_attn,
    gain_mlp,
    cache_keys,
    cache_values,
    knn_index,
    memory_flag,
    pairing,
    cotangent,
):
    length, width = tokens.shape
    parts = lax.axis_size("tensor")
    docs = lax.axis_size("dp")
    piece = length // parts // 2
    me = lax.axis_index("tensor").astype(jnp.int32).reshape(1)
    heads = cache_keys.shape[1]
    rows = cache_keys.shape[2]
    hd = cache_keys.shape[3]
    columns = heads * hd
    groups = knn_index.shape[1] // 2
    spread = rows // groups
    flag = memory_flag[:1].astype(jnp.int32)
    my_doc = lax.axis_index("dp").astype(jnp.int32)
    difference = jnp.bitwise_xor(pairing[0].astype(jnp.int32), my_doc)
    chosen = jnp.zeros((), jnp.int32)
    for b in range(1, axis_bits("dp")):
        chosen = jnp.where(difference == (1 << b), b, chosen)
    chosen = chosen.reshape(1)
    dp_order = list(range(axis_bits("dp")))
    other_order = [dp_order[1], dp_order[0]] + dp_order[2:]
    place, other_place = [
        slot_place(jnp.bitwise_xor(jnp.arange(docs, dtype=jnp.int32), my_doc), o).astype(jnp.int32)
        for o in (dp_order, other_order)
    ]
    table = rotate_table(length, hd)
    gain_a = gain_attn.reshape(1, width)
    gain_m = gain_mlp.reshape(1, width)
    tokens_view = tokens.reshape(parts, 2, piece, width)
    cotangent_view = cotangent.reshape(parts, 2, piece, width)
    table_view = table.reshape(parts, 2, piece, hd)

    def ordered_rows(cache):
        return (
            cache.reshape(heads, groups // GROUP_BLOCK, GROUP_BLOCK, spread, hd)
            .transpose(0, 1, 3, 2, 4)
            .reshape(heads, rows, hd)
        )

    ship, q, k, v, normed_low, own_off = project(
        flag, tokens, knn_index, gain_a, w_query, w_key, w_value, table, parts, heads, spread
    )
    ships = to_all(ship)
    out_weights, distances = gather_tensor(w_output)
    stored_keys = ordered_rows(cache_keys[0])
    stored_values = ordered_rows(cache_values[0])
    local = local_forward(q, k, v, heads, parts)
    own_out, own_lse, own_sel = own_attend(
        flag, ship, own_off, stored_keys, stored_values, spread
    )
    ships = list(after(tuple(ships), own_out, local[0], *out_weights))
    att, lse, their_sel, their_off, returned, pieces = [], [], [], [], [], []
    packs = []
    for c in range(2):
        packed, sel, off, their_flag = their_attend(
            c, chosen, ships, stored_keys, stored_values, spread, groups
        )
        their_sel.append(sel)
        their_off.append(off)
        packs.append(packed)
        returned.append(to_all(packed))
    returned[0] = list(after(tuple(returned[0]), packs[1]))
    for c in range(2):
        a, log_total = merge(c, chosen, local, (own_out, own_lse), returned[c], heads)
        att.append(a)
        lse.append(log_total)
        pieces.append(gather_tensor(a)[0])

    feeds, back = [], []
    for c in range(2):
        pieces[c] = list(after(tuple(pieces[c]), feeds[0][0] if c else att[1]))
        feeds.append(
            feed(
                c, me, pieces[c], out_weights, tokens_view, cotangent_view, gain_m, w_gate.T,
                w_up.T, w_down,
            )
        )
        keep, send = feeds[c][3], feeds[c][4]
        first = swap(send, "tensor", 1)
        back.append((first, add_low(keep[1], first[1])))
    rows_back = (back[0][1], back[1][1])
    gate_slots = two_column_grads(
        (place, other_place),
        after((feeds[0][1], feeds[1][1]), *rows_back),
        (feeds[0][0], feeds[1][0]),
        docs,
        "gate_grads",
    )
    partial, seconds = [], []
    for c in range(2):
        keep, send = feeds[c][5], after(feeds[c][6], *rows_back)
        first = swap(send, "tensor", 1)
        seconds.append(add_low(keep[1], first[1]))
        partial.append(feeds[c][7] + keep[0].astype(F) + first[0].astype(F))
    seconds = jnp.concatenate(seconds, axis=0)
    partial = jnp.concatenate(partial, axis=0)
    arrived = [swap(second, "tensor", 2) for _, second in back]
    arrived = after(tuple(arrived), gate_slots[1], seconds, partial)
    gm, low, gain_part = middle_back(
        me,
        [(feeds[c][3], back[c][0], arrived[c], feeds[c][7]) for c in range(2)],
        cotangent_view,
        gain_m,
    )
    gb_pieces, _ = gather_tensor(low)
    gate_half = fold(*gate_slots[:2], dp_order[0], hold=low)
    up_half = fold(*gate_slots[2:], other_order[0], hold=low)
    down_slots = column_grads(
        place,
        after((feeds[0][2], feeds[1][2]), low),
        cotangent_view,
        docs,
        "down_grads",
    )

    grad_branch, back_ship, stats = branch(
        me, after(tuple(gb_pieces), down_slots[1]), distances, w_output, att, lse, heads
    )
    gate_half = fold(*gate_half, dp_order[1], hold=back_ship)
    up_half = fold(*up_half, other_order[1], hold=back_ship)
    back_ships = to_all(back_ship)
    down_half = fold(*down_slots, dp_order[0], gate_half[1], up_half[1])
    local_dq, dkv = local_backward(q, k, v, back_ship, stats, table, heads, parts)
    dq = own_backward(
        flag, back_ship, stats, own_sel, own_off, stored_keys, stored_values, local_dq, spread
    )
    back_ships = list(after(tuple(back_ships), dq, gate_half[1], up_half[1]))
    their_dq = their_backward(
        chosen, their_flag, back_ships, their_sel, their_off, stored_keys, stored_values, spread
    )
    if len(dp_order) > 2:
        gate_half = fold(*gate_half, dp_order[2], back_ships[0], down_half[1])
    dq_ships = to_all(their_dq)

    keep, send, gn_part = key_grads(
        place, normed_low, after(dkv, their_dq), grad_branch, att, w_key, w_value, docs
    )
    down_half = fold(*down_half, dp_order[1], their_dq, gate_half[1])
    key_half = fold(keep, send, dp_order[0])
    second = swap(after(seconds, their_dq), "tensor", 2)
    output = (partial + second.astype(F)).astype(B)
    keep, send, gn_keep, gn_send = query_grads(
        chosen, me, place, dq, dq_ships, normed_low, gn_part, w_query, table_view, tokens_view,
        gain_part, docs, heads
    )
    first = swap(gn_send, "tensor", 1)
    query_half = fold(keep, send, dp_order[0])
    second = add_low(gn_keep[1], first[1])
    last = swap(second, "tensor", 2)
    pair_half = [
        jnp.concatenate([q, jnp.pad(k, ((0, 0), (0, extra_rows), (0, 0)))], axis=2)
        for q, k in zip(query_half, key_half)
    ]
    pair_half = fold(*pair_half, dp_order[1], second)
    if len(dp_order) > 2:
        up_half = fold(*up_half, other_order[2], gn_send, hold=pair_half[1])
    for b in dp_order[2:]:
        pair_half = fold(*pair_half, b)
        down_half = fold(*down_half, b, gn_send)
    for b in dp_order[3:]:
        gate_half = fold(*gate_half, b)
        up_half = fold(*up_half, b)
    grad_tokens = tokens_back(me, gn_keep, first, last, tokens, gm, gain_a)
    pair_total = total(pair_half)
    query_total = pair_total[:, :columns]
    key_total = pair_total[:, columns:]
    lanes = width // docs
    gains = query_total[lanes : lanes + 8, :lanes]
    gains = gains + sum(swap(gains, "tensor", t) for t in range(1, parts))
    return (
        output,
        grad_tokens,
        query_total[:lanes],
        key_total[:lanes, :columns],
        key_total[:lanes, columns : 2 * columns],
        key_total[:lanes, 2 * columns :].T,
        total(gate_half).T,
        total(up_half).T,
        total(down_half),
        gains[0],
        gains[1],
    )


def solution(mesh):
    placed = (
        P("dp", None),
        P(None, "tensor"),
        P(None, "tensor"),
        P(None, "tensor"),
        P("tensor", None),
        P(None, "tensor"),
        P(None, "tensor"),
        P("tensor", None),
        P(),
        P(),
        P("dp", "tensor", None, None),
        P("dp", "tensor", None, None),
        P("dp", None),
        P("dp"),
        P("dp"),
        P("dp", None),
    )
    return jax.shard_map(
        per_device,
        mesh=mesh,
        in_specs=placed,
        out_specs=(
            P(("dp", "tensor"), None),
            P(("dp", "tensor"), None),
            P("dp", "tensor"),
            P("dp", "tensor"),
            P("dp", "tensor"),
            P("tensor", "dp"),
            P("dp", "tensor"),
            P("dp", "tensor"),
            P("tensor", "dp"),
            P("dp"),
            P("dp"),
        ),
        check_vma=False,
    )
```
